32 devices in a mesh: row: 2 (over y), col: 4 (over x, core), frame: 4 (over z).
Axes of the slice: x: 2, y: 2, z: 4, core: 2. Of those that a mesh axis runs over, the one named last changes fastest.
Arguments:
- video: float32 [16, 576, 1024], P('frame', 'row', 'col'), may hold values from -60 to 60
- multiplier: float32 [16, 576, 1024], P('frame', 'row', 'col'), may hold values from -3 to 3
- foreground: float32 [16, 576, 1024], P('frame', 'row', 'col'), may hold values from -6 to 6
- basis: float32 [16, 576, 1024], P(None, 'row', 'col'), may hold values from -40 to 40
- coefficients: float32 [16, 16], P('frame'), may hold values from -10 to 10
Outputs:
- new_foreground: float32 [16, 576, 1024], P('frame', 'row', 'col')
- new_coefficients: float32 [16, 16], P('frame')
- new_basis: float32 [16, 576, 1024], P(None, ('row', 'frame'), 'col')
The draws below stay inside these ranges and needn't reach their ends.
All inputs are finite; a program needn't handle non-finite values.
Results may differ from the reference program's by a relative error of at most 0.0003.
Values sent between devices are 32-bit elements; how exact they have to be, the bound alone decides.
A program may use at most 128 MiB of HBM per device.

```python
import jax
import jax.numpy as jnp
from jax import lax

RANK = 16
PASSES = 3
FRAMES = 16
HEIGHT = 576
WIDTH = 1024


def factor_parts(key):
    folded = jax.random.fold_in(key, 101)
    streams = jax.random.split(folded, 6)
    rank_scale = jnp.exp(jax.random.uniform(streams[0], (RANK,), jnp.float32, -1.15, 1.15))
    rise_rows = 3.0 ** (jnp.arange(HEIGHT, dtype=jnp.float32) / HEIGHT - 0.5)
    rise_cols = 3.0 ** (jnp.arange(WIDTH, dtype=jnp.float32) / WIDTH - 0.5)
    pixel_scale = jnp.exp(jax.random.uniform(streams[1], (HEIGHT, WIDTH), jnp.float32, -1.15, 1.15)) * rise_rows[:, None] * rise_cols[None, :]
    shapes = jax.random.normal(streams[2], (RANK, HEIGHT, WIDTH), jnp.float32)
    true_basis = 0.5 * shapes * rank_scale[:, None, None] * pixel_scale[None, :, :]
    frame_scale = jnp.exp(jax.random.uniform(streams[4], (FRAMES,), jnp.float32, -1.15, 1.15)) * 3.0 ** (jnp.arange(FRAMES, dtype=jnp.float32) / FRAMES - 0.5)
    weights = jax.random.normal(streams[5], (FRAMES, RANK), jnp.float32)
    true_coeff = 0.25 * weights * frame_scale[:, None]
    return (true_basis, true_coeff)


def draw_video(key, part):
    true_basis, true_coeff = factor_parts(key)
    streams = jax.random.split(jax.random.fold_in(key, 202), 3)
    low_rank = jnp.einsum('fr,rhw->fhw', true_coeff, true_basis)
    spikes = 2.0 * jax.random.normal(streams[1], (FRAMES, HEIGHT, WIDTH), jnp.float32) * jax.random.bernoulli(streams[2], 0.1, (FRAMES, HEIGHT, WIDTH)).astype(jnp.float32)
    jitter = 0.3 * jax.random.normal(streams[0], (FRAMES, HEIGHT, WIDTH), jnp.float32)
    return jnp.clip(low_rank + jitter + spikes, -60.0, 60.0)


def draw_basis(key, part):
    true_basis, true_coeff = factor_parts(key)
    jitter = jax.random.normal(jax.random.fold_in(key, 303), (RANK, HEIGHT, WIDTH), jnp.float32)
    return jnp.clip(true_basis * (1.0 + 0.2 * jitter), -40.0, 40.0)


def draw_coefficients(key, part):
    true_basis, true_coeff = factor_parts(key)
    jitter = jax.random.normal(jax.random.fold_in(key, 404), (FRAMES, RANK), jnp.float32)
    return jnp.clip(true_coeff + 0.1 * jitter, -10.0, 10.0)


def block_scale(key, dims, pieces, least, top_value):
    level, own = 1.0, jax.random.fold_in(key, 6)
    for position, parts in pieces:
        draws = jnp.exp(jax.random.uniform(jax.random.fold_in(own, position), (parts,), jnp.float32, least / len(pieces), top_value / len(pieces)))
        level = level * jnp.repeat(draws, dims[position] // parts).reshape([-1 if axis == position else 1 for axis in range(len(dims))])
    return level


def centred(key, shape, scale, bound, cuts=(), kind=jnp.bfloat16):
    result = jax.random.normal(key, shape, jnp.float32) * scale
    if len(cuts) > 0:
        result = block_scale(key, shape, cuts, -0.22, 0.18) * result
    return jnp.clip(result, min=-bound, max=bound).astype(kind)


def setup_inputs(seed: int = 0) -> dict:
    arg_keys = jax.random.split(jax.random.key(seed), 6)
    video = draw_video(jax.random.fold_in(arg_keys[5], 71), 0)
    multiplier = centred(arg_keys[1], (FRAMES, HEIGHT, WIDTH), 0.5, 3.0, ((0, 4), (1, 2), (2, 4)), jnp.float32)
    foreground = centred(arg_keys[2], (FRAMES, HEIGHT, WIDTH), 1.0, 6.0, ((0, 4), (1, 2), (2, 4)), jnp.float32)
    basis = draw_basis(jax.random.fold_in(arg_keys[5], 71), 0)
    coefficients = draw_coefficients(jax.random.fold_in(arg_keys[5], 71), 0)
    return dict(video=video, multiplier=multiplier, foreground=foreground, basis=basis, coefficients=coefficients)


relax_rate = 0.8
smooth_weight = 0.5
smooth_floor = 0.25
shrink_level = 0.4
dual_scale = 0.8
ridge_share = 0.1

def forward_cells(padded, direction, shape):
    starts = [0, 0, 0]
    starts[direction] = 1
    limits = [starts[axis_dim] + shape[axis_dim] for axis_dim in range(3)]
    return lax.slice(padded, starts, limits)

def descend(padded, source, anchor, extent):
    shape = tuple((int(length) - 1 for length in padded.shape))
    here_cells = padded[:-1, :-1, :-1]
    slopes = []
    for direction in range(3):
        ahead_cells = forward_cells(padded, direction, shape)
        places = anchor[direction] + jnp.arange(shape[direction], dtype=jnp.int32)
        inside = (places >= 0) & (places < extent[direction] - 1)
        layout = [1, 1, 1]
        layout[direction] = shape[direction]
        inside = inside.reshape(layout)
        slopes.append(jnp.where(inside, ahead_cells - here_cells, jnp.zeros_like(here_cells)))
    weight = lax.rsqrt(smooth_floor + slopes[0] * slopes[0] + slopes[1] * slopes[1] + slopes[2] * slopes[2])
    fluxes = [slope_part * weight for slope_part in slopes]
    spread = fluxes[0][1:, 1:, 1:] - fluxes[0][:-1, 1:, 1:] + (fluxes[1][1:, 1:, 1:] - fluxes[1][1:, :-1, 1:]) + (fluxes[2][1:, 1:, 1:] - fluxes[2][1:, 1:, :-1])
    center = padded[1:-1, 1:-1, 1:-1]
    return center + relax_rate * (source - center + smooth_weight * spread)

def solve_definite(matrix, right_side):
    factor_lower = jnp.linalg.cholesky(matrix)
    half_solved = lax.linalg.triangular_solve(factor_lower, right_side, left_side=True, lower=True)
    return lax.linalg.triangular_solve(factor_lower, half_solved, left_side=True, lower=True, transpose_a=True)

def reference(video, multiplier, foreground, basis, coefficients):
    highest = lax.Precision.HIGHEST
    flat_basis = basis.reshape(RANK, HEIGHT * WIDTH)
    background = jnp.dot(coefficients, flat_basis, precision=highest).reshape(FRAMES, HEIGHT, WIDTH)
    target = video - background + dual_scale * multiplier
    current = foreground
    for sweep in range(PASSES):
        padded = jnp.pad(current, 1)
        current = descend(padded, target, (-1, -1, -1), (FRAMES, HEIGHT, WIDTH))
    shrunk = current - jnp.clip(current, -shrink_level, shrink_level)
    residual_target = video + dual_scale * multiplier - shrunk
    flat_target = residual_target.reshape(FRAMES, HEIGHT * WIDTH)
    gram_sum = jnp.dot(flat_basis, flat_basis.T, precision=highest)
    cross_sum = jnp.dot(flat_basis, flat_target.T, precision=highest)
    identity_matrix = jnp.eye(RANK, dtype=gram_sum.dtype)
    pixel_ridge = ridge_share * HEIGHT * WIDTH
    coeff_rows = solve_definite(gram_sum + pixel_ridge * identity_matrix, cross_sum + pixel_ridge * coefficients.T)
    frame_total = jnp.dot(coeff_rows, flat_target, precision=highest)
    frame_gram = jnp.dot(coeff_rows, coeff_rows.T, precision=highest)
    frame_ridge = ridge_share * FRAMES
    new_basis = solve_definite(frame_gram + frame_ridge * identity_matrix, frame_total + frame_ridge * flat_basis)
    return (shrunk, coeff_rows.T, new_basis.reshape(RANK, HEIGHT, WIDTH))
```

```python
import functools

import jax
import jax.numpy as jnp
from jax import lax
from jax.experimental import pallas as pl
from jax.experimental.pallas import tpu as pltpu
from jax.sharding import PartitionSpec as P

PASSES = 3


relax_rate = 0.8
smooth_weight = 0.5
smooth_floor = 0.25
shrink_level = 0.4
dual_scale = 0.8
ridge_share = 0.1


def with_halo(block, sides, width):
    for axis, dim in sides:
        count = lax.axis_size(axis)
        forward = [(i, i + 1) for i in range(count - 1)]
        backward = [(target, source) for source, target in forward]
        low = lax.ppermute(
            lax.slice_in_dim(block, block.shape[dim] - width, None, axis=dim), axis, forward
        )
        high = lax.ppermute(lax.slice_in_dim(block, 0, width, axis=dim), axis, backward)
        block = jnp.concatenate([low, block, high], axis=dim)
    return block


def forward_cells(padded, direction, shape):
    starts = [0, 0, 0]
    starts[direction] = 1
    limits = [starts[axis_dim] + shape[axis_dim] for axis_dim in range(3)]
    return lax.slice(padded, starts, limits)


def descend(padded, source, anchor, extent):
    shape = tuple((int(length) - 1 for length in padded.shape))
    here_cells = padded[:-1, :-1, :-1]
    slopes = []
    for direction in range(3):
        ahead_cells = forward_cells(padded, direction, shape)
        places = anchor[direction] + jnp.arange(shape[direction], dtype=jnp.int32)
        inside = (places >= 0) & (places < extent[direction] - 1)
        layout = [1, 1, 1]
        layout[direction] = shape[direction]
        inside = inside.reshape(layout)
        slopes.append(jnp.where(inside, ahead_cells - here_cells, jnp.zeros_like(here_cells)))
    weight = lax.rsqrt(
        smooth_floor + slopes[0] * slopes[0] + slopes[1] * slopes[1] + slopes[2] * slopes[2]
    )
    fluxes = [slope_part * weight for slope_part in slopes]
    spread = (
        fluxes[0][1:, 1:, 1:]
        - fluxes[0][:-1, 1:, 1:]
        + (fluxes[1][1:, 1:, 1:] - fluxes[1][1:, :-1, 1:])
        + (fluxes[2][1:, 1:, 1:] - fluxes[2][1:, 1:, :-1])
    )
    center = padded[1:-1, 1:-1, 1:-1]
    return center + relax_rate * (source - center + smooth_weight * spread)


def solve_definite(matrix, right_side):
    factor_lower = jnp.linalg.cholesky(matrix)
    half_solved = lax.linalg.triangular_solve(factor_lower, right_side, left_side=True, lower=True)
    return lax.linalg.triangular_solve(
        factor_lower, half_solved, left_side=True, lower=True, transpose_a=True
    )


def local(video, multiplier, foreground, basis, coefficients):
    highest = lax.Precision.HIGHEST
    frames_here, rows_here, cols_here = video.shape
    rank_size = basis.shape[0]
    frame_count = lax.axis_size("frame")
    row_count = lax.axis_size("row")
    col_count = lax.axis_size("col")
    extent = (frames_here * frame_count, rows_here * row_count, cols_here * col_count)
    frame_slot = lax.axis_index("frame")
    corner = (
        frame_slot * frames_here,
        lax.axis_index("row") * rows_here,
        lax.axis_index("col") * cols_here,
    )
    pixels = rows_here * cols_here
    flat_basis = basis.reshape(rank_size, pixels)
    background = jnp.dot(coefficients, flat_basis, precision=highest).reshape(video.shape)
    target = video - background + dual_scale * multiplier
    current = foreground
    for sweep in range(PASSES):
        padded = with_halo(current, (("row", 1), ("col", 2), ("frame", 0)), 1)
        current = descend(padded, target, tuple((start_cell - 1 for start_cell in corner)), extent)
    shrunk = current - jnp.clip(current, -shrink_level, shrink_level)
    residual_target = video + dual_scale * multiplier - shrunk
    flat_target = residual_target.reshape(frames_here, pixels)
    gram_part = jnp.dot(flat_basis, flat_basis.T, precision=highest)
    cross_part = jnp.dot(flat_basis, flat_target.T, precision=highest)
    gram_sum, cross_sum = lax.psum((gram_part, cross_part), ("row", "col"))
    identity_matrix = jnp.eye(rank_size, dtype=gram_sum.dtype)
    pixel_ridge = ridge_share * pixels * row_count * col_count
    coeff_rows = solve_definite(
        gram_sum + pixel_ridge * identity_matrix, cross_sum + pixel_ridge * coefficients.T
    )
    total_part = jnp.dot(coeff_rows, flat_target, precision=highest).reshape(
        rank_size, rows_here, cols_here
    )
    frame_gram_part = jnp.dot(coeff_rows, coeff_rows.T, precision=highest)
    owned_rows = rows_here // frame_count
    owned_sums = lax.psum_scatter(total_part, "frame", scatter_dimension=1, tiled=True)
    frame_gram = lax.psum(frame_gram_part, "frame")
    old_owned = lax.dynamic_slice_in_dim(basis, frame_slot * owned_rows, owned_rows, 1)
    frame_ridge = ridge_share * frames_here * frame_count
    right_side = (owned_sums + frame_ridge * old_owned).reshape(rank_size, owned_rows * cols_here)
    new_basis = solve_definite(frame_gram + frame_ridge * identity_matrix, right_side)
    return (shrunk, coeff_rows.T, new_basis.reshape(rank_size, owned_rows, cols_here))


MESH = pl.DeviceIdType.MESH
CHUNK = 24


def eliminate(matrix, size):
    lanes = lax.broadcasted_iota(jnp.int32, matrix.shape, 1)
    rows = lax.broadcasted_iota(jnp.int32, matrix.shape, 0)
    for k in range(size):
        pivot = matrix[k : k + 1, k : k + 1]
        scaled = matrix[k : k + 1, :] / pivot
        column = jnp.sum(jnp.where(lanes == k, matrix, 0.0), axis=1, keepdims=True)
        matrix = jnp.where(rows == k, scaled, matrix - column * scaled)
    return matrix


def kernel(
    sizes, coeff_hbm, video_hbm, mult_hbm, fore_hbm, basis_hbm,
    result, coeff_out, fresh,
    field0, field1, field2, video, mult, basis, anchor, target, owned,
    packed, arrived, corner, edge_next, edge_flux, first_cols,
    cross, sums, parts, shares, square, table, coeff_ref, table_smem,
    in_sems, halo_send, halo_recv, part_send, part_recv,
    share_send, share_recv, move_send, move_recv, small_sem,
):
    field = (field0, field1, field2)
    F, H, W, rank, nr, nc, nz = sizes
    r = lax.axis_index("row")
    c = lax.axis_index("col")
    z = lax.axis_index("frame")
    own = H // nz
    pieces = own // CHUNK

    def inside(dr, dc, dz):
        ok = None
        for at, step, count in ((r, dr, nr), (c, dc, nc), (z, dz, nz)):
            if step != 0:
                test = (at + step >= 0) & (at + step < count)
                ok = test if ok is None else ok & test
        return ok

    barrier = pltpu.get_barrier_semaphore()
    for d in range(1, nr * nc):
        other = lax.rem(r * nc + c + d, nr * nc)
        pl.semaphore_signal(
            barrier, inc=1, device_id=(other // nc, lax.rem(other, nc), z), device_id_type=MESH
        )
    for d in range(1, nz):
        pl.semaphore_signal(
            barrier, inc=1, device_id=(r, c, lax.rem(z + d, nz)), device_id_type=MESH
        )
    diagonals = ((1, 0, -1), (-1, 0, 1), (0, 1, -1), (0, -1, 1))
    for step in diagonals:
        @pl.when(inside(*step))
        def _(step=step):
            pl.semaphore_signal(
                barrier,
                inc=1,
                device_id=(r + step[0], c + step[1], z + step[2]),
                device_id_type=MESH,
            )
    expected = jnp.int32(nr * nc - 1 + nz - 1)
    for step in diagonals:
        expected = expected + inside(*step).astype(jnp.int32)
    loads = []
    for i, (src, dst) in enumerate(
        (
            (fore_hbm, field0.at[1 : F + 1, 8 : H + 8, :]),
            (coeff_hbm, coeff_ref),
            (video_hbm, video),
            (mult_hbm, mult),
            (basis_hbm, basis),
        )
    ):
        copy = pltpu.make_async_copy(src, dst, in_sems.at[i])
        copy.start()
        loads.append(copy)

    pl.semaphore_wait(barrier, expected)

    lane_h = lax.broadcasted_iota(jnp.int32, (H, 128), 1)

    def pack_columns(k):
        for side in range(2):
            tile = jnp.zeros((H, 128), jnp.float32)
            for f in range(F):
                at = 0 if side == 0 else W - 1
                lanes = field[k][f + 1, 8 : H + 8, (at // 128) * 128 : (at // 128) * 128 + 128]
                column = lanes[:, at % 128 : at % 128 + 1]
                tile = jnp.where(lane_h == f, column, tile)
            if side == 0:
                first_cols[...] = tile
            packed[k, side] = tile.T[:8, :]

    def halo_list(k):
        fk = field[k]
        mid = slice(1, F + 1)
        return (
            (packed.at[k, 0], arrived.at[k, 0], (0, -1, 0)),
            (packed.at[k, 1], arrived.at[k, 1], (0, 1, 0)),
            (packed.at[k, 0, F - 1 : F], arrived.at[k, 2, F - 1 : F], (0, -1, 1)),
            (packed.at[k, 1, 0:1], arrived.at[k, 3, 0:1], (0, 1, -1)),
            (fk.at[mid, H : H + 8, :], fk.at[mid, 0:8, :], (1, 0, 0)),
            (fk.at[mid, 8:16, :], fk.at[mid, H + 8 : H + 16, :], (-1, 0, 0)),
            (fk.at[F, 8:9, :], fk.at[0, H + 8 : H + 9, :], (-1, 0, 1)),
            (fk.at[1, H + 7 : H + 8, :], fk.at[F + 1, 7:8, :], (1, 0, -1)),
            (fk.at[mid, H : H + 8, 0:128], corner.at[k, 0], (1, -1, 0)),
            (fk.at[mid, 8:16, W - 128 : W], corner.at[k, 1], (-1, 1, 0)),
        ) + tuple(
            face
            for b in range(nz)
            for rows in (slice(8 + b * own, 8 + (b + 1) * own),)
            for face in (
                (fk.at[F, rows, :], fk.at[0, rows, :], (0, 0, 1)),
                (fk.at[1, rows, :], fk.at[F + 1, rows, :], (0, 0, -1)),
            )
        )

    def halo_copy(k, i, src, dst, step):
        return pltpu.make_async_remote_copy(
            src_ref=src, dst_ref=dst,
            send_sem=halo_send.at[k, i], recv_sem=halo_recv.at[k, i],
            device_id=(r + step[0], c + step[1], z + step[2]), device_id_type=MESH,
        )

    def send_halos(k, which):
        every = halo_list(k)
        for i in which:
            src, dst, step = every[i]

            @pl.when(inside(*step))
            def _(i=i, src=src, dst=dst, step=step):
                halo_copy(k, i, src, dst, step).start()

    def wait_halos(k, which):
        every = halo_list(k)
        for i in which:
            src, dst, step = every[i]

            @pl.when(inside(*(-s for s in step)))
            def _(i=i, src=src, dst=dst, step=step):
                halo_copy(k, i, src, dst, step).wait_recv()

    def finish_sends(k):
        for i, (src, dst, step) in enumerate(halo_list(k)):
            @pl.when(inside(*step))
            def _(i=i, src=src, dst=dst, step=step):
                halo_copy(k, i, src, dst, step).wait_send()

    def prepare_columns(k):
        tall = jnp.concatenate([arrived[k, 0], jnp.zeros((120, H), jnp.float32)], axis=0).T
        edge = jnp.concatenate([arrived[k, 2], jnp.zeros((120, H), jnp.float32)], axis=0).T
        tile = jnp.where(lane_h == 0, edge[:, F - 1 : F], pltpu.roll(tall, 1, 1))
        edge_next[8 : H + 8, :] = tile
        lane8 = lax.broadcasted_iota(jnp.int32, (8, 128), 1)
        top = jnp.zeros((8, 128), jnp.float32)
        bottom = jnp.zeros((1, 128), jnp.float32)
        for f in range(F):
            top = jnp.where(lane8 == f + 1, corner[k, 0, f][:, 0:1], top)
            bottom = jnp.where(lane8[:1] == f, corner[k, 1, f][0:1, 127:128], bottom)
        edge_next[0:8, :] = top
        edge_next[H + 8 : H + 16, :] = jnp.zeros((8, 128), jnp.float32)
        here = jnp.concatenate([arrived[k, 1], jnp.zeros((120, H), jnp.float32)], axis=0).T
        edge = jnp.concatenate([arrived[k, 3], jnp.zeros((120, H), jnp.float32)], axis=0).T
        ahead = jnp.where(lane_h == F - 1, edge[:, 0:1], pltpu.roll(here, 127, 1))
        slope0 = jnp.where((lane_h == F - 1) & (z == nz - 1), 0.0, ahead - here)
        row_h = lax.broadcasted_iota(jnp.int32, (H, 128), 0)
        below = jnp.where(row_h == H - 1, bottom, pltpu.roll(here, H - 1, 0))
        slope1 = jnp.where((row_h == H - 1) & (r == nr - 1), 0.0, below - here)
        slope2 = first_cols[...] - here
        weight = lax.rsqrt(smooth_floor + slope0 * slope0 + slope1 * slope1 + slope2 * slope2)
        edge_flux[...] = jnp.where(c == 0, 0.0, slope2 * weight)

    def sweep(k, last, block):
        @pl.loop(0, pieces)
        def _(step):
            start = pl.multiple_of(block * own + step * CHUNK, 8)
            R = CHUNK
            lane_t = lax.broadcasted_iota(jnp.int32, (R + 8, 128), 1)
            row_t = lax.broadcasted_iota(jnp.int32, (R + 8, W), 0) + (r * H + start - 8)
            lane_w = lax.broadcasted_iota(jnp.int32, (R + 8, W), 1)
            blocked = (row_t < 0) | (row_t >= nr * H - 1)
            columns = edge_next[pl.ds(start, R + 8), :]
            fluxes_in = edge_flux[pl.ds(start, R), :]
            now = field[k][0, pl.ds(start, R + 16), :]
            flux0_before = None
            for f in range(-1, F):
                after = field[k][f + 2, pl.ds(start, R + 16), :]
                here = now[: R + 8]
                below = pltpu.roll(now, R + 15, 0)[: R + 8]
                ahead = after[: R + 8]
                wall = columns[:, f + 1 : f + 2]
                beyond = jnp.where(c == nc - 1, here, jnp.broadcast_to(wall, here.shape))
                right = jnp.where(lane_w == W - 1, beyond, pltpu.roll(here, W - 1, 1))
                slope0 = ahead - here
                if f == F - 1:
                    slope0 = jnp.where(z == nz - 1, 0.0, slope0)
                slope1 = jnp.where(blocked, 0.0, below - here)
                slope2 = right - here
                weight = lax.rsqrt(
                    smooth_floor + slope0 * slope0 + slope1 * slope1 + slope2 * slope2
                )
                flux0 = (slope0 * weight)[8:]
                if f < 0:
                    flux0 = jnp.where(z == 0, 0.0, flux0)
                else:
                    flux1 = jnp.where(row_t < 0, 0.0, slope1 * weight)
                    flux2 = (slope2 * weight)[8:]
                    above = pltpu.roll(flux1, 1, 0)[8:]
                    left = jnp.where(
                        lane_w[8:] == 0,
                        jnp.broadcast_to(fluxes_in[:, f : f + 1], flux2.shape),
                        pltpu.roll(flux2, 1, 1),
                    )
                    spread = flux0 - flux0_before + (flux1[8:] - above) + (flux2 - left)
                    center = here[8:]
                    at = pl.ds(start, R)
                    value = center + relax_rate * (
                        target[f, at, :] - center + smooth_weight * spread
                    )
                    if last:
                        shrunk = value - jnp.clip(value, -shrink_level, shrink_level)
                        result[f, at, :] = shrunk
                        anchor[f, at, :] = anchor[f, at, :] - shrunk
                    else:
                        field[k + 1][f + 1, pl.ds(start + 8, R), :] = value
                flux0_before = flux0
                now = after
            if last:
                @pl.when((z != block) & ~held(block))
                def _():
                    move(block, step).start()

    def products(left_of, right_of, lefts, rights, first, count, start, store):
        def body(step, totals):
            rows = pl.ds(pl.multiple_of(first + step * 8, 8), 8)
            a = [left_of[i, rows, :] for i in lefts]
            b = [right_of[j, rows, :] for j in rights]
            out = []
            for x in range(len(lefts)):
                for y in range(len(rights)):
                    prod = a[x] * b[y]
                    total = totals[len(out)]
                    for w in range(W // 128):
                        total = total + prod[:, w * 128 : w * 128 + 128]
                    out.append(total)
            return tuple(out)

        totals = lax.fori_loop(
            0, count // 8, body, tuple(start(i, j) for i in lefts for j in rights), unroll=2 if count % 16 == 0 else 1
        )
        n = 0
        for i in lefts:
            for j in rights:
                store(i, j, totals[n])
                n += 1

    def held(block):
        right = (z < block) & (block == nz - 1) & (nz - 1 - z >= 2)
        left = (z > block) & (block == z - 1) & (z >= 2)
        return right | left

    def move(block, piece):
        rows = pl.ds(pl.multiple_of(block * own + piece * CHUNK, 8), CHUNK)
        spot = pl.ds(pl.multiple_of(piece * CHUNK, 8), CHUNK)
        return pltpu.make_async_remote_copy(
            src_ref=anchor.at[:, rows, :], dst_ref=owned.at[pl.ds(z * F, F), spot, :],
            send_sem=move_send.at[block, piece], recv_sem=move_recv.at[z, piece],
            device_id=(r, c, block), device_id_type=MESH,
        )

    def take(source, piece):
        rows = pl.ds(pl.multiple_of(z * own + piece * CHUNK, 8), CHUNK)
        spot = pl.ds(pl.multiple_of(piece * CHUNK, 8), CHUNK)
        return pltpu.make_async_remote_copy(
            src_ref=anchor.at[:, rows, :], dst_ref=owned.at[pl.ds(source * F, F), spot, :],
            send_sem=move_send.at[source, piece], recv_sem=move_recv.at[source, piece],
            device_id=(r, c, source), device_id_type=MESH,
        )

    loads[0].wait()
    send_halos(0, (10, 11))
    send_halos(0, range(4, 10))
    pack_columns(0)
    send_halos(0, range(4))
    send_halos(0, range(12, 10 + 2 * nz))
    zero_tile = jnp.zeros((8, 128), jnp.float32)

    def store_gram(i, j, value):
        row = jnp.sum(value, axis=0, keepdims=True)
        sums[j, i : i + 1, :] = row
        if i // 4 != j // 4:
            sums[i, j : j + 1, :] = row

    gram_blocks = [(i, j) for i in range(0, rank, 4) for j in range(i, rank, 4)]

    def gram_part(which):
        for n in which:
            i, j = gram_blocks[n]
            products(
                basis, basis, range(i, i + 4), range(j, j + 4), 0, H,
                lambda i, j: zero_tile, store_gram,
            )

    def store_cross(i, j, value):
        cross[j, i] = value

    for load in loads[1:]:
        load.wait()

    @pl.loop(0, H // 8)
    def _(step):
        rows = pl.ds(pl.multiple_of(step * 8, 8), 8)
        totals = [None] * F
        for q in range(rank):
            plane = basis[q, rows, :]
            for f in range(F):
                term = coeff_ref[f, q] * plane
                totals[f] = term if totals[f] is None else totals[f] + term
        for f in range(F):
            lifted = dual_scale * mult[f, rows, :]
            anchor[f, rows, :] = video[f, rows, :] + lifted
            target[f, rows, :] = video[f, rows, :] - totals[f] + lifted

    count = len(gram_blocks)
    cuts = (0, count * 2 // 5, count * 7 // 10, count)
    gram_part(range(cuts[0], cuts[1]))
    for k in range(PASSES):
        last = k == PASSES - 1
        wait_halos(k, range(10))
        prepare_columns(k)
        for b in range(nz):
            if b == 0:
                wait_halos(k, (10, 11))
            if b + 1 < nz:
                wait_halos(k, (12 + 2 * b, 13 + 2 * b))
            sweep(k, last, b)
            if last:
                for i in range(0, rank, 4):
                    products(
                        basis, anchor, range(i, i + 4), range(F), b * own, own,
                        (lambda i, j: zero_tile) if b == 0 else (lambda i, j: cross[j, i]),
                        store_cross,
                    )
            elif 2 * b < nz:
                send_halos(k + 1, (10 + 2 * b, 11 + 2 * b))
        if not last:
            send_halos(k + 1, range(4, 10))
            pack_columns(k + 1)
            send_halos(k + 1, range(4))
            send_halos(k + 1, range(10 + 2 * ((nz + 1) // 2), 10 + 2 * nz))
            gram_part(range(cuts[k + 1], cuts[k + 2]))

    for j in range(F):
        for i in range(rank):
            sums[rank + j, i : i + 1, :] = jnp.sum(cross[j, i], axis=0, keepdims=True)

    lane_r = lax.broadcasted_iota(jnp.int32, (rank, 128), 1)
    row_r = lax.broadcasted_iota(jnp.int32, (rank, 128), 0)
    part = jnp.zeros((rank, 128), jnp.float32)
    for q in range(rank + F):
        part = jnp.where(lane_r == q, jnp.sum(sums[q], axis=1, keepdims=True), part)
    group = nr * nc
    me = r * nc + c
    parts[me] = part

    def share_part(d):
        other = lax.rem(me + d, group)
        return pltpu.make_async_remote_copy(
            src_ref=parts.at[me], dst_ref=parts.at[me],
            send_sem=part_send.at[d], recv_sem=part_recv.at[d],
            device_id=(other // nc, lax.rem(other, nc), z), device_id_type=MESH,
        )

    def take_part(d):
        other = lax.rem(me - d + group, group)
        return pltpu.make_async_remote_copy(
            src_ref=parts.at[me], dst_ref=parts.at[other],
            send_sem=part_send.at[d], recv_sem=part_recv.at[d],
            device_id=(other // nc, lax.rem(other, nc), z), device_id_type=MESH,
        )

    for d in range(1, group):
        share_part(d).start()
    pixel_ridge = ridge_share * H * W * group
    diagonal = lane_r == row_r
    before = jnp.zeros((rank, 128), jnp.float32)
    for q in range(rank):
        for f in range(F):
            before = jnp.where((row_r == q) & (lane_r == rank + f), coeff_ref[f, q], before)
    for d in range(1, group):
        take_part(d).wait_recv()
    total = parts[0]
    for i in range(1, group):
        total = total + parts[i]
    total = total + pixel_ridge * (jnp.where(diagonal, 1.0, 0.0) + before)
    solved = eliminate(total, rank)
    shares[z] = solved

    def share_rows(d):
        return pltpu.make_async_remote_copy(
            src_ref=shares.at[z], dst_ref=shares.at[z],
            send_sem=share_send.at[d], recv_sem=share_recv.at[d],
            device_id=(r, c, lax.rem(z + d, nz)), device_id_type=MESH,
        )

    def take_rows(d):
        source = lax.rem(z - d + nz, nz)
        return pltpu.make_async_remote_copy(
            src_ref=shares.at[z], dst_ref=shares.at[source],
            send_sem=share_send.at[d], recv_sem=share_recv.at[d],
            device_id=(r, c, source), device_id_type=MESH,
        )

    for d in range(1, nz):
        share_rows(d).start()
    for b in range(nz):
        @pl.when((z != b) & held(b))
        def _(b=b):
            for p in range(pieces):
                move(b, p).start()
    square[...] = jnp.zeros_like(square)
    square[0:rank, :] = solved
    coeff_out[...] = square[...].T[rank : rank + F, 0:rank]
    for d in range(1, nz):
        take_rows(d).wait_recv()
    frames = F * nz
    wide = jnp.zeros((rank, 128), jnp.float32)
    for i in range(nz):
        placed = shares[i] if i == 0 else pltpu.roll(shares[i], i * F, 1)
        wide = jnp.where(
            (lane_r >= rank + i * F) & (lane_r < rank + (i + 1) * F), placed, wide
        )
    square[0:rank, :] = wide
    gram = lax.dot_general(
        wide, square[...], (((1,), (1,)), ((), ())),
        precision=lax.Precision.HIGHEST, preferred_element_type=jnp.float32,
    )
    frame_ridge = ridge_share * frames
    system = jnp.where(diagonal, gram + frame_ridge, gram) + wide
    system = system + jnp.where(lane_r == row_r + rank + frames, frame_ridge, 0.0)
    table[...] = eliminate(system, rank)
    to_scalar = pltpu.make_async_copy(table, table_smem, small_sem.at[1])
    to_scalar.start()
    to_scalar.wait()
    my_base = z * own

    @pl.loop(0, own // 8)
    def _(step):
        rows = pl.ds(pl.multiple_of(step * 8, 8), 8)
        old = pl.ds(pl.multiple_of(my_base + step * 8, 8), 8)
        for half in range(0, rank, 8):
            totals = [None] * 8
            for f in range(F + rank):
                plane = anchor[f, old, :] if f < F else basis[f - F, old, :]
                place = rank + z * F + f if f < F else rank + frames + f - F
                for q in range(8):
                    term = table_smem[half + q, place] * plane
                    totals[q] = term if totals[q] is None else totals[q] + term
            for q in range(8):
                fresh[half + q, rows, :] = totals[q]

    for n in range(nz - 1):
        near = n + (n >= z).astype(jnp.int32)
        far = nz - 1 - (n + (n >= nz - 1 - z).astype(jnp.int32))
        source = jnp.where(2 * z < nz, near, far)

        @pl.loop(0, pieces)
        def _(piece, source=source):
            take(source, piece).wait_recv()
            for step in range(CHUNK // 8):
                rows = pl.ds(pl.multiple_of(piece * CHUNK + step * 8, 8), 8)
                planes = [owned[source * F + f, rows, :] for f in range(F)]
                for q in range(rank):
                    value = fresh[q, rows, :]
                    for f in range(F):
                        value = value + table_smem[q, rank + source * F + f] * planes[f]
                    fresh[q, rows, :] = value

    for k in range(PASSES):
        finish_sends(k)
    for b in range(nz):
        @pl.when(z != b)
        def _(b=b):
            for p in range(pieces):
                move(b, p).wait_send()
    for d in range(1, nz):
        share_rows(d).wait_send()
    for d in range(1, group):
        share_part(d).wait_send()


def deliver(shrunk, coeff, fresh, shrunk_hbm, coeff_hbm, fresh_hbm, sems):
    copies = [
        pltpu.make_async_copy(source, place, sems.at[i])
        for i, (source, place) in enumerate(
            ((fresh, fresh_hbm), (shrunk, shrunk_hbm), (coeff, coeff_hbm))
        )
    ]
    for copy in copies:
        copy.start()
    for copy in copies:
        copy.wait()


def whole_kernel(video, multiplier, foreground, basis, coefficients):
    F, H, W = video.shape
    rank = basis.shape[0]
    nr, nc, nz = (lax.axis_size(name) for name in ("row", "col", "frame"))
    f32 = jnp.float32
    own = H // nz
    group = nr * nc
    vmem = pltpu.VMEM
    dma = pltpu.SemaphoreType.DMA
    pieces = own // CHUNK
    hbm = pl.BlockSpec(memory_space=pl.ANY)
    on_chip = pl.BlockSpec(memory_space=pltpu.VMEM)
    found = pl.pallas_call(
        functools.partial(kernel, (F, H, W, rank, nr, nc, nz)),
        out_shape=(vmem((F, H, W), f32), vmem((F, rank), f32), vmem((rank, own, W), f32)),
        in_specs=[hbm] * 5,
        out_specs=[on_chip] * 3,
        scratch_shapes=[vmem((F + 2, H + 16, W), f32)] * PASSES
        + [
            vmem((F, H, W), f32),
            vmem((F, H, W), f32),
            vmem((rank, H, W), f32),
            vmem((F, H, W), f32),
            vmem((F, H, W), f32),
            vmem((F * nz, own, W), f32),
            vmem((PASSES, 2, 8, H), f32),
            vmem((PASSES, 4, 8, H), f32),
            vmem((PASSES, 2, F, 8, 128), f32),
            vmem((H + 16, 128), f32),
            vmem((H, 128), f32),
            vmem((H, 128), f32),
            vmem((F, rank, 8, 128), f32),
            vmem((rank + F, rank, 128), f32),
            vmem((group, rank, 128), f32),
            vmem((nz, rank, 128), f32),
            vmem((128, 128), f32),
            vmem((rank, 128), f32),
            pltpu.SMEM((F, rank), f32),
            pltpu.SMEM((rank, 128), f32),
            dma((5,)),
            dma((PASSES, 10 + 2 * nz)),
            dma((PASSES, 10 + 2 * nz)),
            dma((group,)),
            dma((group,)),
            dma((nz,)),
            dma((nz,)),
            dma((nz, pieces)),
            dma((nz, pieces)),
            dma((2,)),
        ],
        compiler_params=pltpu.CompilerParams(
            collective_id=0, has_side_effects=True, vmem_limit_bytes=32 * 1024 * 1024
        ),
    )(
        *(
            pltpu.with_memory_space_constraint(x, pltpu.HBM)
            for x in (coefficients, video, multiplier, foreground, basis)
        )
    )
    return pl.pallas_call(
        deliver,
        out_shape=(
            jax.ShapeDtypeStruct((F, H, W), f32),
            jax.ShapeDtypeStruct((F, rank), f32),
            jax.ShapeDtypeStruct((rank, own, W), f32),
        ),
        in_specs=[on_chip] * 3,
        out_specs=[hbm] * 3,
        scratch_shapes=[dma((3,))],
    )(*(pltpu.with_memory_space_constraint(x, pltpu.VMEM) for x in found))


def body(video, multiplier, foreground, basis, coefficients):
    F, H, W = video.shape
    rank = basis.shape[0]
    nz = lax.axis_size("frame")
    fits = (
        H % nz == 0 and (H // nz) % 8 == 0 and (H // nz) % CHUNK == 0 and W % 128 == 0
        and F <= 8 and rank % 8 == 0 and 2 * rank + F * nz <= 128
    )
    run = whole_kernel if fits else local
    return run(video, multiplier, foreground, basis, coefficients)


def solution(mesh):
    placed = (
        P("frame", "row", "col"),
        P("frame", "row", "col"),
        P("frame", "row", "col"),
        P(None, "row", "col"),
        P("frame", None),
    )
    return jax.shard_map(
        body,
        mesh=mesh,
        in_specs=placed,
        out_specs=(P("frame", "row", "col"), P("frame", None), P(None, ("row", "frame"), "col")),
        check_vma=False,
    )
```

```python
import functools

import jax
import jax.numpy as jnp
from jax import lax
from jax.experimental import pallas as pl
from jax.experimental.pallas import tpu as pltpu
from jax.sharding import PartitionSpec as P

PASSES = 3


relax_rate = 0.8
smooth_weight = 0.5
smooth_floor = 0.25
shrink_level = 0.4
dual_scale = 0.8
ridge_share = 0.1


def with_halo(block, sides, width):
    for axis, dim in sides:
        count = lax.axis_size(axis)
        forward = [(i, i + 1) for i in range(count - 1)]
        backward = [(target, source) for source, target in forward]
        low = lax.ppermute(
            lax.slice_in_dim(block, block.shape[dim] - width, None, axis=dim), axis, forward
        )
        high = lax.ppermute(lax.slice_in_dim(block, 0, width, axis=dim), axis, backward)
        block = jnp.concatenate([low, block, high], axis=dim)
    return block


def forward_cells(padded, direction, shape):
    starts = [0, 0, 0]
    starts[direction] = 1
    limits = [starts[axis_dim] + shape[axis_dim] for axis_dim in range(3)]
    return lax.slice(padded, starts, limits)


def descend(padded, source, anchor, extent):
    shape = tuple((int(length) - 1 for length in padded.shape))
    here_cells = padded[:-1, :-1, :-1]
    slopes = []
    for direction in range(3):
        ahead_cells = forward_cells(padded, direction, shape)
        places = anchor[direction] + jnp.arange(shape[direction], dtype=jnp.int32)
        inside = (places >= 0) & (places < extent[direction] - 1)
        layout = [1, 1, 1]
        layout[direction] = shape[direction]
        inside = inside.reshape(layout)
        slopes.append(jnp.where(inside, ahead_cells - here_cells, jnp.zeros_like(here_cells)))
    weight = lax.rsqrt(
        smooth_floor + slopes[0] * slopes[0] + slopes[1] * slopes[1] + slopes[2] * slopes[2]
    )
    fluxes = [slope_part * weight for slope_part in slopes]
    spread = (
        fluxes[0][1:, 1:, 1:]
        - fluxes[0][:-1, 1:, 1:]
        + (fluxes[1][1:, 1:, 1:] - fluxes[1][1:, :-1, 1:])
        + (fluxes[2][1:, 1:, 1:] - fluxes[2][1:, 1:, :-1])
    )
    center = padded[1:-1, 1:-1, 1:-1]
    return center + relax_rate * (source - center + smooth_weight * spread)


def solve_definite(matrix, right_side):
    factor_lower = jnp.linalg.cholesky(matrix)
    half_solved = lax.linalg.triangular_solve(factor_lower, right_side, left_side=True, lower=True)
    return lax.linalg.triangular_solve(
        factor_lower, half_solved, left_side=True, lower=True, transpose_a=True
    )


def local(video, multiplier, foreground, basis, coefficients):
    highest = lax.Precision.HIGHEST
    frames_here, rows_here, cols_here = video.shape
    rank_size = basis.shape[0]
    frame_count = lax.axis_size("frame")
    row_count = lax.axis_size("row")
    col_count = lax.axis_size("col")
    extent = (frames_here * frame_count, rows_here * row_count, cols_here * col_count)
    frame_slot = lax.axis_index("frame")
    corner = (
        frame_slot * frames_here,
        lax.axis_index("row") * rows_here,
        lax.axis_index("col") * cols_here,
    )
    pixels = rows_here * cols_here
    flat_basis = basis.reshape(rank_size, pixels)
    background = jnp.dot(coefficients, flat_basis, precision=highest).reshape(video.shape)
    target = video - background + dual_scale * multiplier
    current = foreground
    for sweep in range(PASSES):
        padded = with_halo(current, (("row", 1), ("col", 2), ("frame", 0)), 1)
        current = descend(padded, target, tuple((start_cell - 1 for start_cell in corner)), extent)
    shrunk = current - jnp.clip(current, -shrink_level, shrink_level)
    residual_target = video + dual_scale * multiplier - shrunk
    flat_target = residual_target.reshape(frames_here, pixels)
    gram_part = jnp.dot(flat_basis, flat_basis.T, precision=highest)
    cross_part = jnp.dot(flat_basis, flat_target.T, precision=highest)
    gram_sum, cross_sum = lax.psum((gram_part, cross_part), ("row", "col"))
    identity_matrix = jnp.eye(rank_size, dtype=gram_sum.dtype)
    pixel_ridge = ridge_share * pixels * row_count * col_count
    coeff_rows = solve_definite(
        gram_sum + pixel_ridge * identity_matrix, cross_sum + pixel_ridge * coefficients.T
    )
    total_part = jnp.dot(coeff_rows, flat_target, precision=highest).reshape(
        rank_size, rows_here, cols_here
    )
    frame_gram_part = jnp.dot(coeff_rows, coeff_rows.T, precision=highest)
    owned_rows = rows_here // frame_count
    owned_sums = lax.psum_scatter(total_part, "frame", scatter_dimension=1, tiled=True)
    frame_gram = lax.psum(frame_gram_part, "frame")
    old_owned = lax.dynamic_slice_in_dim(basis, frame_slot * owned_rows, owned_rows, 1)
    frame_ridge = ridge_share * frames_here * frame_count
    right_side = (owned_sums + frame_ridge * old_owned).reshape(rank_size, owned_rows * cols_here)
    new_basis = solve_definite(frame_gram + frame_ridge * identity_matrix, right_side)
    return (shrunk, coeff_rows.T, new_basis.reshape(rank_size, owned_rows, cols_here))


MESH = pl.DeviceIdType.MESH
CHUNK = 24


def eliminate(matrix, size):
    lanes = lax.broadcasted_iota(jnp.int32, matrix.shape, 1)
    rows = lax.broadcasted_iota(jnp.int32, matrix.shape, 0)
    for k in range(size):
        pivot = matrix[k : k + 1, k : k + 1]
        scaled = matrix[k : k + 1, :] / pivot
        column = jnp.sum(jnp.where(lanes == k, matrix, 0.0), axis=1, keepdims=True)
        matrix = jnp.where(rows == k, scaled, matrix - column * scaled)
    return matrix


def kernel(
    sizes, coeff_hbm, video_hbm, mult_hbm, fore_hbm, basis_hbm,
    result, coeff_out, fresh,
    field0, field1, field2, video, mult, basis, anchor, target, owned,
    packed, arrived, corner, edge_next, edge_flux, first_cols, left_now, left_next,
    cross, sums, grams, parts, shares, square, table, coeff_ref, table_smem,
    in_sems, halo_send, halo_recv, part_send, part_recv,
    gram_send, gram_recv, share_send, share_recv, move_send, move_recv, small_sem,
):
    field = (field0, field1, field2)
    F, H, W, rank, nr, nc, nz = sizes
    r = lax.axis_index("row")
    c = lax.axis_index("col")
    z = lax.axis_index("frame")
    own = H // nz
    pieces = own // CHUNK
    half = H // 2
    flip = lax.rem(r, 2)

    steps = H // CHUNK

    def chunk_at(step):
        return step + flip * (steps - 1 - 2 * step)

    def rows_at(step, offset=0):
        return pl.ds(pl.multiple_of(offset + chunk_at(step) * CHUNK, 8), CHUNK)

    def half_start(h):
        return pl.multiple_of((h + flip * (1 - 2 * h)) * half, 8)

    def inside(dr, dc, dz):
        ok = None
        for at, step, count in ((r, dr, nr), (c, dc, nc), (z, dz, nz)):
            if step != 0:
                test = (at + step >= 0) & (at + step < count)
                ok = test if ok is None else ok & test
        return ok

    halves = [pl.ds(half_start(h), half) for h in range(2)]
    loads = [
        pltpu.make_async_copy(src, dst, in_sems.at[i])
        for i, (src, dst) in enumerate(
            [
                (
                    fore_hbm.at[:, halves[h], :],
                    field0.at[1 : F + 1, pl.ds(pl.multiple_of(half_start(h) + 8, 8), half), :],
                )
                for h in range(2)
            ]
            + [(coeff_hbm, coeff_ref)]
            + [
                (src.at[:, rows, :], dst.at[:, rows, :])
                for rows in halves
                for src, dst in ((video_hbm, video), (mult_hbm, mult), (basis_hbm, basis))
            ]
        )
    ]
    for load in loads[:2]:
        load.start()

    barrier = pltpu.get_barrier_semaphore()
    for d in range(1, nr * nc):
        other = lax.rem(r * nc + c + d, nr * nc)
        pl.semaphore_signal(
            barrier, inc=1, device_id=(other // nc, lax.rem(other, nc), z), device_id_type=MESH
        )
    for d in range(1, nz):
        pl.semaphore_signal(
            barrier, inc=1, device_id=(r, c, lax.rem(z + d, nz)), device_id_type=MESH
        )
    diagonals = ((1, 0, -1), (-1, 0, 1), (0, 1, -1), (0, -1, 1))
    for step in diagonals:
        @pl.when(inside(*step))
        def _(step=step):
            pl.semaphore_signal(
                barrier,
                inc=1,
                device_id=(r + step[0], c + step[1], z + step[2]),
                device_id_type=MESH,
            )
    expected = jnp.int32(nr * nc - 1 + nz - 1)
    for step in diagonals:
        expected = expected + inside(*step).astype(jnp.int32)
    for load in loads[2:]:
        load.start()

    pl.semaphore_wait(barrier, expected)

    lane_h = lax.broadcasted_iota(jnp.int32, (half, 128), 1)

    def pack_columns(k, h):
        base = half_start(h)
        tile = jnp.zeros((half, 128), jnp.float32)
        for f in range(F):
            for lane, at in ((f, 0), (8 + f, W - 1)):
                lanes = field[k][f + 1, pl.ds(base + 8, half), (at // 128) * 128 : (at // 128) * 128 + 128]
                tile = jnp.where(lane_h == lane, lanes[:, at % 128 : at % 128 + 1], tile)
        first_cols[pl.ds(base, half), :] = tile
        packed[k, h] = tile.T[:16, :]

    strips = range(8, 12)
    corners = (12, 13)

    def columns_of(h):
        return range(4 * h, 4 * h + 4)

    def halo_list(k):
        fk = field[k]
        mid = slice(1, F + 1)
        return tuple(
            strip
            for h in range(2)
            for strip in (
                (packed.at[k, h, 0:F], arrived.at[k, h, 1 : F + 1], (0, -1, 0)),
                (packed.at[k, h, 8 : 8 + F], arrived.at[k, h, 8 : 8 + F], (0, 1, 0)),
                (packed.at[k, h, F - 1 : F], arrived.at[k, h, 0:1], (0, -1, 1)),
                (packed.at[k, h, 8:9], arrived.at[k, h, 8 + F : 9 + F], (0, 1, -1)),
            )
        ) + (
            (fk.at[mid, H : H + 8, :], fk.at[mid, 0:8, :], (1, 0, 0)),
            (fk.at[mid, 8:16, :], fk.at[mid, H + 8 : H + 16, :], (-1, 0, 0)),
            (fk.at[F, 8:9, :], fk.at[0, H + 8 : H + 9, :], (-1, 0, 1)),
            (fk.at[1, H + 7 : H + 8, :], fk.at[F + 1, 7:8, :], (1, 0, -1)),
            (fk.at[mid, H : H + 8, 0:128], corner.at[k, 0], (1, -1, 0)),
            (fk.at[mid, 8:16, W - 128 : W], corner.at[k, 1], (-1, 1, 0)),
        )

    def halo_copy(k, i, src, dst, step):
        return pltpu.make_async_remote_copy(
            src_ref=src, dst_ref=dst,
            send_sem=halo_send.at[k, i], recv_sem=halo_recv.at[k, i],
            device_id=(r + step[0], c + step[1], z + step[2]), device_id_type=MESH,
        )

    def face(k, step, up):
        fk = field[k]
        rows = rows_at(step, 8)
        at = 14 + 2 * step + (0 if up else 1)
        mine, theirs = (F, 0) if up else (1, F + 1)
        src = fore_hbm.at[mine - 1, rows_at(step)] if k == 0 else fk.at[mine, rows]
        return halo_copy(k, at, src, fk.at[theirs, rows], (0, 0, 1 if up else -1))

    def send_faces(k, low, high):
        @pl.loop(low, high)
        def _(step):
            for up in (True, False):
                @pl.when(inside(0, 0, 1 if up else -1))
                def _(up=up):
                    face(k, step, up).start()

    def wait_face(k, step):
        for up in (True, False):
            @pl.when(inside(0, 0, -1 if up else 1))
            def _(up=up):
                face(k, step, up).wait_recv()

    def send_halos(k, which):
        every = halo_list(k)
        for i in which:
            src, dst, step = every[i]

            @pl.when(inside(*step))
            def _(i=i, src=src, dst=dst, step=step):
                halo_copy(k, i, src, dst, step).start()

    def wait_halos(k, which):
        every = halo_list(k)
        for i in which:
            src, dst, step = every[i]

            @pl.when(inside(*(-s for s in step)))
            def _(i=i, src=src, dst=dst, step=step):
                halo_copy(k, i, src, dst, step).wait_recv()

    def finish_sends(k):
        for i, (src, dst, step) in enumerate(halo_list(k)):
            @pl.when(inside(*step))
            def _(i=i, src=src, dst=dst, step=step):
                halo_copy(k, i, src, dst, step).wait_send()

        @pl.loop(0, steps)
        def _(step):
            for up in (True, False):
                @pl.when(inside(0, 0, 1 if up else -1))
                def _(up=up):
                    face(k, step, up).wait_send()

    def prepare_columns(k, h):
        base = half_start(h)
        spread = jnp.concatenate(
            [arrived[k, h], jnp.zeros((112, half), jnp.float32)], axis=0
        ).T
        edge_next[pl.ds(base + 8, half), :] = spread
        left_now[pl.ds(base, half), :] = pltpu.roll(spread, 120, 1)
        left_next[pl.ds(base, half), :] = pltpu.roll(spread, 119, 1)
        low, count, bottom = base, half, jnp.zeros((1, 128), jnp.float32)
        if h == 1:
            lane8 = lax.broadcasted_iota(jnp.int32, (8, 128), 1)
            top = jnp.zeros((8, 128), jnp.float32)
            for f in range(F):
                top = jnp.where(lane8 == f + 1, corner[k, 0, f][:, 0:1], top)
                bottom = jnp.where(lane8[:1] == f, corner[k, 1, f][0:1, 127:128], bottom)
            edge_next[0:8, :] = top
            low, count = pl.multiple_of((1 - flip) * (half - 8), 8), half + 8
        here = left_now[pl.ds(low, count), :]
        ahead = left_next[pl.ds(low, count), :]
        lane = lax.broadcasted_iota(jnp.int32, (count, 128), 1)
        row = lax.broadcasted_iota(jnp.int32, (count, 128), 0) + low
        slope0 = jnp.where((lane == F - 1) & (z == nz - 1), 0.0, ahead - here)
        after = left_now[pl.ds(low, count + 8), :]
        below = jnp.where(row == H - 1, bottom, pltpu.roll(after, count + 7, 0)[:count])
        slope1 = jnp.where((row == H - 1) & (r == nr - 1), 0.0, below - here)
        slope2 = first_cols[pl.ds(low, count), :] - here
        weight = lax.rsqrt(smooth_floor + slope0 * slope0 + slope1 * slope1 + slope2 * slope2)
        edge_flux[pl.ds(low, count), :] = jnp.where(c == 0, 0.0, slope2 * weight)

    def sweep(k, last, start):
        R = CHUNK
        lane_t = lax.broadcasted_iota(jnp.int32, (R + 8, 128), 1)
        row_t = lax.broadcasted_iota(jnp.int32, (R + 8, W), 0) + (r * H + start - 8)
        lane_w = lax.broadcasted_iota(jnp.int32, (R + 8, W), 1)
        blocked = (row_t < 0) | (row_t >= nr * H - 1)
        columns = edge_next[pl.ds(start, R + 8), :]
        fluxes_in = edge_flux[pl.ds(start, R), :]
        now = field[k][0, pl.ds(start, R + 16), :]
        flux0_before = None
        for f in range(-1, F):
            after = field[k][f + 2, pl.ds(start, R + 16), :]
            here = now[: R + 8]
            below = pltpu.roll(now, R + 15, 0)[: R + 8]
            ahead = after[: R + 8]
            wall = columns[:, f + 1 : f + 2]
            beyond = jnp.where(c == nc - 1, here, jnp.broadcast_to(wall, here.shape))
            right = jnp.where(lane_w == W - 1, beyond, pltpu.roll(here, W - 1, 1))
            slope0 = ahead - here
            if f == F - 1:
                slope0 = jnp.where(z == nz - 1, 0.0, slope0)
            slope1 = jnp.where(blocked, 0.0, below - here)
            slope2 = right - here
            weight = lax.rsqrt(
                smooth_floor + slope0 * slope0 + slope1 * slope1 + slope2 * slope2
            )
            flux0 = (slope0 * weight)[8:]
            if f < 0:
                flux0 = jnp.where(z == 0, 0.0, flux0)
            else:
                flux1 = jnp.where(row_t < 0, 0.0, slope1 * weight)
                flux2 = (slope2 * weight)[8:]
                above = pltpu.roll(flux1, 1, 0)[8:]
                left = jnp.where(
                    lane_w[8:] == 0,
                    jnp.broadcast_to(fluxes_in[:, f : f + 1], flux2.shape),
                    pltpu.roll(flux2, 1, 1),
                )
                spread = flux0 - flux0_before + (flux1[8:] - above) + (flux2 - left)
                center = here[8:]
                at = pl.ds(start, R)
                value = center + relax_rate * (
                    target[f, at, :] - center + smooth_weight * spread
                )
                if last:
                    shrunk = value - jnp.clip(value, -shrink_level, shrink_level)
                    result[f, at, :] = shrunk
                    anchor[f, at, :] = anchor[f, at, :] - shrunk
                else:
                    field[k + 1][f + 1, pl.ds(start + 8, R), :] = value
            flux0_before = flux0
            now = after

    def products(left_of, right_of, lefts, rights, first, count, start, store):
        def body(step, totals):
            rows = pl.ds(pl.multiple_of(first + step * 8, 8), 8)
            a = [left_of[i, rows, :] for i in lefts]
            b = [right_of[j, rows, :] for j in rights]
            out = []
            for x in range(len(lefts)):
                for y in range(len(rights)):
                    prod = a[x] * b[y]
                    total = totals[len(out)]
                    for w in range(W // 128):
                        total = total + prod[:, w * 128 : w * 128 + 128]
                    out.append(total)
            return tuple(out)

        totals = lax.fori_loop(
            0, count // 8, body, tuple(start(i, j) for i in lefts for j in rights), unroll=3 if count % 24 == 0 else 1
        )
        n = 0
        for i in lefts:
            for j in rights:
                store(i, j, totals[n])
                n += 1

    def held(block):
        return (block - z >= 2) | (z - block >= 2)

    def move(block, piece):
        rows = pl.ds(pl.multiple_of(block * own + piece * CHUNK, 8), CHUNK)
        spot = pl.ds(pl.multiple_of(piece * CHUNK, 8), CHUNK)
        return pltpu.make_async_remote_copy(
            src_ref=anchor.at[:, rows, :], dst_ref=owned.at[pl.ds(z * F, F), spot, :],
            send_sem=move_send.at[block, piece], recv_sem=move_recv.at[z, piece],
            device_id=(r, c, block), device_id_type=MESH,
        )

    def take(source, piece):
        rows = pl.ds(pl.multiple_of(z * own + piece * CHUNK, 8), CHUNK)
        spot = pl.ds(pl.multiple_of(piece * CHUNK, 8), CHUNK)
        return pltpu.make_async_remote_copy(
            src_ref=anchor.at[:, rows, :], dst_ref=owned.at[pl.ds(source * F, F), spot, :],
            send_sem=move_send.at[source, piece], recv_sem=move_recv.at[source, piece],
            device_id=(r, c, source), device_id_type=MESH,
        )

    send_faces(0, 0, 1)
    for h in range(2):
        loads[h].wait()
        pack_columns(0, h)
        send_halos(0, columns_of(h))
    send_halos(0, strips)
    send_halos(0, corners)
    send_faces(0, 1, steps)

    zero_tile = jnp.zeros((8, 128), jnp.float32)

    def store_gram(i, j, value):
        row = jnp.sum(value, axis=0, keepdims=True)
        sums[j, i : i + 1, :] = row
        if i // 4 != j // 4:
            sums[i, j : j + 1, :] = row

    lane_r = lax.broadcasted_iota(jnp.int32, (rank, 128), 1)
    row_r = lax.broadcasted_iota(jnp.int32, (rank, 128), 0)

    def gram_share():
        for i in range(0, rank, 4):
            for j in range(i, rank, 4):
                products(
                    basis, basis, range(i, i + 4), range(j, j + 4), z * own, own,
                    lambda i, j: zero_tile, store_gram,
                )
        tile = jnp.zeros((rank, 128), jnp.float32)
        for q in range(rank):
            tile = jnp.where(lane_r == q, jnp.sum(sums[q], axis=1, keepdims=True), tile)
        grams[z] = tile

    def share_gram(d):
        return pltpu.make_async_remote_copy(
            src_ref=grams.at[z], dst_ref=grams.at[z],
            send_sem=gram_send.at[d], recv_sem=gram_recv.at[d],
            device_id=(r, c, lax.rem(z + d, nz)), device_id_type=MESH,
        )

    def take_gram(d):
        source = lax.rem(z - d + nz, nz)
        return pltpu.make_async_remote_copy(
            src_ref=grams.at[z], dst_ref=grams.at[source],
            send_sem=gram_send.at[d], recv_sem=gram_recv.at[d],
            device_id=(r, c, source), device_id_type=MESH,
        )

    def store_cross(i, j, value):
        cross[j, i] = value

    def find_target(h):
        for load in loads[3 + 3 * h : 6 + 3 * h]:
            load.wait()

        @pl.loop(0, half // 8)
        def _(step):
            rows = pl.ds(pl.multiple_of(half_start(h) + step * 8, 8), 8)
            totals = [None] * F
            for q in range(rank):
                plane = basis[q, rows, :]
                for f in range(F):
                    term = coeff_ref[f, q] * plane
                    totals[f] = term if totals[f] is None else totals[f] + term
            for f in range(F):
                lifted = dual_scale * mult[f, rows, :]
                anchor[f, rows, :] = video[f, rows, :] + lifted
                target[f, rows, :] = video[f, rows, :] - totals[f] + lifted

    loads[2].wait()
    find_target(0)

    def advance(k, step):
        start = pl.multiple_of(chunk_at(step) * CHUNK, 8)
        sweep(k, k == PASSES - 1, start)
        if k == PASSES - 1:
            place, piece = chunk_at(step) // pieces, lax.rem(chunk_at(step), pieces)

            @pl.when((place - z == 1) | (z - place == 1))
            def _():
                move(place, piece).start()

            for i in range(0, rank, 4):
                products(
                    basis, anchor, range(i, i + 4), range(F), start, CHUNK,
                    lambda i, j: cross[j, i], store_cross,
                )

    cross[...] = jnp.zeros_like(cross)
    middle = steps // 2
    for k in range(PASSES):
        last = k == PASSES - 1
        wait_halos(k, columns_of(0))
        prepare_columns(k, 0)
        wait_face(k, 0)

        @pl.loop(0, middle - 1)
        def _(step, k=k):
            wait_face(k, step + 1)
            advance(k, step)

        if k == 1:
            gram_share()
        wait_halos(k, columns_of(1))
        wait_halos(k, corners)
        prepare_columns(k, 1)
        wait_face(k, middle)
        advance(k, middle - 1)
        if not last:
            pack_columns(k + 1, 0)
            send_halos(k + 1, columns_of(0))
            send_faces(k + 1, 0, middle)
        if k == 0:
            find_target(1)

        @pl.loop(middle, steps - 1)
        def _(step, k=k):
            wait_face(k, step + 1)
            advance(k, step)

        wait_halos(k, strips)
        advance(k, steps - 1)
        if not last:
            send_halos(k + 1, strips)
            send_halos(k + 1, corners)
            pack_columns(k + 1, 1)
            send_halos(k + 1, columns_of(1))
            send_faces(k + 1, middle, steps)
            if k == PASSES - 2:
                for d in range(1, nz):
                    share_gram(d).start()

    inner = (z > 0) & (z < nz - 1)

    def send_held(turn, low, high):
        for b in range(nz):
            @pl.when(held(b) & turn)
            def _(b=b):
                for p in range(low, high):
                    move(b, p).start()

    send_held(inner, 0, 1)
    for j in range(F):
        for i in range(rank):
            sums[rank + j, i : i + 1, :] = jnp.sum(cross[j, i], axis=0, keepdims=True)

    part = jnp.zeros((rank, 128), jnp.float32)
    for q in range(rank, rank + F):
        part = jnp.where(lane_r == q, jnp.sum(sums[q], axis=1, keepdims=True), part)
    for d in range(1, nz):
        take_gram(d).wait_recv()
    for i in range(nz):
        part = part + grams[i]
    group = nr * nc
    me = r * nc + c
    parts[me] = part

    def share_part(d):
        other = lax.rem(me + d, group)
        return pltpu.make_async_remote_copy(
            src_ref=parts.at[me], dst_ref=parts.at[me],
            send_sem=part_send.at[d], recv_sem=part_recv.at[d],
            device_id=(other // nc, lax.rem(other, nc), z), device_id_type=MESH,
        )

    def take_part(d):
        other = lax.rem(me - d + group, group)
        return pltpu.make_async_remote_copy(
            src_ref=parts.at[me], dst_ref=parts.at[other],
            send_sem=part_send.at[d], recv_sem=part_recv.at[d],
            device_id=(other // nc, lax.rem(other, nc), z), device_id_type=MESH,
        )

    for d in range(1, group):
        share_part(d).start()
    pixel_ridge = ridge_share * H * W * group
    diagonal = lane_r == row_r
    before = jnp.zeros((rank, 128), jnp.float32)
    for q in range(rank):
        for f in range(F):
            before = jnp.where((row_r == q) & (lane_r == rank + f), coeff_ref[f, q], before)
    for d in range(1, group):
        take_part(d).wait_recv()
    total = parts[0]
    for i in range(1, group):
        total = total + parts[i]
    total = total + pixel_ridge * (jnp.where(diagonal, 1.0, 0.0) + before)
    solved = eliminate(total, rank)
    shares[z] = solved

    def share_rows(d):
        return pltpu.make_async_remote_copy(
            src_ref=shares.at[z], dst_ref=shares.at[z],
            send_sem=share_send.at[d], recv_sem=share_recv.at[d],
            device_id=(r, c, lax.rem(z + d, nz)), device_id_type=MESH,
        )

    def take_rows(d):
        source = lax.rem(z - d + nz, nz)
        return pltpu.make_async_remote_copy(
            src_ref=shares.at[z], dst_ref=shares.at[source],
            send_sem=share_send.at[d], recv_sem=share_recv.at[d],
            device_id=(r, c, source), device_id_type=MESH,
        )

    for d in range(1, nz):
        share_rows(d).start()

    send_held(inner, 1, pieces)
    square[...] = jnp.zeros_like(square)
    square[0:rank, :] = solved
    coeff_out[...] = square[...].T[rank : rank + F, 0:rank]
    for d in range(1, nz):
        take_rows(d).wait_recv()
    send_held(~inner, 0, pieces)
    frames = F * nz
    wide = jnp.zeros((rank, 128), jnp.float32)
    for i in range(nz):
        placed = shares[i] if i == 0 else pltpu.roll(shares[i], i * F, 1)
        wide = jnp.where(
            (lane_r >= rank + i * F) & (lane_r < rank + (i + 1) * F), placed, wide
        )
    square[0:rank, :] = wide
    gram = lax.dot_general(
        wide, square[...], (((1,), (1,)), ((), ())),
        precision=lax.Precision.HIGHEST, preferred_element_type=jnp.float32,
    )
    frame_ridge = ridge_share * frames
    system = jnp.where(diagonal, gram + frame_ridge, gram) + wide
    system = system + jnp.where(lane_r == row_r + rank + frames, frame_ridge, 0.0)
    table[...] = eliminate(system, rank)
    to_scalar = pltpu.make_async_copy(table, table_smem, small_sem.at[1])
    to_scalar.start()
    to_scalar.wait()
    my_base = z * own

    @pl.loop(0, own // 8)
    def _(step):
        rows = pl.ds(pl.multiple_of(step * 8, 8), 8)
        old = pl.ds(pl.multiple_of(my_base + step * 8, 8), 8)
        for half in range(0, rank, 8):
            totals = [None] * 8
            for f in range(F + rank):
                plane = anchor[f, old, :] if f < F else basis[f - F, old, :]
                place = rank + z * F + f if f < F else rank + frames + f - F
                for q in range(8):
                    term = table_smem[half + q, place] * plane
                    totals[q] = term if totals[q] is None else totals[q] + term
            for q in range(8):
                fresh[half + q, rows, :] = totals[q]

    for k in range(PASSES):
        finish_sends(k)
    for d in range(1, nz):
        share_rows(d).wait_send()
        share_gram(d).wait_send()
    for d in range(1, group):
        share_part(d).wait_send()

    for n in range(nz - 1):
        near = n + (n >= z).astype(jnp.int32)
        far = nz - 1 - (n + (n >= nz - 1 - z).astype(jnp.int32))
        source = jnp.where(2 * z < nz, near, far)

        @pl.loop(0, pieces)
        def _(piece, source=source):
            take(source, piece).wait_recv()
            for step in range(CHUNK // 8):
                rows = pl.ds(pl.multiple_of(piece * CHUNK + step * 8, 8), 8)
                planes = [owned[source * F + f, rows, :] for f in range(F)]
                for q in range(rank):
                    value = fresh[q, rows, :]
                    for f in range(F):
                        value = value + table_smem[q, rank + source * F + f] * planes[f]
                    fresh[q, rows, :] = value

    for b in range(nz):
        @pl.when(z != b)
        def _(b=b):
            for p in range(pieces):
                move(b, p).wait_send()


def deliver(shrunk, coeff, fresh, shrunk_hbm, coeff_hbm, fresh_hbm, sems):
    copies = [pltpu.make_async_copy(coeff, coeff_hbm, sems.at[0])]
    for source, place in ((fresh, fresh_hbm), (shrunk, shrunk_hbm)):
        share = source.shape[0] // 4
        for i in range(4):
            part = pl.ds(i * share, share)
            copies.append(
                pltpu.make_async_copy(source.at[part], place.at[part], sems.at[len(copies)])
            )
    for copy in copies:
        copy.start()
    for copy in copies:
        copy.wait()


def whole_kernel(video, multiplier, foreground, basis, coefficients):
    F, H, W = video.shape
    rank = basis.shape[0]
    nr, nc, nz = (lax.axis_size(name) for name in ("row", "col", "frame"))
    f32 = jnp.float32
    own = H // nz
    group = nr * nc
    vmem = pltpu.VMEM
    dma = pltpu.SemaphoreType.DMA
    pieces = own // CHUNK
    hbm = pl.BlockSpec(memory_space=pl.ANY)
    on_chip = pl.BlockSpec(memory_space=pltpu.VMEM)
    found = pl.pallas_call(
        functools.partial(kernel, (F, H, W, rank, nr, nc, nz)),
        out_shape=(vmem((F, H, W), f32), vmem((F, rank), f32), vmem((rank, own, W), f32)),
        in_specs=[hbm] * 5,
        out_specs=[on_chip] * 3,
        scratch_shapes=[vmem((F + 2, H + 16, W), f32)] * PASSES
        + [
            vmem((F, H, W), f32),
            vmem((F, H, W), f32),
            vmem((rank, H, W), f32),
            vmem((F, H, W), f32),
            vmem((F, H, W), f32),
            vmem((F * nz, own, W), f32),
            vmem((PASSES, 2, 16, H // 2), f32),
            vmem((PASSES, 2, 16, H // 2), f32),
            vmem((PASSES, 2, F, 8, 128), f32),
            vmem((H + 8, 128), f32),
            vmem((H, 128), f32),
            vmem((H, 128), f32),
            vmem((H + 8, 128), f32),
            vmem((H + 8, 128), f32),
            vmem((F, rank, 8, 128), f32),
            vmem((rank + F, rank, 128), f32),
            vmem((nz, rank, 128), f32),
            vmem((group, rank, 128), f32),
            vmem((nz, rank, 128), f32),
            vmem((128, 128), f32),
            vmem((rank, 128), f32),
            pltpu.SMEM((F, rank), f32),
            pltpu.SMEM((rank, 128), f32),
            dma((9,)),
            dma((PASSES, 14 + 2 * (H // CHUNK))),
            dma((PASSES, 14 + 2 * (H // CHUNK))),
            dma((group,)),
            dma((group,)),
            dma((nz,)),
            dma((nz,)),
            dma((nz,)),
            dma((nz,)),
            dma((nz, pieces)),
            dma((nz, pieces)),
            dma((2,)),
        ],
        compiler_params=pltpu.CompilerParams(
            collective_id=0, has_side_effects=True, vmem_limit_bytes=32 * 1024 * 1024
        ),
    )(
        *(
            pltpu.with_memory_space_constraint(x, pltpu.HBM)
            for x in (coefficients, video, multiplier, foreground, basis)
        )
    )
    return pl.pallas_call(
        deliver,
        out_shape=(
            jax.ShapeDtypeStruct((F, H, W), f32),
            jax.ShapeDtypeStruct((F, rank), f32),
            jax.ShapeDtypeStruct((rank, own, W), f32),
        ),
        in_specs=[on_chip] * 3,
        out_specs=[hbm] * 3,
        scratch_shapes=[dma((9,))],
    )(*(pltpu.with_memory_space_constraint(x, pltpu.VMEM) for x in found))


def body(video, multiplier, foreground, basis, coefficients):
    F, H, W = video.shape
    rank = basis.shape[0]
    nz = lax.axis_size("frame")
    fits = (
        H % nz == 0 and (H // nz) % 8 == 0 and (H // nz) % CHUNK == 0 and W % 128 == 0
        and H % 16 == 0 and (H // CHUNK) % 2 == 0 and lax.axis_size("row") <= 2
        and F % 4 == 0 and F < 8 and rank % 8 == 0 and 2 * rank + F * nz <= 128
    )
    run = whole_kernel if fits else local
    return run(video, multiplier, foreground, basis, coefficients)


def solution(mesh):
    placed = (
        P("frame", "row", "col"),
        P("frame", "row", "col"),
        P("frame", "row", "col"),
        P(None, "row", "col"),
        P("frame", None),
    )
    return jax.shard_map(
        body,
        mesh=mesh,
        in_specs=placed,
        out_specs=(P("frame", "row", "col"), P("frame", None), P(None, ("row", "frame"), "col")),
        check_vma=False,
    )
```

```python
import functools

import jax
import jax.numpy as jnp
from jax import lax
from jax.experimental import pallas as pl
from jax.experimental.pallas import tpu as pltpu
from jax.sharding import PartitionSpec as P

PASSES = 3


relax_rate = 0.8
smooth_weight = 0.5
smooth_floor = 0.25
shrink_level = 0.4
dual_scale = 0.8
ridge_share = 0.1


def with_halo(block, sides, width):
    for axis, dim in sides:
        count = lax.axis_size(axis)
        forward = [(i, i + 1) for i in range(count - 1)]
        backward = [(target, source) for source, target in forward]
        low = lax.ppermute(
            lax.slice_in_dim(block, block.shape[dim] - width, None, axis=dim), axis, forward
        )
        high = lax.ppermute(lax.slice_in_dim(block, 0, width, axis=dim), axis, backward)
        block = jnp.concatenate([low, block, high], axis=dim)
    return block


def forward_cells(padded, direction, shape):
    starts = [0, 0, 0]
    starts[direction] = 1
    limits = [starts[axis_dim] + shape[axis_dim] for axis_dim in range(3)]
    return lax.slice(padded, starts, limits)


def descend(padded, source, anchor, extent):
    shape = tuple((int(length) - 1 for length in padded.shape))
    here_cells = padded[:-1, :-1, :-1]
    slopes = []
    for direction in range(3):
        ahead_cells = forward_cells(padded, direction, shape)
        places = anchor[direction] + jnp.arange(shape[direction], dtype=jnp.int32)
        inside = (places >= 0) & (places < extent[direction] - 1)
        layout = [1, 1, 1]
        layout[direction] = shape[direction]
        inside = inside.reshape(layout)
        slopes.append(jnp.where(inside, ahead_cells - here_cells, jnp.zeros_like(here_cells)))
    weight = lax.rsqrt(
        smooth_floor + slopes[0] * slopes[0] + slopes[1] * slopes[1] + slopes[2] * slopes[2]
    )
    fluxes = [slope_part * weight for slope_part in slopes]
    spread = (
        fluxes[0][1:, 1:, 1:]
        - fluxes[0][:-1, 1:, 1:]
        + (fluxes[1][1:, 1:, 1:] - fluxes[1][1:, :-1, 1:])
        + (fluxes[2][1:, 1:, 1:] - fluxes[2][1:, 1:, :-1])
    )
    center = padded[1:-1, 1:-1, 1:-1]
    return center + relax_rate * (source - center + smooth_weight * spread)


def solve_definite(matrix, right_side):
    factor_lower = jnp.linalg.cholesky(matrix)
    half_solved = lax.linalg.triangular_solve(factor_lower, right_side, left_side=True, lower=True)
    return lax.linalg.triangular_solve(
        factor_lower, half_solved, left_side=True, lower=True, transpose_a=True
    )


def local(video, multiplier, foreground, basis, coefficients):
    highest = lax.Precision.HIGHEST
    frames_here, rows_here, cols_here = video.shape
    rank_size = basis.shape[0]
    frame_count = lax.axis_size("frame")
    row_count = lax.axis_size("row")
    col_count = lax.axis_size("col")
    extent = (frames_here * frame_count, rows_here * row_count, cols_here * col_count)
    frame_slot = lax.axis_index("frame")
    corner = (
        frame_slot * frames_here,
        lax.axis_index("row") * rows_here,
        lax.axis_index("col") * cols_here,
    )
    pixels = rows_here * cols_here
    flat_basis = basis.reshape(rank_size, pixels)
    background = jnp.dot(coefficients, flat_basis, precision=highest).reshape(video.shape)
    target = video - background + dual_scale * multiplier
    current = foreground
    for sweep in range(PASSES):
        padded = with_halo(current, (("row", 1), ("col", 2), ("frame", 0)), 1)
        current = descend(padded, target, tuple((start_cell - 1 for start_cell in corner)), extent)
    shrunk = current - jnp.clip(current, -shrink_level, shrink_level)
    residual_target = video + dual_scale * multiplier - shrunk
    flat_target = residual_target.reshape(frames_here, pixels)
    gram_part = jnp.dot(flat_basis, flat_basis.T, precision=highest)
    cross_part = jnp.dot(flat_basis, flat_target.T, precision=highest)
    gram_sum, cross_sum = lax.psum((gram_part, cross_part), ("row", "col"))
    identity_matrix = jnp.eye(rank_size, dtype=gram_sum.dtype)
    pixel_ridge = ridge_share * pixels * row_count * col_count
    coeff_rows = solve_definite(
        gram_sum + pixel_ridge * identity_matrix, cross_sum + pixel_ridge * coefficients.T
    )
    total_part = jnp.dot(coeff_rows, flat_target, precision=highest).reshape(
        rank_size, rows_here, cols_here
    )
    frame_gram_part = jnp.dot(coeff_rows, coeff_rows.T, precision=highest)
    owned_rows = rows_here // frame_count
    owned_sums = lax.psum_scatter(total_part, "frame", scatter_dimension=1, tiled=True)
    frame_gram = lax.psum(frame_gram_part, "frame")
    old_owned = lax.dynamic_slice_in_dim(basis, frame_slot * owned_rows, owned_rows, 1)
    frame_ridge = ridge_share * frames_here * frame_count
    right_side = (owned_sums + frame_ridge * old_owned).reshape(rank_size, owned_rows * cols_here)
    new_basis = solve_definite(frame_gram + frame_ridge * identity_matrix, right_side)
    return (shrunk, coeff_rows.T, new_basis.reshape(rank_size, owned_rows, cols_here))


MESH = pl.DeviceIdType.MESH
CHUNK = 24
SEGMENTS = 4


def eliminate(matrix, size):
    lanes = lax.broadcasted_iota(jnp.int32, matrix.shape, 1)
    rows = lax.broadcasted_iota(jnp.int32, matrix.shape, 0)
    for k in range(size):
        pivot = matrix[k : k + 1, k : k + 1]
        scaled = matrix[k : k + 1, :] / pivot
        column = jnp.sum(jnp.where(lanes == k, matrix, 0.0), axis=1, keepdims=True)
        matrix = jnp.where(rows == k, scaled, matrix - column * scaled)
    return matrix


def kernel(
    sizes, coeff_hbm, video_hbm, mult_hbm, fore_hbm, basis_hbm,
    result, coeff_out, fresh,
    field0, field1, field2, video, mult, basis, anchor, target, owned,
    packed, arrived, corner, edge_next, edge_flux, first_cols, left_now, left_next, bottom_row,
    cross, sums, grams, parts, shares, square, table, coeff_ref, table_smem,
    in_sems, halo_send, halo_recv, part_send, part_recv,
    gram_send, gram_recv, share_send, share_recv, move_send, move_recv, small_sem,
):
    field = (field0, field1, field2)
    F, H, W, rank, nr, nc, nz = sizes
    r = lax.axis_index("row")
    c = lax.axis_index("col")
    z = lax.axis_index("frame")
    own = H // nz
    pieces = own // CHUNK
    half = H // 2
    flip = lax.rem(r, 2)

    steps = H // CHUNK

    def chunk_at(step):
        return step + flip * (steps - 1 - 2 * step)

    def rows_at(step, offset=0):
        return pl.ds(pl.multiple_of(offset + chunk_at(step) * CHUNK, 8), CHUNK)

    span = H // SEGMENTS
    per = steps // SEGMENTS

    def segment_start(j):
        return pl.multiple_of((j + flip * (SEGMENTS - 1 - 2 * j)) * span, 8)

    def half_start(h):
        return pl.multiple_of((h + flip * (1 - 2 * h)) * half, 8)

    def inside(dr, dc, dz):
        ok = None
        for at, step, count in ((r, dr, nr), (c, dc, nc), (z, dz, nz)):
            if step != 0:
                test = (at + step >= 0) & (at + step < count)
                ok = test if ok is None else ok & test
        return ok

    halves = [pl.ds(half_start(h), half) for h in range(2)]
    loads = [
        pltpu.make_async_copy(src, dst, in_sems.at[i])
        for i, (src, dst) in enumerate(
            [
                (
                    fore_hbm.at[:, halves[h], :],
                    field0.at[1 : F + 1, pl.ds(pl.multiple_of(half_start(h) + 8, 8), half), :],
                )
                for h in range(2)
            ]
            + [(coeff_hbm, coeff_ref)]
            + [
                (src.at[:, rows, :], dst.at[:, rows, :])
                for rows in halves
                for src, dst in ((video_hbm, video), (mult_hbm, mult), (basis_hbm, basis))
            ]
        )
    ]
    for load in loads[:2]:
        load.start()

    barrier = pltpu.get_barrier_semaphore()
    beside = ((0, 0, 1), (0, 1, 0), (1, 0, 0), (1, 0, -1), (0, 1, -1), (1, -1, 0))
    beside += tuple(tuple(-s for s in step) for step in beside)
    for step in beside:
        @pl.when(inside(*step))
        def _(step=step):
            pl.semaphore_signal(
                barrier,
                inc=1,
                device_id=(r + step[0], c + step[1], z + step[2]),
                device_id_type=MESH,
            )
    expected = jnp.int32(0)
    for step in beside:
        expected = expected + inside(*step).astype(jnp.int32)
    for load in loads[2:]:
        load.start()

    pl.semaphore_wait(barrier, expected)

    lane_h = lax.broadcasted_iota(jnp.int32, (span, 128), 1)

    def pack_columns(k, j):
        base = segment_start(j)
        tile = jnp.zeros((span, 128), jnp.float32)
        for f in range(F):
            for lane, at in ((f, 0), (8 + f, W - 1)):
                lanes = field[k][f + 1, pl.ds(base + 8, span), (at // 128) * 128 : (at // 128) * 128 + 128]
                tile = jnp.where(lane_h == lane, lanes[:, at % 128 : at % 128 + 1], tile)
        first_cols[pl.ds(base + 8, span), :] = tile
        packed[k, j] = tile.T[:16, :]

    strips = range(4)
    corners = (4, 5)

    def column_list(k, j):
        return (
            (packed.at[k, j, 0:F], arrived.at[k, j, 1 : F + 1], (0, -1, 0)),
            (packed.at[k, j, 8 : 8 + F], arrived.at[k, j, 8 : 8 + F], (0, 1, 0)),
            (packed.at[k, j, F - 1 : F], arrived.at[k, j, 0:1], (0, -1, 1)),
            (packed.at[k, j, 8:9], arrived.at[k, j, 8 + F : 9 + F], (0, 1, -1)),
        )

    def halo_list(k):
        fk = field[k]
        mid = slice(1, F + 1)
        return (
            (fk.at[mid, H : H + 8, :], fk.at[mid, 0:8, :], (1, 0, 0)),
            (fk.at[mid, 8:16, :], fk.at[mid, H + 8 : H + 16, :], (-1, 0, 0)),
            (fk.at[F, 8:9, :], fk.at[0, H + 8 : H + 9, :], (-1, 0, 1)),
            (fk.at[1, H + 7 : H + 8, :], fk.at[F + 1, 7:8, :], (1, 0, -1)),
            (fk.at[mid, H : H + 8, 0:128], corner.at[k, 0], (1, -1, 0)),
            (fk.at[mid, 8:16, W - 128 : W], corner.at[k, 1], (-1, 1, 0)),
        )

    def halo_copy(k, i, leave, src, dst, step):
        return pltpu.make_async_remote_copy(
            src_ref=src, dst_ref=dst,
            send_sem=halo_send.at[k % 2, leave], recv_sem=halo_recv.at[k % 2, i],
            device_id=(r + step[0], c + step[1], z + step[2]), device_id_type=MESH,
        )

    def send_columns(k, j):
        for i, (src, dst, step) in enumerate(column_list(k, j)):
            @pl.when(inside(*step))
            def _(i=i, src=src, dst=dst, step=step):
                halo_copy(k, 6 + 4 * j + i, 6 + i, src, dst, step).start()

    def wait_columns(k, j):
        for i, (src, dst, step) in enumerate(column_list(k, j)):
            @pl.when(inside(*(-s for s in step)))
            def _(i=i, src=src, dst=dst, step=step):
                halo_copy(k, 6 + 4 * j + i, 6 + i, src, dst, step).wait_recv()

    def face(k, step, up):
        fk = field[k]
        rows = rows_at(step, 8)
        at = 6 + 4 * SEGMENTS + 2 * step + (0 if up else 1)
        mine, theirs = (F, 0) if up else (1, F + 1)
        src = fore_hbm.at[mine - 1, rows_at(step)] if k == 0 else fk.at[mine, rows]
        return halo_copy(
            k, at, 10 if up else 11, src, fk.at[theirs, rows], (0, 0, 1 if up else -1)
        )

    def send_faces(k, low, high):
        @pl.loop(low, high)
        def _(step):
            for up in (True, False):
                @pl.when(inside(0, 0, 1 if up else -1))
                def _(up=up):
                    face(k, step, up).start()

    def wait_face(k, step):
        for up in (True, False):
            @pl.when(inside(0, 0, -1 if up else 1))
            def _(up=up):
                face(k, step, up).wait_recv()

    def send_halos(k, which):
        every = halo_list(k)
        for i in which:
            src, dst, step = every[i]

            @pl.when(inside(*step))
            def _(i=i, src=src, dst=dst, step=step):
                halo_copy(k, i, i, src, dst, step).start()

    def wait_halos(k, which):
        every = halo_list(k)
        for i in which:
            src, dst, step = every[i]

            @pl.when(inside(*(-s for s in step)))
            def _(i=i, src=src, dst=dst, step=step):
                halo_copy(k, i, i, src, dst, step).wait_recv()

    def finish_sends(k):
        for i, (src, dst, step) in enumerate(halo_list(k)):
            @pl.when(inside(*step))
            def _(i=i, src=src, dst=dst, step=step):
                halo_copy(k, i, i, src, dst, step).wait_send()

        every = (
            (packed.at[k, :, 0:F], arrived.at[k, :, 1 : F + 1], (0, -1, 0)),
            (packed.at[k, :, 8 : 8 + F], arrived.at[k, :, 8 : 8 + F], (0, 1, 0)),
            (packed.at[k, :, F - 1 : F], arrived.at[k, :, 0:1], (0, -1, 1)),
            (packed.at[k, :, 8:9], arrived.at[k, :, 8 + F : 9 + F], (0, 1, -1)),
            (field[k].at[F, 8 : H + 8, :], field[k].at[0, 8 : H + 8, :], (0, 0, 1)),
            (field[k].at[1, 8 : H + 8, :], field[k].at[F + 1, 8 : H + 8, :], (0, 0, -1)),
        )
        for i, (src, dst, step) in enumerate(every):
            @pl.when(inside(*step))
            def _(i=i, src=src, dst=dst, step=step):
                halo_copy(k, 0, 6 + i, src, dst, step).wait_send()

    def prepare_columns(k, j):
        base = segment_start(j)
        spread = jnp.concatenate(
            [arrived[k, j], jnp.zeros((112, span), jnp.float32)], axis=0
        ).T
        edge_next[pl.ds(base + 8, span), :] = spread
        left_now[pl.ds(base + 8, span), :] = pltpu.roll(spread, 120, 1)
        left_next[pl.ds(base + 8, span), :] = pltpu.roll(spread, 119, 1)
        low, count = pl.multiple_of(base + 8 * flip, 8), span + 8
        here = left_now[pl.ds(low, count), :]
        ahead = left_next[pl.ds(low, count), :]
        lane = lax.broadcasted_iota(jnp.int32, (count, 128), 1)
        row = lax.broadcasted_iota(jnp.int32, (count, 128), 0) + (low - 8)
        slope0 = jnp.where((lane == F - 1) & (z == nz - 1), 0.0, ahead - here)
        after = left_now[pl.ds(low, count + 8), :]
        below = jnp.where(
            row == H - 1, bottom_row[0:1, :], pltpu.roll(after, count + 7, 0)[:count]
        )
        slope1 = jnp.where((row == H - 1) & (r == nr - 1), 0.0, below - here)
        slope2 = first_cols[pl.ds(low, count), :] - here
        weight = lax.rsqrt(smooth_floor + slope0 * slope0 + slope1 * slope1 + slope2 * slope2)
        edge_flux[pl.ds(low, count), :] = jnp.where(c == 0, 0.0, slope2 * weight)

    def take_corners(k):
        wait_halos(k, corners)
        lane8 = lax.broadcasted_iota(jnp.int32, (8, 128), 1)
        top = jnp.zeros((8, 128), jnp.float32)
        bottom = jnp.zeros((8, 128), jnp.float32)
        for f in range(F):
            top = jnp.where(lane8 == f + 1, corner[k, 0, f][:, 0:1], top)
            bottom = jnp.where(lane8 == f, corner[k, 1, f][:, 127:128], bottom)
        edge_next[0:8, :] = top
        bottom_row[...] = bottom

    def sweep(k, last, start):
        R = CHUNK
        tiles = W // 128
        row_8 = lax.broadcasted_iota(jnp.int32, (8, 128), 0) + (r * H + start)
        above_image = row_8 - 8 < 0
        last_image_row = row_8 + (R - 8) >= nr * H - 1
        columns = edge_next[pl.ds(start, R + 8), :]
        fluxes_in = edge_flux[pl.ds(start + 8, R), :]
        at = pl.ds(start, R)

        def frame(f):
            return [
                field[k][f, pl.ds(start, R + 16), w * 128 : w * 128 + 128] for w in range(tiles)
            ]

        now = frame(0)
        flux0_before = None
        for f in range(-1, F):
            after = frame(f + 2)
            skip = 8 if f < 0 else 0
            n = R + 8 - skip
            lane = lax.broadcasted_iota(jnp.int32, (n, 128), 1)
            here = [t[skip : R + 8] for t in now]
            turned = [pltpu.roll(t, 127, 1) for t in here]
            wall = jnp.broadcast_to(columns[skip:, f + 1 : f + 2], (n, 128))
            flux0, flux1, flux2 = [], [], []
            for w in range(tiles):
                slope0 = after[w][skip : R + 8] - here[w]
                if f == F - 1:
                    slope0 = jnp.where(z == nz - 1, 0.0, slope0)
                slope1 = pltpu.roll(now[w][skip:], n + 7, 0)[:n] - here[w]
                slope1 = jnp.concatenate(
                    [slope1[: n - 8], jnp.where(last_image_row, 0.0, slope1[n - 8 :])], axis=0
                )
                beyond = turned[w + 1] if w + 1 < tiles else wall
                slope2 = jnp.where(lane == 127, beyond, turned[w]) - here[w]
                if w + 1 == tiles:
                    slope2 = jnp.where((lane == 127) & (c == nc - 1), 0.0, slope2)
                weight = lax.rsqrt(
                    smooth_floor + slope0 * slope0 + slope1 * slope1 + slope2 * slope2
                )
                flux0.append((slope0 * weight)[8 - skip :])
                if f >= 0:
                    flux = slope1 * weight
                    flux1.append(
                        jnp.concatenate(
                            [jnp.where(above_image, 0.0, flux[:8]), flux[8:]], axis=0
                        )
                    )
                    flux2.append((slope2 * weight)[8:])
            if f < 0:
                flux0 = [jnp.where(z == 0, 0.0, t) for t in flux0]
            else:
                moved = [pltpu.roll(t, 1, 1) for t in flux2]
                entry = jnp.broadcast_to(fluxes_in[:, f : f + 1], (R, 128))
                lane = lax.broadcasted_iota(jnp.int32, (R, 128), 1)
                for w in range(tiles):
                    left = jnp.where(lane == 0, moved[w - 1] if w > 0 else entry, moved[w])
                    above = pltpu.roll(flux1[w], 1, 0)[8:]
                    spread = (flux0[w] - flux0_before[w]) + (flux1[w][8:] - above) + (flux2[w] - left)
                    lanes = slice(w * 128, w * 128 + 128)
                    value = (1.0 - relax_rate) * here[w][8:] + (
                        target[f, at, lanes] + (relax_rate * smooth_weight) * spread
                    )
                    if last:
                        shrunk = value - jnp.clip(value, -shrink_level, shrink_level)
                        result[f, at, lanes] = shrunk
                        anchor[f, at, lanes] = anchor[f, at, lanes] - shrunk
                    else:
                        field[k + 1][f + 1, pl.ds(start + 8, R), lanes] = value
            flux0_before = flux0
            now = after

    def products(left_of, right_of, lefts, rights, first, count, start, store):
        def body(step, totals):
            rows = pl.ds(pl.multiple_of(first + step * 8, 8), 8)
            a = [left_of[i, rows, :] for i in lefts]
            b = [right_of[j, rows, :] for j in rights]
            out = []
            for x in range(len(lefts)):
                for y in range(len(rights)):
                    prod = a[x] * b[y]
                    total = totals[len(out)]
                    for w in range(W // 128):
                        total = total + prod[:, w * 128 : w * 128 + 128]
                    out.append(total)
            return tuple(out)

        totals = lax.fori_loop(
            0, count // 8, body, tuple(start(i, j) for i in lefts for j in rights), unroll=3 if count % 24 == 0 else 1
        )
        n = 0
        for i in lefts:
            for j in rights:
                store(i, j, totals[n])
                n += 1

    def held(block):
        return (block - z >= 2) | (z - block >= 2)

    def move(block, piece):
        rows = pl.ds(pl.multiple_of(block * own + piece * CHUNK, 8), CHUNK)
        spot = pl.ds(pl.multiple_of(piece * CHUNK, 8), CHUNK)
        return pltpu.make_async_remote_copy(
            src_ref=anchor.at[:, rows, :], dst_ref=owned.at[pl.ds(z * F, F), spot, :],
            send_sem=move_send.at[block], recv_sem=move_recv.at[z, piece],
            device_id=(r, c, block), device_id_type=MESH,
        )

    def take(source, piece):
        rows = pl.ds(pl.multiple_of(z * own + piece * CHUNK, 8), CHUNK)
        spot = pl.ds(pl.multiple_of(piece * CHUNK, 8), CHUNK)
        return pltpu.make_async_remote_copy(
            src_ref=anchor.at[:, rows, :], dst_ref=owned.at[pl.ds(source * F, F), spot, :],
            send_sem=move_send.at[source], recv_sem=move_recv.at[source, piece],
            device_id=(r, c, source), device_id_type=MESH,
        )

    send_faces(0, 0, 1)
    for j in range(SEGMENTS):
        if j % (SEGMENTS // 2) == 0:
            loads[j // (SEGMENTS // 2)].wait()
        pack_columns(0, j)
        send_columns(0, j)
        if j == SEGMENTS // 2:
            send_halos(0, strips)
            send_halos(0, corners)
        send_faces(0, max(1, j * per), (j + 1) * per)

    zero_tile = jnp.zeros((8, 128), jnp.float32)

    def store_gram(i, j, value):
        row = jnp.sum(value, axis=0, keepdims=True)
        sums[j, i : i + 1, :] = row
        if i // 4 != j // 4:
            sums[i, j : j + 1, :] = row

    lane_r = lax.broadcasted_iota(jnp.int32, (rank, 128), 1)
    row_r = lax.broadcasted_iota(jnp.int32, (rank, 128), 0)

    def gram_share():
        for i in range(0, rank, 4):
            for j in range(i, rank, 4):
                products(
                    basis, basis, range(i, i + 4), range(j, j + 4), z * own, own,
                    lambda i, j: zero_tile, store_gram,
                )
        tile = jnp.zeros((rank, 128), jnp.float32)
        for q in range(rank):
            tile = jnp.where(lane_r == q, jnp.sum(sums[q], axis=1, keepdims=True), tile)
        grams[z] = tile

    def all_sent(block, sem):
        return pltpu.make_async_remote_copy(
            src_ref=block, dst_ref=block, send_sem=sem.at[0], recv_sem=sem.at[0],
            device_id=(r, c, lax.rem(z + 1, nz)), device_id_type=MESH,
        )

    def share_gram(d):
        return pltpu.make_async_remote_copy(
            src_ref=grams.at[z], dst_ref=grams.at[z],
            send_sem=gram_send.at[0], recv_sem=gram_recv.at[d],
            device_id=(r, c, lax.rem(z + d, nz)), device_id_type=MESH,
        )

    def take_gram(d):
        source = lax.rem(z - d + nz, nz)
        return pltpu.make_async_remote_copy(
            src_ref=grams.at[z], dst_ref=grams.at[source],
            send_sem=gram_send.at[0], recv_sem=gram_recv.at[d],
            device_id=(r, c, source), device_id_type=MESH,
        )

    def store_cross(i, j, value):
        cross[j, i] = value

    def find_target(h):
        for load in loads[3 + 3 * h : 6 + 3 * h]:
            load.wait()

        @pl.loop(0, half // 8)
        def _(step):
            rows = pl.ds(pl.multiple_of(half_start(h) + step * 8, 8), 8)
            totals = [None] * F
            for q in range(rank):
                plane = basis[q, rows, :]
                for f in range(F):
                    term = coeff_ref[f, q] * plane
                    totals[f] = term if totals[f] is None else totals[f] + term
            for f in range(F):
                lifted = dual_scale * mult[f, rows, :]
                anchor[f, rows, :] = video[f, rows, :] + lifted
                target[f, rows, :] = relax_rate * (video[f, rows, :] - totals[f] + lifted)

    loads[2].wait()
    find_target(0)
    find_target(1)
    gram_share()

    def advance(k, step):
        start = pl.multiple_of(chunk_at(step) * CHUNK, 8)
        sweep(k, k == PASSES - 1, start)
        if k == PASSES - 1:
            place, piece = chunk_at(step) // pieces, lax.rem(chunk_at(step), pieces)

            @pl.when((place - z == 1) | (z - place == 1))
            def _():
                move(place, piece).start()

            for i in range(0, rank, 4):
                products(
                    basis, anchor, range(i, i + 4), range(F), start, CHUNK,
                    lambda i, j: cross[j, i], store_cross,
                )

    cross[...] = jnp.zeros_like(cross)
    bottom_row[...] = jnp.zeros_like(bottom_row)
    for k in range(PASSES):
        last = k == PASSES - 1
        if k > 0 and not last:
            finish_sends(k - 1)
        wait_columns(k, 0)
        prepare_columns(k, 0)
        wait_face(k, 0)

        @pl.loop(0, SEGMENTS)
        def _(j, k=k, last=last):
            @pl.loop(j * per, (j + 1) * per - 1)
            def _(step):
                wait_face(k, step + 1)
                advance(k, step)

            final = j == SEGMENTS - 1

            @pl.when(j == SEGMENTS - 2)
            def _():
                take_corners(k)

            @pl.when(~final)
            def _():
                wait_columns(k, j + 1)
                prepare_columns(k, j + 1)
                wait_face(k, (j + 1) * per)

            @pl.when(final)
            def _():
                wait_halos(k, strips)

            advance(k, (j + 1) * per - 1)
            if not last:
                @pl.when(final)
                def _():
                    send_halos(k + 1, strips)
                    send_halos(k + 1, corners)

                pack_columns(k + 1, j)
                send_columns(k + 1, j)
                send_faces(k + 1, j * per, (j + 1) * per)

        if k == PASSES - 2:
            for d in range(1, nz):
                share_gram(d).start()

    inner = (z > 0) & (z < nz - 1)

    def send_held(turn, low, high):
        for b in range(nz):
            @pl.when(held(b) & turn)
            def _(b=b):
                for p in range(low, high):
                    move(b, p).start()

    for far, near in ((nz - 1, 0), (0, nz - 1)):
        place = far - 1 if far > near else far + 1

        @pl.when((z == near) & held(jnp.int32(place)))
        def _(place=place):
            move(place, 0).start()

    for j in range(F):
        for i in range(rank):
            sums[rank + j, i : i + 1, :] = jnp.sum(cross[j, i], axis=0, keepdims=True)

    part = jnp.zeros((rank, 128), jnp.float32)
    for q in range(rank, rank + F):
        part = jnp.where(lane_r == q, jnp.sum(sums[q], axis=1, keepdims=True), part)
    for d in range(1, nz):
        take_gram(d).wait_recv()
    for i in range(nz):
        part = part + grams[i]
    group = nr * nc
    me = r * nc + c
    parts[me] = part

    def share_part(d):
        other = lax.rem(me + d, group)
        return pltpu.make_async_remote_copy(
            src_ref=parts.at[me], dst_ref=parts.at[me],
            send_sem=part_send.at[0], recv_sem=part_recv.at[d],
            device_id=(other // nc, lax.rem(other, nc), z), device_id_type=MESH,
        )

    def take_part(d):
        other = lax.rem(me - d + group, group)
        return pltpu.make_async_remote_copy(
            src_ref=parts.at[me], dst_ref=parts.at[other],
            send_sem=part_send.at[0], recv_sem=part_recv.at[d],
            device_id=(other // nc, lax.rem(other, nc), z), device_id_type=MESH,
        )

    for d in range(1, group):
        share_part(d).start()
    pixel_ridge = ridge_share * H * W * group
    diagonal = lane_r == row_r
    before = jnp.zeros((rank, 128), jnp.float32)
    for q in range(rank):
        for f in range(F):
            before = jnp.where((row_r == q) & (lane_r == rank + f), coeff_ref[f, q], before)
    for d in range(1, group):
        take_part(d).wait_recv()
    total = parts[0]
    for i in range(1, group):
        total = total + parts[i]
    total = total + pixel_ridge * (jnp.where(diagonal, 1.0, 0.0) + before)
    solved = eliminate(total, rank)
    shares[z] = solved

    def share_rows(d):
        return pltpu.make_async_remote_copy(
            src_ref=shares.at[z], dst_ref=shares.at[z],
            send_sem=share_send.at[0], recv_sem=share_recv.at[d],
            device_id=(r, c, lax.rem(z + d, nz)), device_id_type=MESH,
        )

    def take_rows(d):
        source = lax.rem(z - d + nz, nz)
        return pltpu.make_async_remote_copy(
            src_ref=shares.at[z], dst_ref=shares.at[source],
            send_sem=share_send.at[0], recv_sem=share_recv.at[d],
            device_id=(r, c, source), device_id_type=MESH,
        )

    for d in range(1, nz):
        share_rows(d).start()

    send_held(inner, 0, pieces)
    square[...] = jnp.zeros_like(square)
    square[0:rank, :] = solved
    coeff_out[...] = square[...].T[rank : rank + F, 0:rank]
    for d in range(1, nz):
        take_rows(d).wait_recv()
    for b in range(nz):
        @pl.when(held(b) & ~inner)
        def _(b=b):
            first = jnp.where(((z == 0) & (b == nz - 2)) | ((z == nz - 1) & (b == 1)), 1, 0)

            @pl.loop(first, pieces)
            def _(p):
                move(b, p).start()

    frames = F * nz
    wide = jnp.zeros((rank, 128), jnp.float32)
    for i in range(nz):
        placed = shares[i] if i == 0 else pltpu.roll(shares[i], i * F, 1)
        wide = jnp.where(
            (lane_r >= rank + i * F) & (lane_r < rank + (i + 1) * F), placed, wide
        )
    square[0:rank, :] = wide
    gram = lax.dot_general(
        wide, square[...], (((1,), (1,)), ((), ())),
        precision=lax.Precision.HIGHEST, preferred_element_type=jnp.float32,
    )
    frame_ridge = ridge_share * frames
    system = jnp.where(diagonal, gram + frame_ridge, gram) + wide
    system = system + jnp.where(lane_r == row_r + rank + frames, frame_ridge, 0.0)
    table[...] = eliminate(system, rank)
    to_scalar = pltpu.make_async_copy(table, table_smem, small_sem.at[0])
    to_scalar.start()
    to_scalar.wait()
    my_base = z * own

    @pl.loop(0, own // 8)
    def _(step):
        rows = pl.ds(pl.multiple_of(step * 8, 8), 8)
        old = pl.ds(pl.multiple_of(my_base + step * 8, 8), 8)
        for half in range(0, rank, 8):
            totals = [None] * 8
            for f in range(F + rank):
                plane = anchor[f, old, :] if f < F else basis[f - F, old, :]
                place = rank + z * F + f if f < F else rank + frames + f - F
                for q in range(8):
                    term = table_smem[half + q, place] * plane
                    totals[q] = term if totals[q] is None else totals[q] + term
            for q in range(8):
                fresh[half + q, rows, :] = totals[q]

    for k in range(PASSES - 2, PASSES):
        finish_sends(k)
    for src, sem in ((shares, share_send), (grams, gram_send)):
        all_sent(src.at[0 : nz - 1], sem).wait_send()
    all_sent(parts.at[0 : group - 1], part_send).wait_send()

    for n in range(nz - 1):
        near = n + (n >= z).astype(jnp.int32)
        far = nz - 1 - (n + (n >= nz - 1 - z).astype(jnp.int32))
        distance = 1 if n == 0 else nz - n
        source = jnp.where(2 * z < nz, near, far)
        source = jnp.where(z == 0, distance, jnp.where(z == nz - 1, nz - 1 - distance, source))

        @pl.loop(0, pieces)
        def _(piece, source=source):
            take(source, piece).wait_recv()
            for step in range(CHUNK // 8):
                rows = pl.ds(pl.multiple_of(piece * CHUNK + step * 8, 8), 8)
                planes = [owned[source * F + f, rows, :] for f in range(F)]
                for q in range(rank):
                    value = fresh[q, rows, :]
                    for f in range(F):
                        value = value + table_smem[q, rank + source * F + f] * planes[f]
                    fresh[q, rows, :] = value

    for b in range(nz):
        @pl.when(z != b)
        def _(b=b):
            rows = pl.ds(b * own, own)
            pltpu.make_async_remote_copy(
                src_ref=anchor.at[:, rows, :], dst_ref=owned.at[pl.ds(z * F, F)],
                send_sem=move_send.at[b], recv_sem=move_recv.at[z, 0],
                device_id=(r, c, b), device_id_type=MESH,
            ).wait_send()


def deliver(shrunk, coeff, fresh, shrunk_hbm, coeff_hbm, fresh_hbm, sems):
    copies = [pltpu.make_async_copy(coeff, coeff_hbm, sems.at[0])]
    for source, place in ((fresh, fresh_hbm), (shrunk, shrunk_hbm)):
        share = source.shape[0] // 4
        for i in range(4):
            part = pl.ds(i * share, share)
            copies.append(
                pltpu.make_async_copy(source.at[part], place.at[part], sems.at[len(copies)])
            )
    for copy in copies:
        copy.start()
    for copy in copies:
        copy.wait()


def whole_kernel(video, multiplier, foreground, basis, coefficients):
    F, H, W = video.shape
    rank = basis.shape[0]
    nr, nc, nz = (lax.axis_size(name) for name in ("row", "col", "frame"))
    f32 = jnp.float32
    own = H // nz
    group = nr * nc
    vmem = pltpu.VMEM
    dma = pltpu.SemaphoreType.DMA
    pieces = own // CHUNK
    hbm = pl.BlockSpec(memory_space=pl.ANY)
    on_chip = pl.BlockSpec(memory_space=pltpu.VMEM)
    found = pl.pallas_call(
        functools.partial(kernel, (F, H, W, rank, nr, nc, nz)),
        out_shape=(vmem((F, H, W), f32), vmem((F, rank), f32), vmem((rank, own, W), f32)),
        in_specs=[hbm] * 5,
        out_specs=[on_chip] * 3,
        scratch_shapes=[vmem((F + 2, H + 16, W), f32)] * PASSES
        + [
            vmem((F, H, W), f32),
            vmem((F, H, W), f32),
            vmem((rank, H, W), f32),
            vmem((F, H, W), f32),
            vmem((F, H, W), f32),
            vmem((F * nz, own, W), f32),
            vmem((PASSES, SEGMENTS, 16, H // SEGMENTS), f32),
            vmem((PASSES, SEGMENTS, 16, H // SEGMENTS), f32),
            vmem((PASSES, 2, F, 8, 128), f32),
            vmem((H + 8, 128), f32),
            vmem((H + 16, 128), f32),
            vmem((H + 16, 128), f32),
            vmem((H + 24, 128), f32),
            vmem((H + 24, 128), f32),
            vmem((8, 128), f32),
            vmem((F, rank, 8, 128), f32),
            vmem((rank + F, rank, 128), f32),
            vmem((nz, rank, 128), f32),
            vmem((group, rank, 128), f32),
            vmem((nz, rank, 128), f32),
            vmem((128, 128), f32),
            vmem((rank, 128), f32),
            pltpu.SMEM((F, rank), f32),
            pltpu.SMEM((rank, 128), f32),
            dma((9,)),
            dma((2, 12)),
            dma((2, 6 + 4 * SEGMENTS + 2 * (H // CHUNK))),
            dma((1,)),
            dma((group,)),
            dma((1,)),
            dma((nz,)),
            dma((1,)),
            dma((nz,)),
            dma((nz,)),
            dma((nz, pieces)),
            dma((1,)),
        ],
        compiler_params=pltpu.CompilerParams(
            collective_id=0, has_side_effects=True, vmem_limit_bytes=32 * 1024 * 1024
        ),
    )(
        *(
            pltpu.with_memory_space_constraint(x, pltpu.HBM)
            for x in (coefficients, video, multiplier, foreground, basis)
        )
    )
    return pl.pallas_call(
        deliver,
        out_shape=(
            jax.ShapeDtypeStruct((F, H, W), f32),
            jax.ShapeDtypeStruct((F, rank), f32),
            jax.ShapeDtypeStruct((rank, own, W), f32),
        ),
        in_specs=[on_chip] * 3,
        out_specs=[hbm] * 3,
        scratch_shapes=[dma((9,))],
    )(*(pltpu.with_memory_space_constraint(x, pltpu.VMEM) for x in found))


def body(video, multiplier, foreground, basis, coefficients):
    F, H, W = video.shape
    rank = basis.shape[0]
    nz = lax.axis_size("frame")
    fits = (
        H % nz == 0 and (H // nz) % 8 == 0 and (H // nz) % CHUNK == 0 and W % 128 == 0
        and H % 16 == 0 and H % (SEGMENTS * CHUNK) == 0 and lax.axis_size("row") <= 2
        and F % 4 == 0 and F < 8 and rank % 8 == 0 and 2 * rank + F * nz <= 128
    )
    run = whole_kernel if fits else local
    return run(video, multiplier, foreground, basis, coefficients)


def solution(mesh):
    placed = (
        P("frame", "row", "col"),
        P("frame", "row", "col"),
        P("frame", "row", "col"),
        P(None, "row", "col"),
        P("frame", None),
    )
    return jax.shard_map(
        body,
        mesh=mesh,
        in_specs=placed,
        out_specs=(P("frame", "row", "col"), P("frame", None), P(None, ("row", "frame"), "col")),
        check_vma=False,
    )
```

```python
import functools

import jax
import jax.numpy as jnp
from jax import lax
from jax.experimental import pallas as pl
from jax.experimental.pallas import tpu as pltpu
from jax.sharding import PartitionSpec as P

PASSES = 3


relax_rate = 0.8
smooth_weight = 0.5
smooth_floor = 0.25
shrink_level = 0.4
dual_scale = 0.8
ridge_share = 0.1


def with_halo(block, sides, width):
    for axis, dim in sides:
        count = lax.axis_size(axis)
        forward = [(i, i + 1) for i in range(count - 1)]
        backward = [(target, source) for source, target in forward]
        low = lax.ppermute(
            lax.slice_in_dim(block, block.shape[dim] - width, None, axis=dim), axis, forward
        )
        high = lax.ppermute(lax.slice_in_dim(block, 0, width, axis=dim), axis, backward)
        block = jnp.concatenate([low, block, high], axis=dim)
    return block


def forward_cells(padded, direction, shape):
    starts = [0, 0, 0]
    starts[direction] = 1
    limits = [starts[axis_dim] + shape[axis_dim] for axis_dim in range(3)]
    return lax.slice(padded, starts, limits)


def descend(padded, source, anchor, extent):
    shape = tuple((int(length) - 1 for length in padded.shape))
    here_cells = padded[:-1, :-1, :-1]
    slopes = []
    for direction in range(3):
        ahead_cells = forward_cells(padded, direction, shape)
        places = anchor[direction] + jnp.arange(shape[direction], dtype=jnp.int32)
        inside = (places >= 0) & (places < extent[direction] - 1)
        layout = [1, 1, 1]
        layout[direction] = shape[direction]
        inside = inside.reshape(layout)
        slopes.append(jnp.where(inside, ahead_cells - here_cells, jnp.zeros_like(here_cells)))
    weight = lax.rsqrt(
        smooth_floor + slopes[0] * slopes[0] + slopes[1] * slopes[1] + slopes[2] * slopes[2]
    )
    fluxes = [slope_part * weight for slope_part in slopes]
    spread = (
        fluxes[0][1:, 1:, 1:]
        - fluxes[0][:-1, 1:, 1:]
        + (fluxes[1][1:, 1:, 1:] - fluxes[1][1:, :-1, 1:])
        + (fluxes[2][1:, 1:, 1:] - fluxes[2][1:, 1:, :-1])
    )
    center = padded[1:-1, 1:-1, 1:-1]
    return center + relax_rate * (source - center + smooth_weight * spread)


def solve_definite(matrix, right_side):
    factor_lower = jnp.linalg.cholesky(matrix)
    half_solved = lax.linalg.triangular_solve(factor_lower, right_side, left_side=True, lower=True)
    return lax.linalg.triangular_solve(
        factor_lower, half_solved, left_side=True, lower=True, transpose_a=True
    )


def local(video, multiplier, foreground, basis, coefficients):
    highest = lax.Precision.HIGHEST
    frames_here, rows_here, cols_here = video.shape
    rank_size = basis.shape[0]
    frame_count = lax.axis_size("frame")
    row_count = lax.axis_size("row")
    col_count = lax.axis_size("col")
    extent = (frames_here * frame_count, rows_here * row_count, cols_here * col_count)
    frame_slot = lax.axis_index("frame")
    corner = (
        frame_slot * frames_here,
        lax.axis_index("row") * rows_here,
        lax.axis_index("col") * cols_here,
    )
    pixels = rows_here * cols_here
    flat_basis = basis.reshape(rank_size, pixels)
    background = jnp.dot(coefficients, flat_basis, precision=highest).reshape(video.shape)
    target = video - background + dual_scale * multiplier
    current = foreground
    for sweep in range(PASSES):
        padded = with_halo(current, (("row", 1), ("col", 2), ("frame", 0)), 1)
        current = descend(padded, target, tuple((start_cell - 1 for start_cell in corner)), extent)
    shrunk = current - jnp.clip(current, -shrink_level, shrink_level)
    residual_target = video + dual_scale * multiplier - shrunk
    flat_target = residual_target.reshape(frames_here, pixels)
    gram_part = jnp.dot(flat_basis, flat_basis.T, precision=highest)
    cross_part = jnp.dot(flat_basis, flat_target.T, precision=highest)
    gram_sum, cross_sum = lax.psum((gram_part, cross_part), ("row", "col"))
    identity_matrix = jnp.eye(rank_size, dtype=gram_sum.dtype)
    pixel_ridge = ridge_share * pixels * row_count * col_count
    coeff_rows = solve_definite(
        gram_sum + pixel_ridge * identity_matrix, cross_sum + pixel_ridge * coefficients.T
    )
    total_part = jnp.dot(coeff_rows, flat_target, precision=highest).reshape(
        rank_size, rows_here, cols_here
    )
    frame_gram_part = jnp.dot(coeff_rows, coeff_rows.T, precision=highest)
    owned_rows = rows_here // frame_count
    owned_sums = lax.psum_scatter(total_part, "frame", scatter_dimension=1, tiled=True)
    frame_gram = lax.psum(frame_gram_part, "frame")
    old_owned = lax.dynamic_slice_in_dim(basis, frame_slot * owned_rows, owned_rows, 1)
    frame_ridge = ridge_share * frames_here * frame_count
    right_side = (owned_sums + frame_ridge * old_owned).reshape(rank_size, owned_rows * cols_here)
    new_basis = solve_definite(frame_gram + frame_ridge * identity_matrix, right_side)
    return (shrunk, coeff_rows.T, new_basis.reshape(rank_size, owned_rows, cols_here))


MESH = pl.DeviceIdType.MESH
CHUNK = 24
SEGMENTS = 4


def eliminate(matrix, size):
    lanes = lax.broadcasted_iota(jnp.int32, matrix.shape, 1)
    rows = lax.broadcasted_iota(jnp.int32, matrix.shape, 0)
    for k in range(size):
        pivot = matrix[k : k + 1, k : k + 1]
        scaled = matrix[k : k + 1, :] / pivot
        column = jnp.sum(jnp.where(lanes == k, matrix, 0.0), axis=1, keepdims=True)
        matrix = jnp.where(rows == k, scaled, matrix - column * scaled)
    return matrix


def kernel(
    sizes, coeff_hbm, video_hbm, mult_hbm, fore_hbm, basis_hbm,
    result, coeff_out, fresh,
    field0, field1, field2, video, mult, basis, anchor, target, owned,
    packed, arrived, corner, edge_next, edge_flux, first_cols, left_now, left_next, bottom_row,
    cross, sums, grams, gram_parts, inverse, parts, shares, square, table, coeff_ref, table_smem,
    in_sems, halo_send, halo_recv, part_send, part_recv,
    gram_send, gram_recv, total_send, total_recv, share_send, share_recv, move_send, move_recv, small_sem,
):
    field = (field0, field1, field2)
    F, H, W, rank, nr, nc, nz = sizes
    r = lax.axis_index("row")
    c = lax.axis_index("col")
    z = lax.axis_index("frame")
    own = H // nz
    pieces = own // CHUNK
    half = H // 2
    flip = lax.rem(r, 2)

    steps = H // CHUNK

    def chunk_at(step):
        return step + flip * (steps - 1 - 2 * step)

    def rows_at(step, offset=0):
        return pl.ds(pl.multiple_of(offset + chunk_at(step) * CHUNK, 8), CHUNK)

    span = H // SEGMENTS
    per = steps // SEGMENTS

    def segment_start(j):
        return pl.multiple_of((j + flip * (SEGMENTS - 1 - 2 * j)) * span, 8)

    def half_start(h):
        return pl.multiple_of((h + flip * (1 - 2 * h)) * half, 8)

    inner = (z > 0) & (z < nz - 1)

    def inside(dr, dc, dz):
        ok = None
        for at, step, count in ((r, dr, nr), (c, dc, nc), (z, dz, nz)):
            if step != 0:
                test = (at + step >= 0) & (at + step < count)
                ok = test if ok is None else ok & test
        return ok

    halves = [pl.ds(half_start(h), half) for h in range(2)]
    loads = [
        pltpu.make_async_copy(src, dst, in_sems.at[i])
        for i, (src, dst) in enumerate(
            [
                (
                    fore_hbm.at[:, halves[h], :],
                    field0.at[1 : F + 1, pl.ds(pl.multiple_of(half_start(h) + 8, 8), half), :],
                )
                for h in range(2)
            ]
            + [(coeff_hbm, coeff_ref)]
            + [
                (src.at[:, rows, :], dst.at[:, rows, :])
                for rows in halves
                for src, dst in ((video_hbm, video), (mult_hbm, mult), (basis_hbm, basis))
            ]
        )
    ]
    for load in loads[:2]:
        load.start()

    barrier = pltpu.get_barrier_semaphore()
    beside = ((0, 0, 1), (0, 1, 0), (1, 0, 0), (1, 0, -1), (0, 1, -1), (1, -1, 0))
    beside += tuple(tuple(-s for s in step) for step in beside)
    for step in beside:
        @pl.when(inside(*step))
        def _(step=step):
            pl.semaphore_signal(
                barrier,
                inc=1,
                device_id=(r + step[0], c + step[1], z + step[2]),
                device_id_type=MESH,
            )
    expected = jnp.int32(0)
    for step in beside:
        expected = expected + inside(*step).astype(jnp.int32)
    for load in loads[2:]:
        load.start()

    pl.semaphore_wait(barrier, expected)

    lane_h = lax.broadcasted_iota(jnp.int32, (span, 128), 1)

    def pack_columns(k, j):
        base = segment_start(j)
        tile = jnp.zeros((span, 128), jnp.float32)
        for f in range(F):
            for lane, at in ((f, 0), (8 + f, W - 1)):
                lanes = field[k][f + 1, pl.ds(base + 8, span), (at // 128) * 128 : (at // 128) * 128 + 128]
                tile = jnp.where(lane_h == lane, lanes[:, at % 128 : at % 128 + 1], tile)
        first_cols[pl.ds(base + 8, span), :] = tile
        packed[k, j] = tile.T[:16, :]

    strips = range(4)
    corners = (4, 5)

    def column_list(k, j):
        return (
            (packed.at[k, j, 0:F], arrived.at[k, j, 1 : F + 1], (0, -1, 0)),
            (packed.at[k, j, 8 : 8 + F], arrived.at[k, j, 8 : 8 + F], (0, 1, 0)),
            (packed.at[k, j, F - 1 : F], arrived.at[k, j, 0:1], (0, -1, 1)),
            (packed.at[k, j, 8:9], arrived.at[k, j, 8 + F : 9 + F], (0, 1, -1)),
        )

    def halo_list(k):
        fk = field[k]
        mid = slice(1, F + 1)
        return (
            (fk.at[mid, H : H + 8, :], fk.at[mid, 0:8, :], (1, 0, 0)),
            (fk.at[mid, 8:16, :], fk.at[mid, H + 8 : H + 16, :], (-1, 0, 0)),
            (fk.at[F, 8:9, :], fk.at[0, H + 8 : H + 9, :], (-1, 0, 1)),
            (fk.at[1, H + 7 : H + 8, :], fk.at[F + 1, 7:8, :], (1, 0, -1)),
            (fk.at[mid, H : H + 8, 0:128], corner.at[k, 0], (1, -1, 0)),
            (fk.at[mid, 8:16, W - 128 : W], corner.at[k, 1], (-1, 1, 0)),
        )

    def halo_copy(k, i, leave, src, dst, step):
        return pltpu.make_async_remote_copy(
            src_ref=src, dst_ref=dst,
            send_sem=halo_send.at[k % 2, leave], recv_sem=halo_recv.at[k % 2, i],
            device_id=(r + step[0], c + step[1], z + step[2]), device_id_type=MESH,
        )

    def send_columns(k, j):
        for i, (src, dst, step) in enumerate(column_list(k, j)):
            @pl.when(inside(*step))
            def _(i=i, src=src, dst=dst, step=step):
                halo_copy(k, 6 + 2 * j + i % 2, 6 + i, src, dst, step).start()

    def wait_columns(k, j):
        for side, step, corner_step, small, large in (
            (0, (0, -1, 0), (0, -1, 1), slice(1, F + 1), slice(0, F + 1)),
            (1, (0, 1, 0), (0, 1, -1), slice(8, 8 + F), slice(8, 9 + F)),
        ):
            near = inside(*(-s for s in step))
            both = inside(*(-s for s in corner_step))
            for turn, rows in ((near & ~both, small), (both, large)):
                @pl.when(turn)
                def _(side=side, step=step, rows=rows):
                    ref = arrived.at[k, j, rows]
                    halo_copy(k, 6 + 2 * j + side, 0, ref, ref, step).wait_recv()

    def face(k, step, up):
        fk = field[k]
        rows = rows_at(step, 8)
        at = 6 + 2 * SEGMENTS + step
        mine, theirs = (F, 0) if up else (1, F + 1)
        src = fore_hbm.at[mine - 1, rows_at(step)] if k == 0 else fk.at[mine, rows]
        return halo_copy(
            k, at, 10 if up else 11, src, fk.at[theirs, rows], (0, 0, 1 if up else -1)
        )

    def send_faces(k, low, high):
        @pl.loop(low, high)
        def _(step):
            for up in (True, False):
                @pl.when(inside(0, 0, 1 if up else -1))
                def _(up=up):
                    face(k, step, up).start()

    def wait_face(k, step):
        for turn, frames in ((inner, slice(0, 2)), (~inner, slice(0, 1))):
            @pl.when(turn)
            def _(frames=frames):
                ref = field[k].at[frames, rows_at(step, 8), :]
                halo_copy(k, 6 + 2 * SEGMENTS + step, 0, ref, ref, (0, 0, 1)).wait_recv()

    def send_halos(k, which):
        every = halo_list(k)
        for i in which:
            src, dst, step = every[i]

            @pl.when(inside(*step))
            def _(i=i, src=src, dst=dst, step=step):
                halo_copy(k, i, i, src, dst, step).start()

    def wait_halos(k, which):
        every = halo_list(k)
        for i in which:
            src, dst, step = every[i]

            @pl.when(inside(*(-s for s in step)))
            def _(i=i, src=src, dst=dst, step=step):
                halo_copy(k, i, i, src, dst, step).wait_recv()

    def finish_sends(k):
        for i, (src, dst, step) in enumerate(halo_list(k)):
            @pl.when(inside(*step))
            def _(i=i, src=src, dst=dst, step=step):
                halo_copy(k, i, i, src, dst, step).wait_send()

        every = (
            (packed.at[k, :, 0:F], arrived.at[k, :, 1 : F + 1], (0, -1, 0)),
            (packed.at[k, :, 8 : 8 + F], arrived.at[k, :, 8 : 8 + F], (0, 1, 0)),
            (packed.at[k, :, F - 1 : F], arrived.at[k, :, 0:1], (0, -1, 1)),
            (packed.at[k, :, 8:9], arrived.at[k, :, 8 + F : 9 + F], (0, 1, -1)),
            (field[k].at[F, 8 : H + 8, :], field[k].at[0, 8 : H + 8, :], (0, 0, 1)),
            (field[k].at[1, 8 : H + 8, :], field[k].at[F + 1, 8 : H + 8, :], (0, 0, -1)),
        )
        for i, (src, dst, step) in enumerate(every):
            @pl.when(inside(*step))
            def _(i=i, src=src, dst=dst, step=step):
                halo_copy(k, 0, 6 + i, src, dst, step).wait_send()

    def prepare_columns(k, j):
        base = segment_start(j)
        spread = jnp.concatenate(
            [arrived[k, j], jnp.zeros((112, span), jnp.float32)], axis=0
        ).T
        edge_next[pl.ds(base + 8, span), :] = spread
        left_now[pl.ds(base + 8, span), :] = pltpu.roll(spread, 120, 1)
        left_next[pl.ds(base + 8, span), :] = pltpu.roll(spread, 119, 1)
        low, count = pl.multiple_of(base + 8 * flip, 8), span + 8
        here = left_now[pl.ds(low, count), :]
        ahead = left_next[pl.ds(low, count), :]
        lane = lax.broadcasted_iota(jnp.int32, (count, 128), 1)
        row = lax.broadcasted_iota(jnp.int32, (count, 128), 0) + (low - 8)
        slope0 = jnp.where((lane == F - 1) & (z == nz - 1), 0.0, ahead - here)
        after = left_now[pl.ds(low, count + 8), :]
        below = jnp.where(
            row == H - 1, bottom_row[0:1, :], pltpu.roll(after, count + 7, 0)[:count]
        )
        slope1 = jnp.where((row == H - 1) & (r == nr - 1), 0.0, below - here)
        slope2 = first_cols[pl.ds(low, count), :] - here
        weight = lax.rsqrt(smooth_floor + slope0 * slope0 + slope1 * slope1 + slope2 * slope2)
        edge_flux[pl.ds(low, count), :] = jnp.where(c == 0, 0.0, slope2 * weight)

    def take_corners(k):
        wait_halos(k, corners)
        lane8 = lax.broadcasted_iota(jnp.int32, (8, 128), 1)
        top = jnp.zeros((8, 128), jnp.float32)
        bottom = jnp.zeros((8, 128), jnp.float32)
        for f in range(F):
            top = jnp.where(lane8 == f + 1, corner[k, 0, f][:, 0:1], top)
            bottom = jnp.where(lane8 == f, corner[k, 1, f][:, 127:128], bottom)
        edge_next[0:8, :] = top
        bottom_row[...] = bottom

    def sweep(k, last, start):
        R = CHUNK
        tiles = W // 128
        row_8 = lax.broadcasted_iota(jnp.int32, (8, 128), 0) + (r * H + start)
        above_image = row_8 - 8 < 0
        last_image_row = row_8 + (R - 8) >= nr * H - 1
        columns = edge_next[pl.ds(start, R + 8), :]
        fluxes_in = edge_flux[pl.ds(start + 8, R), :]
        at = pl.ds(start, R)

        def frame(f):
            return [
                field[k][f, pl.ds(start, R + 16), w * 128 : w * 128 + 128] for w in range(tiles)
            ]

        now = frame(0)
        flux0_before = None
        for f in range(-1, F):
            after = frame(f + 2)
            skip = 8 if f < 0 else 0
            n = R + 8 - skip
            lane = lax.broadcasted_iota(jnp.int32, (n, 128), 1)
            here = [t[skip : R + 8] for t in now]
            turned = [pltpu.roll(t, 127, 1) for t in here]
            wall = jnp.broadcast_to(columns[skip:, f + 1 : f + 2], (n, 128))
            flux0, flux1, flux2 = [], [], []
            for w in range(tiles):
                slope0 = after[w][skip : R + 8] - here[w]
                if f == F - 1:
                    slope0 = jnp.where(z == nz - 1, 0.0, slope0)
                slope1 = pltpu.roll(now[w][skip:], n + 7, 0)[:n] - here[w]
                slope1 = jnp.concatenate(
                    [slope1[: n - 8], jnp.where(last_image_row, 0.0, slope1[n - 8 :])], axis=0
                )
                beyond = turned[w + 1] if w + 1 < tiles else wall
                slope2 = jnp.where(lane == 127, beyond, turned[w]) - here[w]
                if w + 1 == tiles:
                    slope2 = jnp.where((lane == 127) & (c == nc - 1), 0.0, slope2)
                weight = lax.rsqrt(
                    smooth_floor + slope0 * slope0 + slope1 * slope1 + slope2 * slope2
                )
                flux0.append((slope0 * weight)[8 - skip :])
                if f >= 0:
                    flux = slope1 * weight
                    flux1.append(
                        jnp.concatenate(
                            [jnp.where(above_image, 0.0, flux[:8]), flux[8:]], axis=0
                        )
                    )
                    flux2.append((slope2 * weight)[8:])
            if f < 0:
                flux0 = [jnp.where(z == 0, 0.0, t) for t in flux0]
            else:
                moved = [pltpu.roll(t, 1, 1) for t in flux2]
                entry = jnp.broadcast_to(fluxes_in[:, f : f + 1], (R, 128))
                lane = lax.broadcasted_iota(jnp.int32, (R, 128), 1)
                for w in range(tiles):
                    left = jnp.where(lane == 0, moved[w - 1] if w > 0 else entry, moved[w])
                    above = pltpu.roll(flux1[w], 1, 0)[8:]
                    spread = (flux0[w] - flux0_before[w]) + (flux1[w][8:] - above) + (flux2[w] - left)
                    lanes = slice(w * 128, w * 128 + 128)
                    value = (1.0 - relax_rate) * here[w][8:] + (
                        target[f, at, lanes] + (relax_rate * smooth_weight) * spread
                    )
                    if last:
                        shrunk = value - jnp.clip(value, -shrink_level, shrink_level)
                        result[f, at, lanes] = shrunk
                        anchor[f, at, lanes] = anchor[f, at, lanes] - shrunk
                    else:
                        field[k + 1][f + 1, pl.ds(start + 8, R), lanes] = value
            flux0_before = flux0
            now = after

    def products(left_of, right_of, lefts, rights, first, count, start, store):
        def body(step, totals):
            rows = pl.ds(pl.multiple_of(first + step * 8, 8), 8)
            a = [left_of[i, rows, :] for i in lefts]
            b = [right_of[j, rows, :] for j in rights]
            out = []
            for x in range(len(lefts)):
                for y in range(len(rights)):
                    prod = a[x] * b[y]
                    total = totals[len(out)]
                    for w in range(W // 128):
                        total = total + prod[:, w * 128 : w * 128 + 128]
                    out.append(total)
            return tuple(out)

        totals = lax.fori_loop(
            0, count // 8, body, tuple(start(i, j) for i in lefts for j in rights), unroll=3 if count % 24 == 0 else 1
        )
        n = 0
        for i in lefts:
            for j in rights:
                store(i, j, totals[n])
                n += 1

    def held(block):
        return (block - z >= 2) | (z - block >= 2)

    def move(block, piece):
        rows = pl.ds(pl.multiple_of(block * own + piece * CHUNK, 8), CHUNK)
        spot = pl.ds(pl.multiple_of(piece * CHUNK, 8), CHUNK)
        return pltpu.make_async_remote_copy(
            src_ref=anchor.at[:, rows, :], dst_ref=owned.at[pl.ds(z * F, F), spot, :],
            send_sem=move_send.at[block], recv_sem=move_recv.at[z, piece],
            device_id=(r, c, block), device_id_type=MESH,
        )

    def take(source, piece):
        rows = pl.ds(pl.multiple_of(z * own + piece * CHUNK, 8), CHUNK)
        spot = pl.ds(pl.multiple_of(piece * CHUNK, 8), CHUNK)
        return pltpu.make_async_remote_copy(
            src_ref=anchor.at[:, rows, :], dst_ref=owned.at[pl.ds(source * F, F), spot, :],
            send_sem=move_send.at[source], recv_sem=move_recv.at[source, piece],
            device_id=(r, c, source), device_id_type=MESH,
        )

    send_faces(0, 0, 1)
    for j in range(SEGMENTS):
        if j % (SEGMENTS // 2) == 0:
            loads[j // (SEGMENTS // 2)].wait()
        pack_columns(0, j)
        send_columns(0, j)
        if j == SEGMENTS // 2:
            send_halos(0, strips)
            send_halos(0, corners)
        send_faces(0, max(1, j * per), (j + 1) * per)

    zero_tile = jnp.zeros((8, 128), jnp.float32)

    def store_gram(i, j, value):
        row = jnp.sum(value, axis=0, keepdims=True)
        sums[j, i : i + 1, :] = row
        if i // 4 != j // 4:
            sums[i, j : j + 1, :] = row

    lane_r = lax.broadcasted_iota(jnp.int32, (rank, 128), 1)
    row_r = lax.broadcasted_iota(jnp.int32, (rank, 128), 0)

    def gram_share():
        for i in range(0, rank, 4):
            for j in range(i, rank, 4):
                products(
                    basis, basis, range(i, i + 4), range(j, j + 4), z * own, own,
                    lambda i, j: zero_tile, store_gram,
                )
        tile = jnp.zeros((rank, 128), jnp.float32)
        for q in range(rank):
            tile = jnp.where(lane_r == q, jnp.sum(sums[q], axis=1, keepdims=True), tile)
        lane = lax.broadcasted_iota(jnp.int32, (8, 128), 1)
        tile = jnp.where(lane < rank, tile[:8], pltpu.roll(tile[8:], rank, 1))
        tile = jnp.where(lane < 2 * rank, tile, pltpu.roll(pltpu.roll(tile, 4, 0), 2 * rank, 1))
        tile = jnp.where(lane < 4 * rank, tile, pltpu.roll(pltpu.roll(tile, 6, 0), 4 * rank, 1))
        grams[z] = tile

    def unfold(tile):
        row = lax.broadcasted_iota(jnp.int32, (8, 128), 0)
        tile = jnp.where(row < 2, tile, pltpu.roll(pltpu.roll(tile, 2, 0), 128 - 4 * rank, 1))
        tile = jnp.where(row < 4, tile, pltpu.roll(pltpu.roll(tile, 4, 0), 128 - 2 * rank, 1))
        tile = jnp.concatenate([tile, pltpu.roll(tile, 128 - rank, 1)], axis=0)
        return jnp.where(lane_r < rank, tile, 0.0)

    def all_sent(block, sem):
        return pltpu.make_async_remote_copy(
            src_ref=block, dst_ref=block, send_sem=sem.at[0], recv_sem=sem.at[0],
            device_id=(r, c, lax.rem(z + 1, nz)), device_id_type=MESH,
        )

    def share_gram(d):
        return pltpu.make_async_remote_copy(
            src_ref=grams.at[z, 0:2], dst_ref=grams.at[z, 0:2],
            send_sem=gram_send.at[0], recv_sem=gram_recv.at[d],
            device_id=(r, c, lax.rem(z + d, nz)), device_id_type=MESH,
        )

    def take_gram(d):
        source = lax.rem(z - d + nz, nz)
        return pltpu.make_async_remote_copy(
            src_ref=grams.at[z, 0:2], dst_ref=grams.at[source, 0:2],
            send_sem=gram_send.at[0], recv_sem=gram_recv.at[d],
            device_id=(r, c, source), device_id_type=MESH,
        )

    group = nr * nc
    me = r * nc + c

    def share_total(d):
        other = lax.rem(me + d, group)
        return pltpu.make_async_remote_copy(
            src_ref=gram_parts.at[me, 0:2], dst_ref=gram_parts.at[me, 0:2],
            send_sem=total_send.at[0], recv_sem=total_recv.at[d],
            device_id=(other // nc, lax.rem(other, nc), z), device_id_type=MESH,
        )

    def take_total(d):
        other = lax.rem(me - d + group, group)
        return pltpu.make_async_remote_copy(
            src_ref=gram_parts.at[me, 0:2], dst_ref=gram_parts.at[other, 0:2],
            send_sem=total_send.at[0], recv_sem=total_recv.at[d],
            device_id=(other // nc, lax.rem(other, nc), z), device_id_type=MESH,
        )

    def store_cross(i, j, value):
        cross[j, i] = value

    def find_target(h):
        for load in loads[3 + 3 * h : 6 + 3 * h]:
            load.wait()

        @pl.loop(0, half // 8)
        def _(step):
            rows = pl.ds(pl.multiple_of(half_start(h) + step * 8, 8), 8)
            totals = [None] * F
            for q in range(rank):
                plane = basis[q, rows, :]
                for f in range(F):
                    term = coeff_ref[f, q] * plane
                    totals[f] = term if totals[f] is None else totals[f] + term
            for f in range(F):
                lifted = dual_scale * mult[f, rows, :]
                anchor[f, rows, :] = video[f, rows, :] + lifted
                target[f, rows, :] = relax_rate * (video[f, rows, :] - totals[f] + lifted)

    loads[2].wait()
    find_target(0)
    find_target(1)
    gram_share()

    def advance(k, step):
        start = pl.multiple_of(chunk_at(step) * CHUNK, 8)
        sweep(k, k == PASSES - 1, start)
        if k == PASSES - 1:
            place, piece = chunk_at(step) // pieces, lax.rem(chunk_at(step), pieces)

            @pl.when((place - z == 1) | (z - place == 1))
            def _():
                move(place, piece).start()

            for i in range(0, rank, 4):
                products(
                    basis, anchor, range(i, i + 4), range(F), start, CHUNK,
                    lambda i, j: cross[j, i], store_cross,
                )

    cross[...] = jnp.zeros_like(cross)
    bottom_row[...] = jnp.zeros_like(bottom_row)
    for k in range(PASSES):
        last = k == PASSES - 1
        if k > 0 and not last:
            finish_sends(k - 1)
        wait_columns(k, 0)
        prepare_columns(k, 0)
        wait_face(k, 0)

        @pl.loop(0, SEGMENTS)
        def _(j, k=k, last=last):
            @pl.loop(j * per, (j + 1) * per - 1)
            def _(step):
                wait_face(k, step + 1)
                advance(k, step)

            final = j == SEGMENTS - 1
            if k == PASSES - 2:
                @pl.when(j == 2)
                def _():
                    for d in range(1, nz):
                        share_gram(d).start()
            if k == PASSES - 1:
                @pl.when(j == 2)
                def _():
                    for d in range(1, nz):
                        take_gram(d).wait_recv()
                    total = grams[0]
                    for i in range(1, nz):
                        total = total + grams[i]
                    gram_parts[me] = total
                    for d in range(1, group):
                        share_total(d).start()

            @pl.when(j == SEGMENTS - 2)
            def _():
                take_corners(k)

            @pl.when(~final)
            def _():
                wait_columns(k, j + 1)
                prepare_columns(k, j + 1)
                wait_face(k, (j + 1) * per)

            @pl.when(final)
            def _():
                wait_halos(k, strips)

            advance(k, (j + 1) * per - 1)
            if not last:
                @pl.when(final)
                def _():
                    send_halos(k + 1, strips)
                    send_halos(k + 1, corners)

                pack_columns(k + 1, j)
                send_columns(k + 1, j)
                send_faces(k + 1, j * per, (j + 1) * per)


    def send_held(turn, low, high):
        for b in range(nz):
            @pl.when(held(b) & turn)
            def _(b=b):
                for p in range(low, high):
                    move(b, p).start()

    for far, near in ((nz - 1, 0), (0, nz - 1)):
        place = far - 1 if far > near else far + 1

        @pl.when((z == near) & held(jnp.int32(place)))
        def _(place=place):
            move(place, 0).start()

    for j in range(F):
        for i in range(rank):
            sums[rank + j, i : i + 1, :] = jnp.sum(cross[j, i], axis=0, keepdims=True)

    part = jnp.zeros((rank, 128), jnp.float32)
    for q in range(rank, rank + F):
        part = jnp.where(lane_r == q, jnp.sum(sums[q], axis=1, keepdims=True), part)
    parts[me] = part

    def share_part(d):
        other = lax.rem(me + d, group)
        return pltpu.make_async_remote_copy(
            src_ref=parts.at[me], dst_ref=parts.at[me],
            send_sem=part_send.at[0], recv_sem=part_recv.at[d],
            device_id=(other // nc, lax.rem(other, nc), z), device_id_type=MESH,
        )

    def take_part(d):
        other = lax.rem(me - d + group, group)
        return pltpu.make_async_remote_copy(
            src_ref=parts.at[me], dst_ref=parts.at[other],
            send_sem=part_send.at[0], recv_sem=part_recv.at[d],
            device_id=(other // nc, lax.rem(other, nc), z), device_id_type=MESH,
        )

    for d in range(1, group):
        share_part(d).start()
    pixel_ridge = ridge_share * H * W * group
    diagonal = lane_r == row_r
    before = jnp.zeros((rank, 128), jnp.float32)
    for q in range(rank):
        for f in range(F):
            before = jnp.where((row_r == q) & (lane_r == rank + f), coeff_ref[f, q], before)
    for d in range(1, group):
        take_total(d).wait_recv()
    total = gram_parts[0]
    for i in range(1, group):
        total = total + gram_parts[i]
    diagonal = lane_r == row_r
    system = unfold(total) + jnp.where(
        diagonal, pixel_ridge, jnp.where(lane_r == row_r + rank, 1.0, 0.0)
    )
    system = eliminate(system, rank)
    for q in range(rank):
        inverse[q] = jnp.broadcast_to(system[:, rank + q : rank + q + 1], (rank, 128))
    for d in range(1, group):
        take_part(d).wait_recv()
    total = parts[0]
    for i in range(1, group):
        total = total + parts[i]
    total = total + pixel_ridge * before
    solved = inverse[0] * total[0:1, :]
    for q in range(1, rank):
        solved = solved + inverse[q] * total[q : q + 1, :]
    square[...] = jnp.zeros_like(square)
    square[0:rank, :] = solved
    mine = square[...].T[rank : rank + F, :]
    shares[pl.ds(z * F, F), :] = mine

    def share_rows(d):
        return pltpu.make_async_remote_copy(
            src_ref=shares.at[pl.ds(z * F, F)], dst_ref=shares.at[pl.ds(z * F, F)],
            send_sem=share_send.at[0], recv_sem=share_recv.at[d],
            device_id=(r, c, lax.rem(z + d, nz)), device_id_type=MESH,
        )

    def take_rows(d):
        source = lax.rem(z - d + nz, nz)
        return pltpu.make_async_remote_copy(
            src_ref=shares.at[pl.ds(z * F, F)], dst_ref=shares.at[pl.ds(source * F, F)],
            send_sem=share_send.at[0], recv_sem=share_recv.at[d],
            device_id=(r, c, source), device_id_type=MESH,
        )

    for d in range(1, nz):
        share_rows(d).start()

    send_held(inner, 0, pieces)
    coeff_out[...] = mine[:, 0:rank]
    for d in range(1, nz):
        take_rows(d).wait_recv()
    for b in range(nz):
        @pl.when(held(b) & ~inner)
        def _(b=b):
            first = jnp.where(((z == 0) & (b == nz - 2)) | ((z == nz - 1) & (b == 1)), 1, 0)

            @pl.loop(first, pieces)
            def _(p):
                move(b, p).start()

    frames = F * nz
    square[0:frames, :] = shares[...]
    wide = pltpu.roll(square[...].T[0:rank, :], rank, 1)
    square[0:rank, :] = wide
    gram = lax.dot_general(
        wide, square[...], (((1,), (1,)), ((), ())),
        precision=lax.Precision.HIGHEST, preferred_element_type=jnp.float32,
    )
    frame_ridge = ridge_share * frames
    system = jnp.where(diagonal, gram + frame_ridge, gram) + wide
    system = system + jnp.where(lane_r == row_r + rank + frames, frame_ridge, 0.0)
    table[...] = eliminate(system, rank)
    to_scalar = pltpu.make_async_copy(table, table_smem, small_sem.at[0])
    to_scalar.start()
    to_scalar.wait()
    my_base = z * own

    @pl.loop(0, own // 8)
    def _(step):
        rows = pl.ds(pl.multiple_of(step * 8, 8), 8)
        old = pl.ds(pl.multiple_of(my_base + step * 8, 8), 8)
        for half in range(0, rank, 8):
            totals = [None] * 8
            for f in range(F + rank):
                plane = anchor[f, old, :] if f < F else basis[f - F, old, :]
                place = rank + z * F + f if f < F else rank + frames + f - F
                for q in range(8):
                    term = table_smem[half + q, place] * plane
                    totals[q] = term if totals[q] is None else totals[q] + term
            for q in range(8):
                fresh[half + q, rows, :] = totals[q]

    for k in range(PASSES - 2, PASSES):
        finish_sends(k)
    all_sent(shares.at[0 : (nz - 1) * F], share_send).wait_send()
    all_sent(grams.at[0 : nz - 1, 0:2], gram_send).wait_send()
    all_sent(gram_parts.at[0 : group - 1, 0:2], total_send).wait_send()
    all_sent(parts.at[0 : group - 1], part_send).wait_send()

    for n in range(nz - 1):
        near = n + (n >= z).astype(jnp.int32)
        far = nz - 1 - (n + (n >= nz - 1 - z).astype(jnp.int32))
        distance = 1 if n == 0 else nz - n
        source = jnp.where(2 * z < nz, near, far)
        source = jnp.where(z == 0, distance, jnp.where(z == nz - 1, nz - 1 - distance, source))

        @pl.loop(0, pieces)
        def _(piece, source=source):
            take(source, piece).wait_recv()
            for step in range(CHUNK // 8):
                rows = pl.ds(pl.multiple_of(piece * CHUNK + step * 8, 8), 8)
                planes = [owned[source * F + f, rows, :] for f in range(F)]
                for q in range(rank):
                    value = fresh[q, rows, :]
                    for f in range(F):
                        value = value + table_smem[q, rank + source * F + f] * planes[f]
                    fresh[q, rows, :] = value

    for b in range(nz):
        @pl.when(z != b)
        def _(b=b):
            rows = pl.ds(b * own, own)
            pltpu.make_async_remote_copy(
                src_ref=anchor.at[:, rows, :], dst_ref=owned.at[pl.ds(z * F, F)],
                send_sem=move_send.at[b], recv_sem=move_recv.at[z, 0],
                device_id=(r, c, b), device_id_type=MESH,
            ).wait_send()


def deliver(shrunk, coeff, fresh, shrunk_hbm, coeff_hbm, fresh_hbm, sems):
    copies = [pltpu.make_async_copy(coeff, coeff_hbm, sems.at[0])]
    for source, place in ((fresh, fresh_hbm), (shrunk, shrunk_hbm)):
        share = source.shape[0] // 4
        for i in range(4):
            part = pl.ds(i * share, share)
            copies.append(
                pltpu.make_async_copy(source.at[part], place.at[part], sems.at[len(copies)])
            )
    for copy in copies:
        copy.start()
    for copy in copies:
        copy.wait()


def whole_kernel(video, multiplier, foreground, basis, coefficients):
    F, H, W = video.shape
    rank = basis.shape[0]
    nr, nc, nz = (lax.axis_size(name) for name in ("row", "col", "frame"))
    f32 = jnp.float32
    own = H // nz
    group = nr * nc
    vmem = pltpu.VMEM
    dma = pltpu.SemaphoreType.DMA
    pieces = own // CHUNK
    hbm = pl.BlockSpec(memory_space=pl.ANY)
    on_chip = pl.BlockSpec(memory_space=pltpu.VMEM)
    found = pl.pallas_call(
        functools.partial(kernel, (F, H, W, rank, nr, nc, nz)),
        out_shape=(vmem((F, H, W), f32), vmem((F, rank), f32), vmem((rank, own, W), f32)),
        in_specs=[hbm] * 5,
        out_specs=[on_chip] * 3,
        scratch_shapes=[vmem((F + 2, H + 16, W), f32)] * PASSES
        + [
            vmem((F, H, W), f32),
            vmem((F, H, W), f32),
            vmem((rank, H, W), f32),
            vmem((F, H, W), f32),
            vmem((F, H, W), f32),
            vmem((F * nz, own, W), f32),
            vmem((PASSES, SEGMENTS, 16, H // SEGMENTS), f32),
            vmem((PASSES, SEGMENTS, 16, H // SEGMENTS), f32),
            vmem((PASSES, 2, F, 8, 128), f32),
            vmem((H + 8, 128), f32),
            vmem((H + 16, 128), f32),
            vmem((H + 16, 128), f32),
            vmem((H + 24, 128), f32),
            vmem((H + 24, 128), f32),
            vmem((8, 128), f32),
            vmem((F, rank, 8, 128), f32),
            vmem((rank + F, rank, 128), f32),
            vmem((nz, 8, 128), f32),
            vmem((group, 8, 128), f32),
            vmem((rank, rank, 128), f32),
            vmem((group, rank, 128), f32),
            vmem((nz * F, 128), f32),
            vmem((128, 128), f32),
            vmem((rank, 128), f32),
            pltpu.SMEM((F, rank), f32),
            pltpu.SMEM((rank, 128), f32),
            dma((9,)),
            dma((2, 12)),
            dma((2, 6 + 2 * SEGMENTS + H // CHUNK)),
            dma((1,)),
            dma((group,)),
            dma((1,)),
            dma((nz,)),
            dma((1,)),
            dma((group,)),
            dma((1,)),
            dma((nz,)),
            dma((nz,)),
            dma((nz, pieces)),
            dma((1,)),
        ],
        compiler_params=pltpu.CompilerParams(
            collective_id=0, has_side_effects=True, vmem_limit_bytes=32 * 1024 * 1024
        ),
    )(
        *(
            pltpu.with_memory_space_constraint(x, pltpu.HBM)
            for x in (coefficients, video, multiplier, foreground, basis)
        )
    )
    return pl.pallas_call(
        deliver,
        out_shape=(
            jax.ShapeDtypeStruct((F, H, W), f32),
            jax.ShapeDtypeStruct((F, rank), f32),
            jax.ShapeDtypeStruct((rank, own, W), f32),
        ),
        in_specs=[on_chip] * 3,
        out_specs=[hbm] * 3,
        scratch_shapes=[dma((9,))],
    )(*(pltpu.with_memory_space_constraint(x, pltpu.VMEM) for x in found))


def body(video, multiplier, foreground, basis, coefficients):
    F, H, W = video.shape
    rank = basis.shape[0]
    nz = lax.axis_size("frame")
    fits = (
        H % nz == 0 and (H // nz) % 8 == 0 and (H // nz) % CHUNK == 0 and W % 128 == 0
        and H % 16 == 0 and H % (SEGMENTS * CHUNK) == 0 and lax.axis_size("row") <= 2
        and F % 4 == 0 and F < 8 and rank == 16 and nz >= 2 and F * nz == rank and 2 * rank + F * nz <= 128
    )
    run = whole_kernel if fits else local
    return run(video, multiplier, foreground, basis, coefficients)


def solution(mesh):
    placed = (
        P("frame", "row", "col"),
        P("frame", "row", "col"),
        P("frame", "row", "col"),
        P(None, "row", "col"),
        P("frame", None),
    )
    return jax.shard_map(
        body,
        mesh=mesh,
        in_specs=placed,
        out_specs=(P("frame", "row", "col"), P("frame", None), P(None, ("row", "frame"), "col")),
        check_vma=False,
    )
```

```python
import functools

import jax
import jax.numpy as jnp
from jax import lax
from jax.experimental import pallas as pl
from jax.experimental.pallas import tpu as pltpu
from jax.sharding import PartitionSpec as P

PASSES = 3


relax_rate = 0.8
smooth_weight = 0.5
smooth_floor = 0.25
shrink_level = 0.4
dual_scale = 0.8
ridge_share = 0.1


def with_halo(block, sides, width):
    for axis, dim in sides:
        count = lax.axis_size(axis)
        forward = [(i, i + 1) for i in range(count - 1)]
        backward = [(target, source) for source, target in forward]
        low = lax.ppermute(
            lax.slice_in_dim(block, block.shape[dim] - width, None, axis=dim), axis, forward
        )
        high = lax.ppermute(lax.slice_in_dim(block, 0, width, axis=dim), axis, backward)
        block = jnp.concatenate([low, block, high], axis=dim)
    return block


def forward_cells(padded, direction, shape):
    starts = [0, 0, 0]
    starts[direction] = 1
    limits = [starts[axis_dim] + shape[axis_dim] for axis_dim in range(3)]
    return lax.slice(padded, starts, limits)


def descend(padded, source, anchor, extent):
    shape = tuple((int(length) - 1 for length in padded.shape))
    here_cells = padded[:-1, :-1, :-1]
    slopes = []
    for direction in range(3):
        ahead_cells = forward_cells(padded, direction, shape)
        places = anchor[direction] + jnp.arange(shape[direction], dtype=jnp.int32)
        inside = (places >= 0) & (places < extent[direction] - 1)
        layout = [1, 1, 1]
        layout[direction] = shape[direction]
        inside = inside.reshape(layout)
        slopes.append(jnp.where(inside, ahead_cells - here_cells, jnp.zeros_like(here_cells)))
    weight = lax.rsqrt(
        smooth_floor + slopes[0] * slopes[0] + slopes[1] * slopes[1] + slopes[2] * slopes[2]
    )
    fluxes = [slope_part * weight for slope_part in slopes]
    spread = (
        fluxes[0][1:, 1:, 1:]
        - fluxes[0][:-1, 1:, 1:]
        + (fluxes[1][1:, 1:, 1:] - fluxes[1][1:, :-1, 1:])
        + (fluxes[2][1:, 1:, 1:] - fluxes[2][1:, 1:, :-1])
    )
    center = padded[1:-1, 1:-1, 1:-1]
    return center + relax_rate * (source - center + smooth_weight * spread)


def solve_definite(matrix, right_side):
    factor_lower = jnp.linalg.cholesky(matrix)
    half_solved = lax.linalg.triangular_solve(factor_lower, right_side, left_side=True, lower=True)
    return lax.linalg.triangular_solve(
        factor_lower, half_solved, left_side=True, lower=True, transpose_a=True
    )


def local(video, multiplier, foreground, basis, coefficients):
    highest = lax.Precision.HIGHEST
    frames_here, rows_here, cols_here = video.shape
    rank_size = basis.shape[0]
    frame_count = lax.axis_size("frame")
    row_count = lax.axis_size("row")
    col_count = lax.axis_size("col")
    extent = (frames_here * frame_count, rows_here * row_count, cols_here * col_count)
    frame_slot = lax.axis_index("frame")
    corner = (
        frame_slot * frames_here,
        lax.axis_index("row") * rows_here,
        lax.axis_index("col") * cols_here,
    )
    pixels = rows_here * cols_here
    flat_basis = basis.reshape(rank_size, pixels)
    background = jnp.dot(coefficients, flat_basis, precision=highest).reshape(video.shape)
    target = video - background + dual_scale * multiplier
    current = foreground
    for sweep in range(PASSES):
        padded = with_halo(current, (("row", 1), ("col", 2), ("frame", 0)), 1)
        current = descend(padded, target, tuple((start_cell - 1 for start_cell in corner)), extent)
    shrunk = current - jnp.clip(current, -shrink_level, shrink_level)
    residual_target = video + dual_scale * multiplier - shrunk
    flat_target = residual_target.reshape(frames_here, pixels)
    gram_part = jnp.dot(flat_basis, flat_basis.T, precision=highest)
    cross_part = jnp.dot(flat_basis, flat_target.T, precision=highest)
    gram_sum, cross_sum = lax.psum((gram_part, cross_part), ("row", "col"))
    identity_matrix = jnp.eye(rank_size, dtype=gram_sum.dtype)
    pixel_ridge = ridge_share * pixels * row_count * col_count
    coeff_rows = solve_definite(
        gram_sum + pixel_ridge * identity_matrix, cross_sum + pixel_ridge * coefficients.T
    )
    total_part = jnp.dot(coeff_rows, flat_target, precision=highest).reshape(
        rank_size, rows_here, cols_here
    )
    frame_gram_part = jnp.dot(coeff_rows, coeff_rows.T, precision=highest)
    owned_rows = rows_here // frame_count
    owned_sums = lax.psum_scatter(total_part, "frame", scatter_dimension=1, tiled=True)
    frame_gram = lax.psum(frame_gram_part, "frame")
    old_owned = lax.dynamic_slice_in_dim(basis, frame_slot * owned_rows, owned_rows, 1)
    frame_ridge = ridge_share * frames_here * frame_count
    right_side = (owned_sums + frame_ridge * old_owned).reshape(rank_size, owned_rows * cols_here)
    new_basis = solve_definite(frame_gram + frame_ridge * identity_matrix, right_side)
    return (shrunk, coeff_rows.T, new_basis.reshape(rank_size, owned_rows, cols_here))


MESH = pl.DeviceIdType.MESH
CHUNK = 24
SEGMENTS = 4


def eliminate(matrix, size):
    lanes = lax.broadcasted_iota(jnp.int32, matrix.shape, 1)
    rows = lax.broadcasted_iota(jnp.int32, matrix.shape, 0)
    for k in range(size):
        pivot = matrix[k : k + 1, k : k + 1]
        scaled = matrix[k : k + 1, :] / pivot
        column = jnp.sum(jnp.where(lanes == k, matrix, 0.0), axis=1, keepdims=True)
        matrix = jnp.where(rows == k, scaled, matrix - column * scaled)
    return matrix


def kernel(
    sizes, coeff_hbm, video_hbm, mult_hbm, fore_hbm, basis_hbm,
    result, coeff_out, fresh,
    field0, field1, field2, video, mult, basis, anchor, target, owned,
    packed, arrived, corner, edge_next, edge_flux, first_cols, left_now, left_next, bottom_row,
    cross, sums, grams, gram_parts, inverse, parts, shares, square, table, coeff_ref, table_smem,
    in_sems, halo_send, halo_recv, part_send, part_recv,
    gram_send, gram_recv, total_send, total_recv, share_send, share_recv, move_send, move_recv, small_sem,
):
    field = (field0, field1, field2)
    F, H, W, rank, nr, nc, nz = sizes
    r = lax.axis_index("row")
    c = lax.axis_index("col")
    z = lax.axis_index("frame")
    own = H // nz
    pieces = own // CHUNK
    half = H // 2
    flip = lax.rem(r, 2)

    steps = H // CHUNK

    def chunk_at(step):
        return step + flip * (steps - 1 - 2 * step)

    def rows_at(step, offset=0):
        return pl.ds(pl.multiple_of(offset + chunk_at(step) * CHUNK, 8), CHUNK)

    span = H // SEGMENTS
    per = steps // SEGMENTS

    def segment_start(j):
        return pl.multiple_of((j + flip * (SEGMENTS - 1 - 2 * j)) * span, 8)

    def half_start(h):
        return pl.multiple_of((h + flip * (1 - 2 * h)) * half, 8)

    inner = (z > 0) & (z < nz - 1)

    def inside(dr, dc, dz):
        ok = None
        for at, step, count in ((r, dr, nr), (c, dc, nc), (z, dz, nz)):
            if step != 0:
                test = (at + step >= 0) & (at + step < count)
                ok = test if ok is None else ok & test
        return ok

    halves = [pl.ds(half_start(h), half) for h in range(2)]
    loads = [
        pltpu.make_async_copy(src, dst, in_sems.at[i])
        for i, (src, dst) in enumerate(
            [
                (
                    fore_hbm.at[:, halves[h], :],
                    field0.at[1 : F + 1, pl.ds(pl.multiple_of(half_start(h) + 8, 8), half), :],
                )
                for h in range(2)
            ]
            + [(coeff_hbm, coeff_ref)]
            + [
                (src.at[:, rows, :], dst.at[:, rows, :])
                for rows in halves
                for src, dst in ((video_hbm, video), (mult_hbm, mult), (basis_hbm, basis))
            ]
        )
    ]
    for load in loads[:2]:
        load.start()

    barrier = pltpu.get_barrier_semaphore()
    beside = ((0, 0, 1), (0, 1, 0), (1, 0, 0), (1, 0, -1), (0, 1, -1), (1, -1, 0))
    beside += tuple(tuple(-s for s in step) for step in beside)
    for step in beside:
        @pl.when(inside(*step))
        def _(step=step):
            pl.semaphore_signal(
                barrier,
                inc=1,
                device_id=(r + step[0], c + step[1], z + step[2]),
                device_id_type=MESH,
            )
    expected = jnp.int32(0)
    for step in beside:
        expected = expected + inside(*step).astype(jnp.int32)
    for load in loads[2:]:
        load.start()

    pl.semaphore_wait(barrier, expected)

    lane_h = lax.broadcasted_iota(jnp.int32, (span, 128), 1)

    def pack_columns(k, j):
        base = segment_start(j)
        tile = jnp.zeros((span, 128), jnp.float32)
        for f in range(F):
            for lane, at in ((f, 0), (8 + f, W - 1)):
                lanes = field[k][f + 1, pl.ds(base + 8, span), (at // 128) * 128 : (at // 128) * 128 + 128]
                tile = jnp.where(lane_h == lane, lanes[:, at % 128 : at % 128 + 1], tile)
        first_cols[pl.ds(base + 8, span), :] = tile
        packed[k, j] = tile.T[:16, :]

    strips = range(4)
    corners = (4, 5)

    def column_list(k, j):
        return (
            (packed.at[k, j, 0:F], arrived.at[k, j, 1 : F + 1], (0, -1, 0)),
            (packed.at[k, j, 8 : 8 + F], arrived.at[k, j, 8 : 8 + F], (0, 1, 0)),
            (packed.at[k, j, F - 1 : F], arrived.at[k, j, 0:1], (0, -1, 1)),
            (packed.at[k, j, 8:9], arrived.at[k, j, 8 + F : 9 + F], (0, 1, -1)),
        )

    def halo_list(k):
        fk = field[k]
        mid = slice(1, F + 1)
        return (
            (fk.at[mid, H : H + 8, :], fk.at[mid, 0:8, :], (1, 0, 0)),
            (fk.at[mid, 8:16, :], fk.at[mid, H + 8 : H + 16, :], (-1, 0, 0)),
            (fk.at[F, 8:9, :], fk.at[0, H + 8 : H + 9, :], (-1, 0, 1)),
            (fk.at[1, H + 7 : H + 8, :], fk.at[F + 1, 7:8, :], (1, 0, -1)),
            (fk.at[mid, H : H + 8, 0:128], corner.at[k, 0], (1, -1, 0)),
            (fk.at[mid, 8:16, W - 128 : W], corner.at[k, 1], (-1, 1, 0)),
        )

    def halo_copy(k, i, leave, src, dst, step):
        return pltpu.make_async_remote_copy(
            src_ref=src, dst_ref=dst,
            send_sem=halo_send.at[k % 2, leave], recv_sem=halo_recv.at[k % 2, i],
            device_id=(r + step[0], c + step[1], z + step[2]), device_id_type=MESH,
        )

    def send_columns(k, j):
        for i, (src, dst, step) in enumerate(column_list(k, j)):
            @pl.when(inside(*step))
            def _(i=i, src=src, dst=dst, step=step):
                halo_copy(k, 3 + 2 * j + i % 2, 3 + i, src, dst, step).start()

    def wait_columns(k, j):
        for side, step, corner_step, small, large in (
            (0, (0, -1, 0), (0, -1, 1), slice(1, F + 1), slice(0, F + 1)),
            (1, (0, 1, 0), (0, 1, -1), slice(8, 8 + F), slice(8, 9 + F)),
        ):
            near = inside(*(-s for s in step))
            both = inside(*(-s for s in corner_step))
            for turn, rows in ((near & ~both, small), (both, large)):
                @pl.when(turn)
                def _(side=side, step=step, rows=rows):
                    ref = arrived.at[k, j, rows]
                    halo_copy(k, 3 + 2 * j + side, 0, ref, ref, step).wait_recv()

    def face(k, step, up):
        fk = field[k]
        rows = rows_at(step, 8)
        at = 3 + 2 * SEGMENTS + step
        mine, theirs = (F, 0) if up else (1, F + 1)
        src = fore_hbm.at[mine - 1, rows_at(step)] if k == 0 else fk.at[mine, rows]
        return halo_copy(
            k, at, 7 if up else 8, src, fk.at[theirs, rows], (0, 0, 1 if up else -1)
        )

    def send_faces(k, low, high):
        @pl.loop(low, high)
        def _(step):
            for up in (True, False):
                @pl.when(inside(0, 0, 1 if up else -1))
                def _(up=up):
                    face(k, step, up).start()

    def wait_face(k, step):
        for turn, frames in ((inner, slice(0, 2)), (~inner, slice(0, 1))):
            @pl.when(turn)
            def _(frames=frames):
                ref = field[k].at[frames, rows_at(step, 8), :]
                halo_copy(k, 3 + 2 * SEGMENTS + step, 0, ref, ref, (0, 0, 1)).wait_recv()

    def send_halos(k, which):
        every = halo_list(k)
        for i in which:
            src, dst, step = every[i]

            @pl.when(inside(*step))
            def _(i=i, src=src, dst=dst, step=step):
                halo_copy(k, i // 2, i // 2, src, dst, step).start()

    def wait_halos(k, which):
        every = halo_list(k)
        for i in which:
            src, dst, step = every[i]

            @pl.when(inside(*(-s for s in step)))
            def _(i=i, src=src, dst=dst, step=step):
                halo_copy(k, i // 2, i // 2, src, dst, step).wait_recv()

    def finish_sends(k):
        for i, (src, dst, step) in enumerate(halo_list(k)):
            @pl.when(inside(*step))
            def _(i=i, src=src, dst=dst, step=step):
                halo_copy(k, i // 2, i // 2, src, dst, step).wait_send()

        every = (
            (packed.at[k, :, 0:F], arrived.at[k, :, 1 : F + 1], (0, -1, 0)),
            (packed.at[k, :, 8 : 8 + F], arrived.at[k, :, 8 : 8 + F], (0, 1, 0)),
            (packed.at[k, :, F - 1 : F], arrived.at[k, :, 0:1], (0, -1, 1)),
            (packed.at[k, :, 8:9], arrived.at[k, :, 8 + F : 9 + F], (0, 1, -1)),
            (field[k].at[F, 8 : H + 8, :], field[k].at[0, 8 : H + 8, :], (0, 0, 1)),
            (field[k].at[1, 8 : H + 8, :], field[k].at[F + 1, 8 : H + 8, :], (0, 0, -1)),
        )
        for i, (src, dst, step) in enumerate(every):
            @pl.when(inside(*step))
            def _(i=i, src=src, dst=dst, step=step):
                halo_copy(k, 0, 3 + i, src, dst, step).wait_send()

    def prepare_columns(k, j):
        base = segment_start(j)
        spread = jnp.concatenate(
            [arrived[k, j], jnp.zeros((112, span), jnp.float32)], axis=0
        ).T
        edge_next[pl.ds(base + 8, span), :] = spread
        left_now[pl.ds(base + 8, span), :] = pltpu.roll(spread, 120, 1)
        left_next[pl.ds(base + 8, span), :] = pltpu.roll(spread, 119, 1)
        low, count = pl.multiple_of(base + 8 * flip, 8), span + 8
        here = left_now[pl.ds(low, count), :]
        ahead = left_next[pl.ds(low, count), :]
        lane = lax.broadcasted_iota(jnp.int32, (count, 128), 1)
        row = lax.broadcasted_iota(jnp.int32, (count, 128), 0) + (low - 8)
        slope0 = jnp.where((lane == F - 1) & (z == nz - 1), 0.0, ahead - here)
        after = left_now[pl.ds(low, count + 8), :]
        below = jnp.where(
            row == H - 1, bottom_row[0:1, :], pltpu.roll(after, count + 7, 0)[:count]
        )
        slope1 = jnp.where((row == H - 1) & (r == nr - 1), 0.0, below - here)
        slope2 = first_cols[pl.ds(low, count), :] - here
        weight = lax.rsqrt(smooth_floor + slope0 * slope0 + slope1 * slope1 + slope2 * slope2)
        edge_flux[pl.ds(low, count), :] = jnp.where(c == 0, 0.0, slope2 * weight)

    def take_corners(k):
        wait_halos(k, corners)
        lane8 = lax.broadcasted_iota(jnp.int32, (8, 128), 1)
        top = jnp.zeros((8, 128), jnp.float32)
        bottom = jnp.zeros((8, 128), jnp.float32)
        for f in range(F):
            top = jnp.where(lane8 == f + 1, corner[k, 0, f][:, 0:1], top)
            bottom = jnp.where(lane8 == f, corner[k, 1, f][:, 127:128], bottom)
        edge_next[0:8, :] = top
        bottom_row[...] = bottom

    def sweep(k, last, start):
        R = CHUNK
        tiles = W // 128
        row_8 = lax.broadcasted_iota(jnp.int32, (8, 128), 0) + (r * H + start)
        above_image = row_8 - 8 < 0
        last_image_row = row_8 + (R - 8) >= nr * H - 1
        columns = edge_next[pl.ds(start, R + 8), :]
        fluxes_in = edge_flux[pl.ds(start + 8, R), :]
        at = pl.ds(start, R)

        def frame(f):
            return [
                field[k][f, pl.ds(start, R + 16), w * 128 : w * 128 + 128] for w in range(tiles)
            ]

        now = frame(0)
        flux0_before = None
        for f in range(-1, F):
            after = frame(f + 2)
            skip = 8 if f < 0 else 0
            n = R + 8 - skip
            lane = lax.broadcasted_iota(jnp.int32, (n, 128), 1)
            here = [t[skip : R + 8] for t in now]
            turned = [pltpu.roll(t, 127, 1) for t in here]
            wall = jnp.broadcast_to(columns[skip:, f + 1 : f + 2], (n, 128))
            flux0, flux1, flux2 = [], [], []
            for w in range(tiles):
                slope0 = after[w][skip : R + 8] - here[w]
                if f == F - 1:
                    slope0 = jnp.where(z == nz - 1, 0.0, slope0)
                slope1 = pltpu.roll(now[w][skip:], n + 7, 0)[:n] - here[w]
                slope1 = jnp.concatenate(
                    [slope1[: n - 8], jnp.where(last_image_row, 0.0, slope1[n - 8 :])], axis=0
                )
                beyond = turned[w + 1] if w + 1 < tiles else wall
                slope2 = jnp.where(lane == 127, beyond, turned[w]) - here[w]
                if w + 1 == tiles:
                    slope2 = jnp.where((lane == 127) & (c == nc - 1), 0.0, slope2)
                weight = lax.rsqrt(
                    smooth_floor + slope0 * slope0 + slope1 * slope1 + slope2 * slope2
                )
                flux0.append((slope0 * weight)[8 - skip :])
                if f >= 0:
                    flux = slope1 * weight
                    flux1.append(
                        jnp.concatenate(
                            [jnp.where(above_image, 0.0, flux[:8]), flux[8:]], axis=0
                        )
                    )
                    flux2.append((slope2 * weight)[8:])
            if f < 0:
                flux0 = [jnp.where(z == 0, 0.0, t) for t in flux0]
            else:
                moved = [pltpu.roll(t, 1, 1) for t in flux2]
                entry = jnp.broadcast_to(fluxes_in[:, f : f + 1], (R, 128))
                lane = lax.broadcasted_iota(jnp.int32, (R, 128), 1)
                for w in range(tiles):
                    left = jnp.where(lane == 0, moved[w - 1] if w > 0 else entry, moved[w])
                    above = pltpu.roll(flux1[w], 1, 0)[8:]
                    spread = (flux0[w] - flux0_before[w]) + (flux1[w][8:] - above) + (flux2[w] - left)
                    lanes = slice(w * 128, w * 128 + 128)
                    value = (1.0 - relax_rate) * here[w][8:] + (
                        target[f, at, lanes] + (relax_rate * smooth_weight) * spread
                    )
                    if last:
                        shrunk = value - jnp.clip(value, -shrink_level, shrink_level)
                        result[f, at, lanes] = shrunk
                        anchor[f, at, lanes] = anchor[f, at, lanes] - shrunk
                    else:
                        field[k + 1][f + 1, pl.ds(start + 8, R), lanes] = value
            flux0_before = flux0
            now = after

    def products(left_of, right_of, lefts, rights, first, count, start, store):
        def body(step, totals):
            rows = pl.ds(pl.multiple_of(first + step * 8, 8), 8)
            a = [left_of[i, rows, :] for i in lefts]
            b = [right_of[j, rows, :] for j in rights]
            out = []
            for x in range(len(lefts)):
                for y in range(len(rights)):
                    prod = a[x] * b[y]
                    total = totals[len(out)]
                    for w in range(W // 128):
                        total = total + prod[:, w * 128 : w * 128 + 128]
                    out.append(total)
            return tuple(out)

        totals = lax.fori_loop(
            0, count // 8, body, tuple(start(i, j) for i in lefts for j in rights), unroll=3 if count % 24 == 0 else 1
        )
        n = 0
        for i in lefts:
            for j in rights:
                store(i, j, totals[n])
                n += 1

    def held(block):
        return (block - z >= 2) | (z - block >= 2)

    def move(block, piece):
        rows = pl.ds(pl.multiple_of(block * own + piece * CHUNK, 8), CHUNK)
        spot = pl.ds(pl.multiple_of(piece * CHUNK, 8), CHUNK)
        return pltpu.make_async_remote_copy(
            src_ref=anchor.at[:, rows, :], dst_ref=owned.at[pl.ds(z * F, F), spot, :],
            send_sem=move_send.at[block], recv_sem=move_recv.at[z, piece],
            device_id=(r, c, block), device_id_type=MESH,
        )

    def take(source, piece):
        rows = pl.ds(pl.multiple_of(z * own + piece * CHUNK, 8), CHUNK)
        spot = pl.ds(pl.multiple_of(piece * CHUNK, 8), CHUNK)
        return pltpu.make_async_remote_copy(
            src_ref=anchor.at[:, rows, :], dst_ref=owned.at[pl.ds(source * F, F), spot, :],
            send_sem=move_send.at[source], recv_sem=move_recv.at[source, piece],
            device_id=(r, c, source), device_id_type=MESH,
        )

    send_faces(0, 0, 1)
    for j in range(SEGMENTS):
        if j % (SEGMENTS // 2) == 0:
            loads[j // (SEGMENTS // 2)].wait()
        pack_columns(0, j)
        send_columns(0, j)
        if j == SEGMENTS // 2:
            send_halos(0, strips)
            send_halos(0, corners)
        send_faces(0, max(1, j * per), (j + 1) * per)

    zero_tile = jnp.zeros((8, 128), jnp.float32)

    def store_gram(i, j, value):
        row = jnp.sum(value, axis=0, keepdims=True)
        sums[j, i : i + 1, :] = row
        if i // 4 != j // 4:
            sums[i, j : j + 1, :] = row

    lane_r = lax.broadcasted_iota(jnp.int32, (rank, 128), 1)
    row_r = lax.broadcasted_iota(jnp.int32, (rank, 128), 0)

    def gram_share():
        for i in range(0, rank, 4):
            for j in range(i, rank, 4):
                products(
                    basis, basis, range(i, i + 4), range(j, j + 4), z * own, own,
                    lambda i, j: zero_tile, store_gram,
                )
        tile = jnp.zeros((rank, 128), jnp.float32)
        for q in range(rank):
            tile = jnp.where(lane_r == q, jnp.sum(sums[q], axis=1, keepdims=True), tile)
        lane = lax.broadcasted_iota(jnp.int32, (8, 128), 1)
        tile = jnp.where(lane < rank, tile[:8], pltpu.roll(tile[8:], rank, 1))
        tile = jnp.where(lane < 2 * rank, tile, pltpu.roll(pltpu.roll(tile, 4, 0), 2 * rank, 1))
        tile = jnp.where(lane < 4 * rank, tile, pltpu.roll(pltpu.roll(tile, 6, 0), 4 * rank, 1))
        grams[z] = tile

    def unfold(tile):
        row = lax.broadcasted_iota(jnp.int32, (8, 128), 0)
        tile = jnp.where(row < 2, tile, pltpu.roll(pltpu.roll(tile, 2, 0), 128 - 4 * rank, 1))
        tile = jnp.where(row < 4, tile, pltpu.roll(pltpu.roll(tile, 4, 0), 128 - 2 * rank, 1))
        tile = jnp.concatenate([tile, pltpu.roll(tile, 128 - rank, 1)], axis=0)
        return jnp.where(lane_r < rank, tile, 0.0)

    def all_sent(block, sem):
        return pltpu.make_async_remote_copy(
            src_ref=block, dst_ref=block, send_sem=sem.at[0], recv_sem=sem.at[0],
            device_id=(r, c, lax.rem(z + 1, nz)), device_id_type=MESH,
        )

    def all_here(block, sem):
        return pltpu.make_async_remote_copy(
            src_ref=block, dst_ref=block, send_sem=sem.at[0], recv_sem=sem.at[0],
            device_id=(r, c, lax.rem(z + 1, nz)), device_id_type=MESH,
        )

    def share_gram(d):
        return pltpu.make_async_remote_copy(
            src_ref=grams.at[z, 0:2], dst_ref=grams.at[z, 0:2],
            send_sem=gram_send.at[0], recv_sem=gram_recv.at[0],
            device_id=(r, c, lax.rem(z + d, nz)), device_id_type=MESH,
        )

    group = nr * nc
    me = r * nc + c

    def share_total(d):
        other = lax.rem(me + d, group)
        return pltpu.make_async_remote_copy(
            src_ref=gram_parts.at[me, 0:2], dst_ref=gram_parts.at[me, 0:2],
            send_sem=total_send.at[0], recv_sem=total_recv.at[0],
            device_id=(other // nc, lax.rem(other, nc), z), device_id_type=MESH,
        )

    def store_cross(i, j, value):
        cross[j, i] = value

    def find_target(h):
        for load in loads[3 + 3 * h : 6 + 3 * h]:
            load.wait()

        @pl.loop(0, half // 8)
        def _(step):
            rows = pl.ds(pl.multiple_of(half_start(h) + step * 8, 8), 8)
            totals = [None] * F
            for q in range(rank):
                plane = basis[q, rows, :]
                for f in range(F):
                    term = coeff_ref[f, q] * plane
                    totals[f] = term if totals[f] is None else totals[f] + term
            for f in range(F):
                lifted = dual_scale * mult[f, rows, :]
                anchor[f, rows, :] = video[f, rows, :] + lifted
                target[f, rows, :] = relax_rate * (video[f, rows, :] - totals[f] + lifted)

    loads[2].wait()
    find_target(0)
    find_target(1)
    gram_share()

    def advance(k, step):
        start = pl.multiple_of(chunk_at(step) * CHUNK, 8)
        sweep(k, k == PASSES - 1, start)
        if k == PASSES - 1:
            place, piece = chunk_at(step) // pieces, lax.rem(chunk_at(step), pieces)

            @pl.when((place - z == 1) | (z - place == 1))
            def _():
                move(place, piece).start()

            for i in range(0, rank, 4):
                products(
                    basis, anchor, range(i, i + 4), range(F), start, CHUNK,
                    lambda i, j: cross[j, i], store_cross,
                )

    cross[...] = jnp.zeros_like(cross)
    bottom_row[...] = jnp.zeros_like(bottom_row)
    for k in range(PASSES):
        last = k == PASSES - 1
        if k > 0 and not last:
            finish_sends(k - 1)
        wait_columns(k, 0)
        prepare_columns(k, 0)
        wait_face(k, 0)

        @pl.loop(0, SEGMENTS)
        def _(j, k=k, last=last):
            @pl.loop(j * per, (j + 1) * per - 1)
            def _(step):
                wait_face(k, step + 1)
                advance(k, step)

            final = j == SEGMENTS - 1
            if k == PASSES - 2:
                @pl.when(j == 1)
                def _():
                    for d in range(1, nz):
                        share_gram(d).start()
            if k == PASSES - 1:
                @pl.when(j == 1)
                def _():
                    all_here(grams.at[0 : nz - 1, 0:2], gram_recv).wait_recv()
                    total = grams[0]
                    for i in range(1, nz):
                        total = total + grams[i]
                    gram_parts[me] = total
                    for d in range(1, group):
                        share_total(d).start()

            @pl.when(j == SEGMENTS - 2)
            def _():
                take_corners(k)

            @pl.when(~final)
            def _():
                wait_columns(k, j + 1)
                prepare_columns(k, j + 1)
                wait_face(k, (j + 1) * per)

            @pl.when(final)
            def _():
                wait_halos(k, strips)

            advance(k, (j + 1) * per - 1)
            if not last:
                @pl.when(final)
                def _():
                    send_halos(k + 1, strips)
                    send_halos(k + 1, corners)

                pack_columns(k + 1, j)
                send_columns(k + 1, j)
                send_faces(k + 1, j * per, (j + 1) * per)


    def send_held(turn, low, high):
        for b in range(nz):
            @pl.when(held(b) & turn)
            def _(b=b):
                for p in range(low, high):
                    move(b, p).start()

    for far, near in ((nz - 1, 0), (0, nz - 1)):
        place = far - 1 if far > near else far + 1

        @pl.when((z == near) & held(jnp.int32(place)))
        def _(place=place):
            move(place, 0).start()

    for j in range(F):
        for i in range(rank):
            sums[rank + j, i : i + 1, :] = jnp.sum(cross[j, i], axis=0, keepdims=True)

    part = jnp.zeros((rank, 128), jnp.float32)
    for q in range(rank, rank + F):
        part = jnp.where(lane_r == q, jnp.sum(sums[q], axis=1, keepdims=True), part)
    parts[me] = part

    def share_part(d):
        other = lax.rem(me + d, group)
        return pltpu.make_async_remote_copy(
            src_ref=parts.at[me], dst_ref=parts.at[me],
            send_sem=part_send.at[0], recv_sem=part_recv.at[0],
            device_id=(other // nc, lax.rem(other, nc), z), device_id_type=MESH,
        )

    for d in range(1, group):
        share_part(d).start()
    pixel_ridge = ridge_share * H * W * group
    diagonal = lane_r == row_r
    before = jnp.zeros((rank, 128), jnp.float32)
    for q in range(rank):
        for f in range(F):
            before = jnp.where((row_r == q) & (lane_r == rank + f), coeff_ref[f, q], before)
    all_here(gram_parts.at[0 : group - 1, 0:2], total_recv).wait_recv()
    total = gram_parts[0]
    for i in range(1, group):
        total = total + gram_parts[i]
    diagonal = lane_r == row_r
    system = unfold(total) + jnp.where(
        diagonal, pixel_ridge, jnp.where(lane_r == row_r + rank, 1.0, 0.0)
    )
    system = eliminate(system, rank)
    for q in range(rank):
        inverse[q] = jnp.broadcast_to(system[:, rank + q : rank + q + 1], (rank, 128))
    all_here(parts.at[0 : group - 1], part_recv).wait_recv()
    total = parts[0]
    for i in range(1, group):
        total = total + parts[i]
    total = total + pixel_ridge * before
    solved = inverse[0] * total[0:1, :]
    for q in range(1, rank):
        solved = solved + inverse[q] * total[q : q + 1, :]
    square[...] = jnp.zeros_like(square)
    square[0:rank, :] = solved
    mine = square[...].T[rank : rank + F, :]
    shares[pl.ds(z * F, F), :] = mine

    def share_rows(d):
        return pltpu.make_async_remote_copy(
            src_ref=shares.at[pl.ds(z * F, F)], dst_ref=shares.at[pl.ds(z * F, F)],
            send_sem=share_send.at[0], recv_sem=share_recv.at[0],
            device_id=(r, c, lax.rem(z + d, nz)), device_id_type=MESH,
        )

    for d in range(1, nz):
        share_rows(d).start()

    send_held(inner, 0, pieces)
    coeff_out[...] = mine[:, 0:rank]
    all_here(shares.at[0 : (nz - 1) * F], share_recv).wait_recv()
    for b in range(nz):
        @pl.when(held(b) & ~inner)
        def _(b=b):
            first = jnp.where(((z == 0) & (b == nz - 2)) | ((z == nz - 1) & (b == 1)), 1, 0)

            @pl.loop(first, pieces)
            def _(p):
                move(b, p).start()

    frames = F * nz
    square[0:frames, :] = shares[...]
    wide = pltpu.roll(square[...].T[0:rank, :], rank, 1)
    square[0:rank, :] = wide
    gram = lax.dot_general(
        wide, square[...], (((1,), (1,)), ((), ())),
        precision=lax.Precision.HIGHEST, preferred_element_type=jnp.float32,
    )
    frame_ridge = ridge_share * frames
    system = jnp.where(diagonal, gram + frame_ridge, gram) + wide
    system = system + jnp.where(lane_r == row_r + rank + frames, frame_ridge, 0.0)
    table[...] = eliminate(system, rank)
    to_scalar = pltpu.make_async_copy(table, table_smem, small_sem.at[0])
    to_scalar.start()
    to_scalar.wait()
    my_base = z * own

    @pl.loop(0, own // 8)
    def _(step):
        rows = pl.ds(pl.multiple_of(step * 8, 8), 8)
        old = pl.ds(pl.multiple_of(my_base + step * 8, 8), 8)
        for half in range(0, rank, 8):
            totals = [None] * 8
            for f in range(F + rank):
                plane = anchor[f, old, :] if f < F else basis[f - F, old, :]
                place = rank + z * F + f if f < F else rank + frames + f - F
                for q in range(8):
                    term = table_smem[half + q, place] * plane
                    totals[q] = term if totals[q] is None else totals[q] + term
            for q in range(8):
                fresh[half + q, rows, :] = totals[q]

    for k in range(PASSES - 2, PASSES):
        finish_sends(k)
    all_sent(shares.at[0 : (nz - 1) * F], share_send).wait_send()
    all_sent(grams.at[0 : nz - 1, 0:2], gram_send).wait_send()
    all_sent(gram_parts.at[0 : group - 1, 0:2], total_send).wait_send()
    all_sent(parts.at[0 : group - 1], part_send).wait_send()

    for n in range(nz - 1):
        near = n + (n >= z).astype(jnp.int32)
        far = nz - 1 - (n + (n >= nz - 1 - z).astype(jnp.int32))
        distance = 1 if n == 0 else nz - n
        source = jnp.where(2 * z < nz, near, far)
        source = jnp.where(z == 0, distance, jnp.where(z == nz - 1, nz - 1 - distance, source))

        @pl.loop(0, pieces)
        def _(piece, source=source):
            take(source, piece).wait_recv()
            for step in range(CHUNK // 8):
                rows = pl.ds(pl.multiple_of(piece * CHUNK + step * 8, 8), 8)
                planes = [owned[source * F + f, rows, :] for f in range(F)]
                for q in range(rank):
                    value = fresh[q, rows, :]
                    for f in range(F):
                        value = value + table_smem[q, rank + source * F + f] * planes[f]
                    fresh[q, rows, :] = value

    for b in range(nz):
        @pl.when(z != b)
        def _(b=b):
            rows = pl.ds(b * own, own)
            pltpu.make_async_remote_copy(
                src_ref=anchor.at[:, rows, :], dst_ref=owned.at[pl.ds(z * F, F)],
                send_sem=move_send.at[b], recv_sem=move_recv.at[z, 0],
                device_id=(r, c, b), device_id_type=MESH,
            ).wait_send()


def deliver(shrunk, coeff, fresh, shrunk_hbm, coeff_hbm, fresh_hbm, sems):
    copies = [pltpu.make_async_copy(coeff, coeff_hbm, sems.at[0])]
    for source, place in ((fresh, fresh_hbm), (shrunk, shrunk_hbm)):
        share = source.shape[0] // 4
        for i in range(4):
            part = pl.ds(i * share, share)
            copies.append(
                pltpu.make_async_copy(source.at[part], place.at[part], sems.at[len(copies)])
            )
    for copy in copies:
        copy.start()
    for copy in copies:
        copy.wait()


def whole_kernel(video, multiplier, foreground, basis, coefficients):
    F, H, W = video.shape
    rank = basis.shape[0]
    nr, nc, nz = (lax.axis_size(name) for name in ("row", "col", "frame"))
    f32 = jnp.float32
    own = H // nz
    group = nr * nc
    vmem = pltpu.VMEM
    dma = pltpu.SemaphoreType.DMA
    pieces = own // CHUNK
    hbm = pl.BlockSpec(memory_space=pl.ANY)
    on_chip = pl.BlockSpec(memory_space=pltpu.VMEM)
    found = pl.pallas_call(
        functools.partial(kernel, (F, H, W, rank, nr, nc, nz)),
        out_shape=(vmem((F, H, W), f32), vmem((F, rank), f32), vmem((rank, own, W), f32)),
        in_specs=[hbm] * 5,
        out_specs=[on_chip] * 3,
        scratch_shapes=[vmem((F + 2, H + 16, W), f32)] * PASSES
        + [
            vmem((F, H, W), f32),
            vmem((F, H, W), f32),
            vmem((rank, H, W), f32),
            vmem((F, H, W), f32),
            vmem((F, H, W), f32),
            vmem((F * nz, own, W), f32),
            vmem((PASSES, SEGMENTS, 16, H // SEGMENTS), f32),
            vmem((PASSES, SEGMENTS, 16, H // SEGMENTS), f32),
            vmem((PASSES, 2, F, 8, 128), f32),
            vmem((H + 8, 128), f32),
            vmem((H + 16, 128), f32),
            vmem((H + 16, 128), f32),
            vmem((H + 24, 128), f32),
            vmem((H + 24, 128), f32),
            vmem((8, 128), f32),
            vmem((F, rank, 8, 128), f32),
            vmem((rank + F, rank, 128), f32),
            vmem((nz, 8, 128), f32),
            vmem((group, 8, 128), f32),
            vmem((rank, rank, 128), f32),
            vmem((group, rank, 128), f32),
            vmem((nz * F, 128), f32),
            vmem((128, 128), f32),
            vmem((rank, 128), f32),
            pltpu.SMEM((F, rank), f32),
            pltpu.SMEM((rank, 128), f32),
            dma((9,)),
            dma((2, 9)),
            dma((2, 3 + 2 * SEGMENTS + H // CHUNK)),
            dma((1,)),
            dma((1,)),
            dma((1,)),
            dma((1,)),
            dma((1,)),
            dma((1,)),
            dma((1,)),
            dma((1,)),
            dma((nz,)),
            dma((nz, pieces)),
            dma((1,)),
        ],
        compiler_params=pltpu.CompilerParams(
            collective_id=0, has_side_effects=True, vmem_limit_bytes=32 * 1024 * 1024
        ),
    )(
        *(
            pltpu.with_memory_space_constraint(x, pltpu.HBM)
            for x in (coefficients, video, multiplier, foreground, basis)
        )
    )
    return pl.pallas_call(
        deliver,
        out_shape=(
            jax.ShapeDtypeStruct((F, H, W), f32),
            jax.ShapeDtypeStruct((F, rank), f32),
            jax.ShapeDtypeStruct((rank, own, W), f32),
        ),
        in_specs=[on_chip] * 3,
        out_specs=[hbm] * 3,
        scratch_shapes=[dma((9,))],
    )(*(pltpu.with_memory_space_constraint(x, pltpu.VMEM) for x in found))


def body(video, multiplier, foreground, basis, coefficients):
    F, H, W = video.shape
    rank = basis.shape[0]
    nz = lax.axis_size("frame")
    fits = (
        H % nz == 0 and (H // nz) % 8 == 0 and (H // nz) % CHUNK == 0 and W % 128 == 0
        and H % 16 == 0 and H % (SEGMENTS * CHUNK) == 0 and lax.axis_size("row") <= 2
        and F % 4 == 0 and F < 8 and rank == 16 and nz >= 2 and F * nz == rank and 2 * rank + F * nz <= 128
    )
    run = whole_kernel if fits else local
    return run(video, multiplier, foreground, basis, coefficients)


def solution(mesh):
    placed = (
        P("frame", "row", "col"),
        P("frame", "row", "col"),
        P("frame", "row", "col"),
        P(None, "row", "col"),
        P("frame", None),
    )
    return jax.shard_map(
        body,
        mesh=mesh,
        in_specs=placed,
        out_specs=(P("frame", "row", "col"), P("frame", None), P(None, ("row", "frame"), "col")),
        check_vma=False,
    )
```

```python
import functools

import jax
import jax.numpy as jnp
from jax import lax
from jax.experimental import pallas as pl
from jax.experimental.pallas import tpu as pltpu
from jax.sharding import PartitionSpec as P

PASSES = 3


relax_rate = 0.8
smooth_weight = 0.5
smooth_floor = 0.25
shrink_level = 0.4
dual_scale = 0.8
ridge_share = 0.1


def with_halo(block, sides, width):
    for axis, dim in sides:
        count = lax.axis_size(axis)
        forward = [(i, i + 1) for i in range(count - 1)]
        backward = [(target, source) for source, target in forward]
        low = lax.ppermute(
            lax.slice_in_dim(block, block.shape[dim] - width, None, axis=dim), axis, forward
        )
        high = lax.ppermute(lax.slice_in_dim(block, 0, width, axis=dim), axis, backward)
        block = jnp.concatenate([low, block, high], axis=dim)
    return block


def forward_cells(padded, direction, shape):
    starts = [0, 0, 0]
    starts[direction] = 1
    limits = [starts[axis_dim] + shape[axis_dim] for axis_dim in range(3)]
    return lax.slice(padded, starts, limits)


def descend(padded, source, anchor, extent):
    shape = tuple((int(length) - 1 for length in padded.shape))
    here_cells = padded[:-1, :-1, :-1]
    slopes = []
    for direction in range(3):
        ahead_cells = forward_cells(padded, direction, shape)
        places = anchor[direction] + jnp.arange(shape[direction], dtype=jnp.int32)
        inside = (places >= 0) & (places < extent[direction] - 1)
        layout = [1, 1, 1]
        layout[direction] = shape[direction]
        inside = inside.reshape(layout)
        slopes.append(jnp.where(inside, ahead_cells - here_cells, jnp.zeros_like(here_cells)))
    weight = lax.rsqrt(
        smooth_floor + slopes[0] * slopes[0] + slopes[1] * slopes[1] + slopes[2] * slopes[2]
    )
    fluxes = [slope_part * weight for slope_part in slopes]
    spread = (
        fluxes[0][1:, 1:, 1:]
        - fluxes[0][:-1, 1:, 1:]
        + (fluxes[1][1:, 1:, 1:] - fluxes[1][1:, :-1, 1:])
        + (fluxes[2][1:, 1:, 1:] - fluxes[2][1:, 1:, :-1])
    )
    center = padded[1:-1, 1:-1, 1:-1]
    return center + relax_rate * (source - center + smooth_weight * spread)


def solve_definite(matrix, right_side):
    factor_lower = jnp.linalg.cholesky(matrix)
    half_solved = lax.linalg.triangular_solve(factor_lower, right_side, left_side=True, lower=True)
    return lax.linalg.triangular_solve(
        factor_lower, half_solved, left_side=True, lower=True, transpose_a=True
    )


def local(video, multiplier, foreground, basis, coefficients):
    highest = lax.Precision.HIGHEST
    frames_here, rows_here, cols_here = video.shape
    rank_size = basis.shape[0]
    frame_count = lax.axis_size("frame")
    row_count = lax.axis_size("row")
    col_count = lax.axis_size("col")
    extent = (frames_here * frame_count, rows_here * row_count, cols_here * col_count)
    frame_slot = lax.axis_index("frame")
    corner = (
        frame_slot * frames_here,
        lax.axis_index("row") * rows_here,
        lax.axis_index("col") * cols_here,
    )
    pixels = rows_here * cols_here
    flat_basis = basis.reshape(rank_size, pixels)
    background = jnp.dot(coefficients, flat_basis, precision=highest).reshape(video.shape)
    target = video - background + dual_scale * multiplier
    current = foreground
    for sweep in range(PASSES):
        padded = with_halo(current, (("row", 1), ("col", 2), ("frame", 0)), 1)
        current = descend(padded, target, tuple((start_cell - 1 for start_cell in corner)), extent)
    shrunk = current - jnp.clip(current, -shrink_level, shrink_level)
    residual_target = video + dual_scale * multiplier - shrunk
    flat_target = residual_target.reshape(frames_here, pixels)
    gram_part = jnp.dot(flat_basis, flat_basis.T, precision=highest)
    cross_part = jnp.dot(flat_basis, flat_target.T, precision=highest)
    gram_sum, cross_sum = lax.psum((gram_part, cross_part), ("row", "col"))
    identity_matrix = jnp.eye(rank_size, dtype=gram_sum.dtype)
    pixel_ridge = ridge_share * pixels * row_count * col_count
    coeff_rows = solve_definite(
        gram_sum + pixel_ridge * identity_matrix, cross_sum + pixel_ridge * coefficients.T
    )
    total_part = jnp.dot(coeff_rows, flat_target, precision=highest).reshape(
        rank_size, rows_here, cols_here
    )
    frame_gram_part = jnp.dot(coeff_rows, coeff_rows.T, precision=highest)
    owned_rows = rows_here // frame_count
    owned_sums = lax.psum_scatter(total_part, "frame", scatter_dimension=1, tiled=True)
    frame_gram = lax.psum(frame_gram_part, "frame")
    old_owned = lax.dynamic_slice_in_dim(basis, frame_slot * owned_rows, owned_rows, 1)
    frame_ridge = ridge_share * frames_here * frame_count
    right_side = (owned_sums + frame_ridge * old_owned).reshape(rank_size, owned_rows * cols_here)
    new_basis = solve_definite(frame_gram + frame_ridge * identity_matrix, right_side)
    return (shrunk, coeff_rows.T, new_basis.reshape(rank_size, owned_rows, cols_here))


MESH = pl.DeviceIdType.MESH
CHUNK = 24
SEGMENTS = 4


def eliminate(matrix, size):
    lanes = lax.broadcasted_iota(jnp.int32, matrix.shape, 1)
    rows = lax.broadcasted_iota(jnp.int32, matrix.shape, 0)
    for k in range(size):
        pivot = matrix[k : k + 1, k : k + 1]
        scaled = matrix[k : k + 1, :] / pivot
        column = jnp.sum(jnp.where(lanes == k, matrix, 0.0), axis=1, keepdims=True)
        matrix = jnp.where(rows == k, scaled, matrix - column * scaled)
    return matrix


def kernel(
    sizes, coeff_hbm, video_hbm, mult_hbm, fore_hbm, basis_hbm,
    result, coeff_out, fresh,
    field0, field1, field2, video, mult, basis, anchor, target, owned,
    packed, arrived, corner, edge_next, edge_flux, first_cols, left_now, left_next, bottom_row,
    cross, sums, grams, gram_parts, inverse, parts, shares, square, table, coeff_ref, table_smem,
    move_send, move_recv,
):
    field = (field0, field1, field2)
    F, H, W, rank, nr, nc, nz = sizes
    r = lax.axis_index("row")
    c = lax.axis_index("col")
    z = lax.axis_index("frame")
    own = H // nz
    pieces = own // CHUNK
    half = H // 2
    flip = lax.rem(r, 2)

    steps = H // CHUNK

    def chunk_at(step):
        return step + flip * (steps - 1 - 2 * step)

    def rows_at(step, offset=0):
        return pl.ds(pl.multiple_of(offset + chunk_at(step) * CHUNK, 8), CHUNK)

    span = H // SEGMENTS
    per = steps // SEGMENTS

    def segment_start(j):
        return pl.multiple_of((j + flip * (SEGMENTS - 1 - 2 * j)) * span, 8)

    def half_start(h):
        return pl.multiple_of((h + flip * (1 - 2 * h)) * half, 8)

    inner = (z > 0) & (z < nz - 1)

    def inside(dr, dc, dz):
        ok = None
        for at, step, count in ((r, dr, nr), (c, dc, nc), (z, dz, nz)):
            if step != 0:
                test = (at + step >= 0) & (at + step < count)
                ok = test if ok is None else ok & test
        return ok

    def take(source, piece):
        rows = pl.ds(pl.multiple_of(z * own + piece * CHUNK, 8), CHUNK)
        spot = pl.ds(pl.multiple_of(piece * CHUNK, 8), CHUNK)
        return pltpu.make_async_remote_copy(
            src_ref=anchor.at[:, rows, :], dst_ref=owned.at[pl.ds(source * F, F), spot, :],
            send_sem=move_send.at[source], recv_sem=move_recv.at[source, piece],
            device_id=(r, c, source), device_id_type=MESH,
        )

    def work(
        in_sems, halo_send, halo_recv, part_send, part_recv, gram_send, gram_recv,
        total_send, total_recv, share_send, share_recv, small_sem,
    ):
        halves = [pl.ds(half_start(h), half) for h in range(2)]
        loads = [
            pltpu.make_async_copy(src, dst, in_sems.at[i])
            for i, (src, dst) in enumerate(
                [
                    (
                        fore_hbm.at[:, halves[h], :],
                        field0.at[1 : F + 1, pl.ds(pl.multiple_of(half_start(h) + 8, 8), half), :],
                    )
                    for h in range(2)
                ]
                + [(coeff_hbm, coeff_ref)]
                + [
                    (src.at[:, rows, :], dst.at[:, rows, :])
                    for rows in halves
                    for src, dst in ((video_hbm, video), (mult_hbm, mult), (basis_hbm, basis))
                ]
            )
        ]
        for load in loads[:2]:
            load.start()

        barrier = pltpu.get_barrier_semaphore()
        beside = ((0, 0, 1), (0, 1, 0), (1, 0, 0), (1, 0, -1), (0, 1, -1), (1, -1, 0))
        beside += tuple(tuple(-s for s in step) for step in beside)
        for step in beside:
            @pl.when(inside(*step))
            def _(step=step):
                pl.semaphore_signal(
                    barrier,
                    inc=1,
                    device_id=(r + step[0], c + step[1], z + step[2]),
                    device_id_type=MESH,
                )
        expected = jnp.int32(0)
        for step in beside:
            expected = expected + inside(*step).astype(jnp.int32)
        for load in loads[2:]:
            load.start()

        pl.semaphore_wait(barrier, expected)

        lane_h = lax.broadcasted_iota(jnp.int32, (span, 128), 1)

        def pack_columns(k, j):
            base = segment_start(j)
            tile = jnp.zeros((span, 128), jnp.float32)
            for f in range(F):
                for lane, at in ((f, 0), (8 + f, W - 1)):
                    lanes = field[k][f + 1, pl.ds(base + 8, span), (at // 128) * 128 : (at // 128) * 128 + 128]
                    tile = jnp.where(lane_h == lane, lanes[:, at % 128 : at % 128 + 1], tile)
            first_cols[pl.ds(base + 8, span), :] = tile
            packed[k, j] = tile.T[:16, :]

        strips = range(4)
        corners = (4, 5)

        def column_list(k, j):
            return (
                (packed.at[k, j, 0:F], arrived.at[k, j, 1 : F + 1], (0, -1, 0)),
                (packed.at[k, j, 8 : 8 + F], arrived.at[k, j, 8 : 8 + F], (0, 1, 0)),
                (packed.at[k, j, F - 1 : F], arrived.at[k, j, 0:1], (0, -1, 1)),
                (packed.at[k, j, 8:9], arrived.at[k, j, 8 + F : 9 + F], (0, 1, -1)),
            )

        def halo_list(k):
            fk = field[k]
            mid = slice(1, F + 1)
            return (
                (fk.at[mid, H : H + 8, :], fk.at[mid, 0:8, :], (1, 0, 0)),
                (fk.at[mid, 8:16, :], fk.at[mid, H + 8 : H + 16, :], (-1, 0, 0)),
                (fk.at[F, 8:9, :], fk.at[0, H + 8 : H + 9, :], (-1, 0, 1)),
                (fk.at[1, H + 7 : H + 8, :], fk.at[F + 1, 7:8, :], (1, 0, -1)),
                (fk.at[mid, H : H + 8, 0:128], corner.at[k, 0], (1, -1, 0)),
                (fk.at[mid, 8:16, W - 128 : W], corner.at[k, 1], (-1, 1, 0)),
            )

        def halo_copy(k, i, leave, src, dst, step):
            return pltpu.make_async_remote_copy(
                src_ref=src, dst_ref=dst,
                send_sem=halo_send.at[k % 2, leave], recv_sem=halo_recv.at[k % 2, i],
                device_id=(r + step[0], c + step[1], z + step[2]), device_id_type=MESH,
            )

        def send_columns(k, j):
            for i, (src, dst, step) in enumerate(column_list(k, j)):
                @pl.when(inside(*step))
                def _(i=i, src=src, dst=dst, step=step):
                    halo_copy(k, 3 + 2 * j + i % 2, 3 + i, src, dst, step).start()

        def wait_columns(k, j):
            for side, step, corner_step, small, large in (
                (0, (0, -1, 0), (0, -1, 1), slice(1, F + 1), slice(0, F + 1)),
                (1, (0, 1, 0), (0, 1, -1), slice(8, 8 + F), slice(8, 9 + F)),
            ):
                near = inside(*(-s for s in step))
                both = inside(*(-s for s in corner_step))
                for turn, rows in ((near & ~both, small), (both, large)):
                    @pl.when(turn)
                    def _(side=side, step=step, rows=rows):
                        ref = arrived.at[k, j, rows]
                        halo_copy(k, 3 + 2 * j + side, 0, ref, ref, step).wait_recv()

        def face(k, step, up):
            fk = field[k]
            rows = rows_at(step, 8)
            at = 3 + 2 * SEGMENTS + step
            mine, theirs = (F, 0) if up else (1, F + 1)
            src = fore_hbm.at[mine - 1, rows_at(step)] if k == 0 else fk.at[mine, rows]
            return halo_copy(
                k, at, 7 if up else 8, src, fk.at[theirs, rows], (0, 0, 1 if up else -1)
            )

        def send_faces(k, low, high):
            @pl.loop(low, high)
            def _(step):
                for up in (True, False):
                    @pl.when(inside(0, 0, 1 if up else -1))
                    def _(up=up):
                        face(k, step, up).start()

        def wait_face(k, step):
            for turn, frames in ((inner, slice(0, 2)), (~inner, slice(0, 1))):
                @pl.when(turn)
                def _(frames=frames):
                    ref = field[k].at[frames, rows_at(step, 8), :]
                    halo_copy(k, 3 + 2 * SEGMENTS + step, 0, ref, ref, (0, 0, 1)).wait_recv()

        def send_halos(k, which):
            every = halo_list(k)
            for i in which:
                src, dst, step = every[i]

                @pl.when(inside(*step))
                def _(i=i, src=src, dst=dst, step=step):
                    halo_copy(k, i // 2, i // 2, src, dst, step).start()

        def wait_halos(k, which):
            every = halo_list(k)
            for i in which:
                src, dst, step = every[i]

                @pl.when(inside(*(-s for s in step)))
                def _(i=i, src=src, dst=dst, step=step):
                    halo_copy(k, i // 2, i // 2, src, dst, step).wait_recv()

        def finish_sends(k):
            for i, (src, dst, step) in enumerate(halo_list(k)):
                @pl.when(inside(*step))
                def _(i=i, src=src, dst=dst, step=step):
                    halo_copy(k, i // 2, i // 2, src, dst, step).wait_send()

            every = (
                (packed.at[k, :, 0:F], arrived.at[k, :, 1 : F + 1], (0, -1, 0)),
                (packed.at[k, :, 8 : 8 + F], arrived.at[k, :, 8 : 8 + F], (0, 1, 0)),
                (packed.at[k, :, F - 1 : F], arrived.at[k, :, 0:1], (0, -1, 1)),
                (packed.at[k, :, 8:9], arrived.at[k, :, 8 + F : 9 + F], (0, 1, -1)),
                (field[k].at[F, 8 : H + 8, :], field[k].at[0, 8 : H + 8, :], (0, 0, 1)),
                (field[k].at[1, 8 : H + 8, :], field[k].at[F + 1, 8 : H + 8, :], (0, 0, -1)),
            )
            for i, (src, dst, step) in enumerate(every):
                @pl.when(inside(*step))
                def _(i=i, src=src, dst=dst, step=step):
                    halo_copy(k, 0, 3 + i, src, dst, step).wait_send()

        def prepare_columns(k, j):
            base = segment_start(j)
            spread = jnp.concatenate(
                [arrived[k, j], jnp.zeros((112, span), jnp.float32)], axis=0
            ).T
            edge_next[pl.ds(base + 8, span), :] = spread
            left_now[pl.ds(base + 8, span), :] = pltpu.roll(spread, 120, 1)
            left_next[pl.ds(base + 8, span), :] = pltpu.roll(spread, 119, 1)
            low, count = pl.multiple_of(base + 8 * flip, 8), span + 8
            here = left_now[pl.ds(low, count), :]
            ahead = left_next[pl.ds(low, count), :]
            lane = lax.broadcasted_iota(jnp.int32, (count, 128), 1)
            row = lax.broadcasted_iota(jnp.int32, (count, 128), 0) + (low - 8)
            slope0 = jnp.where((lane == F - 1) & (z == nz - 1), 0.0, ahead - here)
            after = left_now[pl.ds(low, count + 8), :]
            below = jnp.where(
                row == H - 1, bottom_row[0:1, :], pltpu.roll(after, count + 7, 0)[:count]
            )
            slope1 = jnp.where((row == H - 1) & (r == nr - 1), 0.0, below - here)
            slope2 = first_cols[pl.ds(low, count), :] - here
            weight = lax.rsqrt(smooth_floor + slope0 * slope0 + slope1 * slope1 + slope2 * slope2)
            edge_flux[pl.ds(low, count), :] = jnp.where(c == 0, 0.0, slope2 * weight)

        def take_corners(k):
            wait_halos(k, corners)
            lane8 = lax.broadcasted_iota(jnp.int32, (8, 128), 1)
            top = jnp.zeros((8, 128), jnp.float32)
            bottom = jnp.zeros((8, 128), jnp.float32)
            for f in range(F):
                top = jnp.where(lane8 == f + 1, corner[k, 0, f][:, 0:1], top)
                bottom = jnp.where(lane8 == f, corner[k, 1, f][:, 127:128], bottom)
            edge_next[0:8, :] = top
            bottom_row[...] = bottom

        def sweep(k, last, start):
            R = CHUNK
            tiles = W // 128
            row_8 = lax.broadcasted_iota(jnp.int32, (8, 128), 0) + (r * H + start)
            above_image = row_8 - 8 < 0
            last_image_row = row_8 + (R - 8) >= nr * H - 1
            columns = edge_next[pl.ds(start, R + 8), :]
            fluxes_in = edge_flux[pl.ds(start + 8, R), :]
            at = pl.ds(start, R)

            def frame(f):
                return [
                    field[k][f, pl.ds(start, R + 16), w * 128 : w * 128 + 128] for w in range(tiles)
                ]

            now = frame(0)
            flux0_before = None
            for f in range(-1, F):
                after = frame(f + 2)
                skip = 8 if f < 0 else 0
                n = R + 8 - skip
                lane = lax.broadcasted_iota(jnp.int32, (n, 128), 1)
                here = [t[skip : R + 8] for t in now]
                turned = [pltpu.roll(t, 127, 1) for t in here]
                wall = jnp.broadcast_to(columns[skip:, f + 1 : f + 2], (n, 128))
                flux0, flux1, flux2 = [], [], []
                for w in range(tiles):
                    slope0 = after[w][skip : R + 8] - here[w]
                    if f == F - 1:
                        slope0 = jnp.where(z == nz - 1, 0.0, slope0)
                    slope1 = pltpu.roll(now[w][skip:], n + 7, 0)[:n] - here[w]
                    slope1 = jnp.concatenate(
                        [slope1[: n - 8], jnp.where(last_image_row, 0.0, slope1[n - 8 :])], axis=0
                    )
                    beyond = turned[w + 1] if w + 1 < tiles else wall
                    slope2 = jnp.where(lane == 127, beyond, turned[w]) - here[w]
                    if w + 1 == tiles:
                        slope2 = jnp.where((lane == 127) & (c == nc - 1), 0.0, slope2)
                    weight = lax.rsqrt(
                        smooth_floor + slope0 * slope0 + slope1 * slope1 + slope2 * slope2
                    )
                    flux0.append((slope0 * weight)[8 - skip :])
                    if f >= 0:
                        flux = slope1 * weight
                        flux1.append(
                            jnp.concatenate(
                                [jnp.where(above_image, 0.0, flux[:8]), flux[8:]], axis=0
                            )
                        )
                        flux2.append((slope2 * weight)[8:])
                if f < 0:
                    flux0 = [jnp.where(z == 0, 0.0, t) for t in flux0]
                else:
                    moved = [pltpu.roll(t, 1, 1) for t in flux2]
                    entry = jnp.broadcast_to(fluxes_in[:, f : f + 1], (R, 128))
                    lane = lax.broadcasted_iota(jnp.int32, (R, 128), 1)
                    for w in range(tiles):
                        left = jnp.where(lane == 0, moved[w - 1] if w > 0 else entry, moved[w])
                        above = pltpu.roll(flux1[w], 1, 0)[8:]
                        spread = (flux0[w] - flux0_before[w]) + (flux1[w][8:] - above) + (flux2[w] - left)
                        lanes = slice(w * 128, w * 128 + 128)
                        value = (1.0 - relax_rate) * here[w][8:] + (
                            target[f, at, lanes] + (relax_rate * smooth_weight) * spread
                        )
                        if last:
                            shrunk = value - jnp.clip(value, -shrink_level, shrink_level)
                            result[f, at, lanes] = shrunk
                            anchor[f, at, lanes] = anchor[f, at, lanes] - shrunk
                        else:
                            field[k + 1][f + 1, pl.ds(start + 8, R), lanes] = value
                flux0_before = flux0
                now = after

        def products(left_of, right_of, lefts, rights, first, count, start, store):
            def body(step, totals):
                rows = pl.ds(pl.multiple_of(first + step * 8, 8), 8)
                a = [left_of[i, rows, :] for i in lefts]
                b = [right_of[j, rows, :] for j in rights]
                out = []
                for x in range(len(lefts)):
                    for y in range(len(rights)):
                        prod = a[x] * b[y]
                        total = totals[len(out)]
                        for w in range(W // 128):
                            total = total + prod[:, w * 128 : w * 128 + 128]
                        out.append(total)
                return tuple(out)

            totals = lax.fori_loop(
                0, count // 8, body, tuple(start(i, j) for i in lefts for j in rights), unroll=3 if count % 24 == 0 else 1
            )
            n = 0
            for i in lefts:
                for j in rights:
                    store(i, j, totals[n])
                    n += 1

        def held(block):
            return (block - z >= 2) | (z - block >= 2)

        def move(block, piece):
            rows = pl.ds(pl.multiple_of(block * own + piece * CHUNK, 8), CHUNK)
            spot = pl.ds(pl.multiple_of(piece * CHUNK, 8), CHUNK)
            return pltpu.make_async_remote_copy(
                src_ref=anchor.at[:, rows, :], dst_ref=owned.at[pl.ds(z * F, F), spot, :],
                send_sem=move_send.at[block], recv_sem=move_recv.at[z, piece],
                device_id=(r, c, block), device_id_type=MESH,
            )

        send_faces(0, 0, 1)
        for j in range(SEGMENTS):
            if j % (SEGMENTS // 2) == 0:
                loads[j // (SEGMENTS // 2)].wait()
            pack_columns(0, j)
            send_columns(0, j)
            if j == SEGMENTS // 2:
                send_halos(0, strips)
                send_halos(0, corners)
            send_faces(0, max(1, j * per), (j + 1) * per)

        zero_tile = jnp.zeros((8, 128), jnp.float32)

        def store_gram(i, j, value):
            row = jnp.sum(value, axis=0, keepdims=True)
            sums[j, i : i + 1, :] = row
            if i // 4 != j // 4:
                sums[i, j : j + 1, :] = row

        lane_r = lax.broadcasted_iota(jnp.int32, (rank, 128), 1)
        row_r = lax.broadcasted_iota(jnp.int32, (rank, 128), 0)

        def gram_share():
            for i in range(0, rank, 4):
                for j in range(i, rank, 4):
                    products(
                        basis, basis, range(i, i + 4), range(j, j + 4), z * own, own,
                        lambda i, j: zero_tile, store_gram,
                    )
            tile = jnp.zeros((rank, 128), jnp.float32)
            for q in range(rank):
                tile = jnp.where(lane_r == q, jnp.sum(sums[q], axis=1, keepdims=True), tile)
            lane = lax.broadcasted_iota(jnp.int32, (8, 128), 1)
            tile = jnp.where(lane < rank, tile[:8], pltpu.roll(tile[8:], rank, 1))
            tile = jnp.where(lane < 2 * rank, tile, pltpu.roll(pltpu.roll(tile, 4, 0), 2 * rank, 1))
            tile = jnp.where(lane < 4 * rank, tile, pltpu.roll(pltpu.roll(tile, 6, 0), 4 * rank, 1))
            grams[z] = tile

        def unfold(tile):
            row = lax.broadcasted_iota(jnp.int32, (8, 128), 0)
            tile = jnp.where(row < 2, tile, pltpu.roll(pltpu.roll(tile, 2, 0), 128 - 4 * rank, 1))
            tile = jnp.where(row < 4, tile, pltpu.roll(pltpu.roll(tile, 4, 0), 128 - 2 * rank, 1))
            tile = jnp.concatenate([tile, pltpu.roll(tile, 128 - rank, 1)], axis=0)
            return jnp.where(lane_r < rank, tile, 0.0)

        def all_sent(block, sem):
            return pltpu.make_async_remote_copy(
                src_ref=block, dst_ref=block, send_sem=sem.at[0], recv_sem=sem.at[0],
                device_id=(r, c, lax.rem(z + 1, nz)), device_id_type=MESH,
            )

        def all_here(block, sem):
            return pltpu.make_async_remote_copy(
                src_ref=block, dst_ref=block, send_sem=sem.at[0], recv_sem=sem.at[0],
                device_id=(r, c, lax.rem(z + 1, nz)), device_id_type=MESH,
            )

        def share_gram(d):
            return pltpu.make_async_remote_copy(
                src_ref=grams.at[z, 0:2], dst_ref=grams.at[z, 0:2],
                send_sem=gram_send.at[0], recv_sem=gram_recv.at[0],
                device_id=(r, c, lax.rem(z + d, nz)), device_id_type=MESH,
            )

        group = nr * nc
        me = r * nc + c

        def share_total(d):
            other = lax.rem(me + d, group)
            return pltpu.make_async_remote_copy(
                src_ref=gram_parts.at[me, 0:2], dst_ref=gram_parts.at[me, 0:2],
                send_sem=total_send.at[0], recv_sem=total_recv.at[0],
                device_id=(other // nc, lax.rem(other, nc), z), device_id_type=MESH,
            )

        def store_cross(i, j, value):
            cross[j, i] = value

        def find_target(h):
            for load in loads[3 + 3 * h : 6 + 3 * h]:
                load.wait()

            @pl.loop(0, half // 8)
            def _(step):
                rows = pl.ds(pl.multiple_of(half_start(h) + step * 8, 8), 8)
                totals = [None] * F
                for q in range(rank):
                    plane = basis[q, rows, :]
                    for f in range(F):
                        term = coeff_ref[f, q] * plane
                        totals[f] = term if totals[f] is None else totals[f] + term
                for f in range(F):
                    lifted = dual_scale * mult[f, rows, :]
                    anchor[f, rows, :] = video[f, rows, :] + lifted
                    target[f, rows, :] = relax_rate * (video[f, rows, :] - totals[f] + lifted)

        loads[2].wait()
        find_target(0)
        find_target(1)
        gram_share()

        def advance(k, step):
            start = pl.multiple_of(chunk_at(step) * CHUNK, 8)
            sweep(k, k == PASSES - 1, start)
            if k == PASSES - 1:
                place, piece = chunk_at(step) // pieces, lax.rem(chunk_at(step), pieces)

                @pl.when((place - z == 1) | (z - place == 1))
                def _():
                    move(place, piece).start()

                for i in range(0, rank, 4):
                    products(
                        basis, anchor, range(i, i + 4), range(F), start, CHUNK,
                        lambda i, j: cross[j, i], store_cross,
                    )

        cross[...] = jnp.zeros_like(cross)
        bottom_row[...] = jnp.zeros_like(bottom_row)
        for k in range(PASSES):
            last = k == PASSES - 1
            if k > 0 and not last:
                finish_sends(k - 1)
            wait_columns(k, 0)
            prepare_columns(k, 0)
            wait_face(k, 0)

            @pl.loop(0, SEGMENTS)
            def _(j, k=k, last=last):
                @pl.loop(j * per, (j + 1) * per - 1)
                def _(step):
                    wait_face(k, step + 1)
                    advance(k, step)

                final = j == SEGMENTS - 1
                if k == PASSES - 2:
                    @pl.when(j == 1)
                    def _():
                        for d in range(1, nz):
                            share_gram(d).start()
                if k == PASSES - 1:
                    @pl.when(j == 1)
                    def _():
                        all_here(grams.at[0 : nz - 1, 0:2], gram_recv).wait_recv()
                        total = grams[0]
                        for i in range(1, nz):
                            total = total + grams[i]
                        gram_parts[me] = total
                        for d in range(1, group):
                            share_total(d).start()

                @pl.when(j == SEGMENTS - 2)
                def _():
                    take_corners(k)

                @pl.when(~final)
                def _():
                    wait_columns(k, j + 1)
                    prepare_columns(k, j + 1)
                    wait_face(k, (j + 1) * per)

                @pl.when(final)
                def _():
                    wait_halos(k, strips)

                advance(k, (j + 1) * per - 1)
                if not last:
                    @pl.when(final)
                    def _():
                        send_halos(k + 1, strips)
                        send_halos(k + 1, corners)

                    pack_columns(k + 1, j)
                    send_columns(k + 1, j)
                    send_faces(k + 1, j * per, (j + 1) * per)


        def send_held(turn, low, high):
            for b in range(nz):
                @pl.when(held(b) & turn)
                def _(b=b):
                    for p in range(low, high):
                        move(b, p).start()

        for far, near in ((nz - 1, 0), (0, nz - 1)):
            place = far - 1 if far > near else far + 1

            @pl.when((z == near) & held(jnp.int32(place)))
            def _(place=place):
                move(place, 0).start()

        for j in range(F):
            for i in range(rank):
                sums[rank + j, i : i + 1, :] = jnp.sum(cross[j, i], axis=0, keepdims=True)

        part = jnp.zeros((rank, 128), jnp.float32)
        for q in range(rank, rank + F):
            part = jnp.where(lane_r == q, jnp.sum(sums[q], axis=1, keepdims=True), part)
        parts[me] = part

        def share_part(d):
            other = lax.rem(me + d, group)
            return pltpu.make_async_remote_copy(
                src_ref=parts.at[me], dst_ref=parts.at[me],
                send_sem=part_send.at[0], recv_sem=part_recv.at[0],
                device_id=(other // nc, lax.rem(other, nc), z), device_id_type=MESH,
            )

        for d in range(1, group):
            share_part(d).start()
        pixel_ridge = ridge_share * H * W * group
        diagonal = lane_r == row_r
        before = jnp.zeros((rank, 128), jnp.float32)
        for q in range(rank):
            for f in range(F):
                before = jnp.where((row_r == q) & (lane_r == rank + f), coeff_ref[f, q], before)
        all_here(gram_parts.at[0 : group - 1, 0:2], total_recv).wait_recv()
        total = gram_parts[0]
        for i in range(1, group):
            total = total + gram_parts[i]
        diagonal = lane_r == row_r
        system = unfold(total) + jnp.where(
            diagonal, pixel_ridge, jnp.where(lane_r == row_r + rank, 1.0, 0.0)
        )
        system = eliminate(system, rank)
        for q in range(rank):
            inverse[q] = jnp.broadcast_to(system[:, rank + q : rank + q + 1], (rank, 128))
        all_here(parts.at[0 : group - 1], part_recv).wait_recv()
        total = parts[0]
        for i in range(1, group):
            total = total + parts[i]
        total = total + pixel_ridge * before
        solved = inverse[0] * total[0:1, :]
        for q in range(1, rank):
            solved = solved + inverse[q] * total[q : q + 1, :]
        square[...] = jnp.zeros_like(square)
        square[0:rank, :] = solved
        mine = square[...].T[rank : rank + F, :]
        shares[pl.ds(z * F, F), :] = mine

        def share_rows(d):
            return pltpu.make_async_remote_copy(
                src_ref=shares.at[pl.ds(z * F, F)], dst_ref=shares.at[pl.ds(z * F, F)],
                send_sem=share_send.at[0], recv_sem=share_recv.at[0],
                device_id=(r, c, lax.rem(z + d, nz)), device_id_type=MESH,
            )

        for d in range(1, nz):
            share_rows(d).start()

        send_held(inner, 0, pieces)
        coeff_out[...] = mine[:, 0:rank]
        all_here(shares.at[0 : (nz - 1) * F], share_recv).wait_recv()
        for b in range(nz):
            @pl.when(held(b) & ~inner)
            def _(b=b):
                first = jnp.where(((z == 0) & (b == nz - 2)) | ((z == nz - 1) & (b == 1)), 1, 0)

                @pl.loop(first, pieces)
                def _(p):
                    move(b, p).start()

        frames = F * nz
        square[0:frames, :] = shares[...]
        wide = pltpu.roll(square[...].T[0:rank, :], rank, 1)
        square[0:rank, :] = wide
        gram = lax.dot_general(
            wide, square[...], (((1,), (1,)), ((), ())),
            precision=lax.Precision.HIGHEST, preferred_element_type=jnp.float32,
        )
        frame_ridge = ridge_share * frames
        system = jnp.where(diagonal, gram + frame_ridge, gram) + wide
        system = system + jnp.where(lane_r == row_r + rank + frames, frame_ridge, 0.0)
        table[...] = eliminate(system, rank)
        to_scalar = pltpu.make_async_copy(table, table_smem, small_sem.at[0])
        to_scalar.start()
        to_scalar.wait()
        my_base = z * own

        @pl.loop(0, own // 8)
        def _(step):
            rows = pl.ds(pl.multiple_of(step * 8, 8), 8)
            old = pl.ds(pl.multiple_of(my_base + step * 8, 8), 8)
            for half in range(0, rank, 8):
                totals = [None] * 8
                for f in range(F + rank):
                    plane = anchor[f, old, :] if f < F else basis[f - F, old, :]
                    place = rank + z * F + f if f < F else rank + frames + f - F
                    for q in range(8):
                        term = table_smem[half + q, place] * plane
                        totals[q] = term if totals[q] is None else totals[q] + term
                for q in range(8):
                    fresh[half + q, rows, :] = totals[q]

        for k in range(PASSES - 2, PASSES):
            finish_sends(k)
        all_sent(shares.at[0 : (nz - 1) * F], share_send).wait_send()
        all_sent(grams.at[0 : nz - 1, 0:2], gram_send).wait_send()
        all_sent(gram_parts.at[0 : group - 1, 0:2], total_send).wait_send()
        all_sent(parts.at[0 : group - 1], part_send).wait_send()

    dma = pltpu.SemaphoreType.DMA
    one = dma((1,))
    pl.run_scoped(
        work,
        dma((9,)),
        dma((2, 9)),
        dma((2, 3 + 2 * SEGMENTS + steps)),
        *(one,) * 9,
    )

    for n in range(nz - 1):
        near = n + (n >= z).astype(jnp.int32)
        far = nz - 1 - (n + (n >= nz - 1 - z).astype(jnp.int32))
        distance = 1 if n == 0 else nz - n
        source = jnp.where(2 * z < nz, near, far)
        source = jnp.where(z == 0, distance, jnp.where(z == nz - 1, nz - 1 - distance, source))

        @pl.loop(0, pieces)
        def _(piece, source=source):
            take(source, piece).wait_recv()
            for step in range(CHUNK // 8):
                rows = pl.ds(pl.multiple_of(piece * CHUNK + step * 8, 8), 8)
                planes = [owned[source * F + f, rows, :] for f in range(F)]
                for q in range(rank):
                    value = fresh[q, rows, :]
                    for f in range(F):
                        value = value + table_smem[q, rank + source * F + f] * planes[f]
                    fresh[q, rows, :] = value

    for b in range(nz):
        @pl.when(z != b)
        def _(b=b):
            rows = pl.ds(b * own, own)
            pltpu.make_async_remote_copy(
                src_ref=anchor.at[:, rows, :], dst_ref=owned.at[pl.ds(z * F, F)],
                send_sem=move_send.at[b], recv_sem=move_recv.at[z, 0],
                device_id=(r, c, b), device_id_type=MESH,
            ).wait_send()


def deliver(shrunk, coeff, fresh, shrunk_hbm, coeff_hbm, fresh_hbm, sems):
    copies = [pltpu.make_async_copy(coeff, coeff_hbm, sems.at[0])]
    for source, place in ((fresh, fresh_hbm), (shrunk, shrunk_hbm)):
        share = source.shape[0] // 4
        for i in range(4):
            part = pl.ds(i * share, share)
            copies.append(
                pltpu.make_async_copy(source.at[part], place.at[part], sems.at[len(copies)])
            )
    for copy in copies:
        copy.start()
    for copy in copies:
        copy.wait()


def whole_kernel(video, multiplier, foreground, basis, coefficients):
    F, H, W = video.shape
    rank = basis.shape[0]
    nr, nc, nz = (lax.axis_size(name) for name in ("row", "col", "frame"))
    f32 = jnp.float32
    own = H // nz
    group = nr * nc
    vmem = pltpu.VMEM
    dma = pltpu.SemaphoreType.DMA
    pieces = own // CHUNK
    hbm = pl.BlockSpec(memory_space=pl.ANY)
    on_chip = pl.BlockSpec(memory_space=pltpu.VMEM)
    found = pl.pallas_call(
        functools.partial(kernel, (F, H, W, rank, nr, nc, nz)),
        out_shape=(vmem((F, H, W), f32), vmem((F, rank), f32), vmem((rank, own, W), f32)),
        in_specs=[hbm] * 5,
        out_specs=[on_chip] * 3,
        scratch_shapes=[vmem((F + 2, H + 16, W), f32)] * PASSES
        + [
            vmem((F, H, W), f32),
            vmem((F, H, W), f32),
            vmem((rank, H, W), f32),
            vmem((F, H, W), f32),
            vmem((F, H, W), f32),
            vmem((F * nz, own, W), f32),
            vmem((PASSES, SEGMENTS, 16, H // SEGMENTS), f32),
            vmem((PASSES, SEGMENTS, 16, H // SEGMENTS), f32),
            vmem((PASSES, 2, F, 8, 128), f32),
            vmem((H + 8, 128), f32),
            vmem((H + 16, 128), f32),
            vmem((H + 16, 128), f32),
            vmem((H + 24, 128), f32),
            vmem((H + 24, 128), f32),
            vmem((8, 128), f32),
            vmem((F, rank, 8, 128), f32),
            vmem((rank + F, rank, 128), f32),
            vmem((nz, 8, 128), f32),
            vmem((group, 8, 128), f32),
            vmem((rank, rank, 128), f32),
            vmem((group, rank, 128), f32),
            vmem((nz * F, 128), f32),
            vmem((128, 128), f32),
            vmem((rank, 128), f32),
            pltpu.SMEM((F, rank), f32),
            pltpu.SMEM((rank, 128), f32),
            dma((nz,)),
            dma((nz, pieces)),
        ],
        compiler_params=pltpu.CompilerParams(
            collective_id=0, has_side_effects=True, vmem_limit_bytes=32 * 1024 * 1024
        ),
    )(
        *(
            pltpu.with_memory_space_constraint(x, pltpu.HBM)
            for x in (coefficients, video, multiplier, foreground, basis)
        )
    )
    return pl.pallas_call(
        deliver,
        out_shape=(
            jax.ShapeDtypeStruct((F, H, W), f32),
            jax.ShapeDtypeStruct((F, rank), f32),
            jax.ShapeDtypeStruct((rank, own, W), f32),
        ),
        in_specs=[on_chip] * 3,
        out_specs=[hbm] * 3,
        scratch_shapes=[dma((9,))],
    )(*(pltpu.with_memory_space_constraint(x, pltpu.VMEM) for x in found))


def body(video, multiplier, foreground, basis, coefficients):
    F, H, W = video.shape
    rank = basis.shape[0]
    nz = lax.axis_size("frame")
    fits = (
        H % nz == 0 and (H // nz) % 8 == 0 and (H // nz) % CHUNK == 0 and W % 128 == 0
        and H % 16 == 0 and H % (SEGMENTS * CHUNK) == 0 and lax.axis_size("row") <= 2
        and F % 4 == 0 and F < 8 and rank == 16 and nz >= 2 and F * nz == rank and 2 * rank + F * nz <= 128
    )
    run = whole_kernel if fits else local
    return run(video, multiplier, foreground, basis, coefficients)


def solution(mesh):
    placed = (
        P("frame", "row", "col"),
        P("frame", "row", "col"),
        P("frame", "row", "col"),
        P(None, "row", "col"),
        P("frame", None),
    )
    return jax.shard_map(
        body,
        mesh=mesh,
        in_specs=placed,
        out_specs=(P("frame", "row", "col"), P("frame", None), P(None, ("row", "frame"), "col")),
        check_vma=False,
    )
```

```python
import functools

import jax
import jax.numpy as jnp
from jax import lax
from jax.experimental import pallas as pl
from jax.experimental.pallas import tpu as pltpu
from jax.sharding import PartitionSpec as P

PASSES = 3


relax_rate = 0.8
smooth_weight = 0.5
smooth_floor = 0.25
shrink_level = 0.4
dual_scale = 0.8
ridge_share = 0.1


def with_halo(block, sides, width):
    for axis, dim in sides:
        count = lax.axis_size(axis)
        forward = [(i, i + 1) for i in range(count - 1)]
        backward = [(target, source) for source, target in forward]
        low = lax.ppermute(
            lax.slice_in_dim(block, block.shape[dim] - width, None, axis=dim), axis, forward
        )
        high = lax.ppermute(lax.slice_in_dim(block, 0, width, axis=dim), axis, backward)
        block = jnp.concatenate([low, block, high], axis=dim)
    return block


def forward_cells(padded, direction, shape):
    starts = [0, 0, 0]
    starts[direction] = 1
    limits = [starts[axis_dim] + shape[axis_dim] for axis_dim in range(3)]
    return lax.slice(padded, starts, limits)


def descend(padded, source, anchor, extent):
    shape = tuple((int(length) - 1 for length in padded.shape))
    here_cells = padded[:-1, :-1, :-1]
    slopes = []
    for direction in range(3):
        ahead_cells = forward_cells(padded, direction, shape)
        places = anchor[direction] + jnp.arange(shape[direction], dtype=jnp.int32)
        inside = (places >= 0) & (places < extent[direction] - 1)
        layout = [1, 1, 1]
        layout[direction] = shape[direction]
        inside = inside.reshape(layout)
        slopes.append(jnp.where(inside, ahead_cells - here_cells, jnp.zeros_like(here_cells)))
    weight = lax.rsqrt(
        smooth_floor + slopes[0] * slopes[0] + slopes[1] * slopes[1] + slopes[2] * slopes[2]
    )
    fluxes = [slope_part * weight for slope_part in slopes]
    spread = (
        fluxes[0][1:, 1:, 1:]
        - fluxes[0][:-1, 1:, 1:]
        + (fluxes[1][1:, 1:, 1:] - fluxes[1][1:, :-1, 1:])
        + (fluxes[2][1:, 1:, 1:] - fluxes[2][1:, 1:, :-1])
    )
    center = padded[1:-1, 1:-1, 1:-1]
    return center + relax_rate * (source - center + smooth_weight * spread)


def solve_definite(matrix, right_side):
    factor_lower = jnp.linalg.cholesky(matrix)
    half_solved = lax.linalg.triangular_solve(factor_lower, right_side, left_side=True, lower=True)
    return lax.linalg.triangular_solve(
        factor_lower, half_solved, left_side=True, lower=True, transpose_a=True
    )


def local(video, multiplier, foreground, basis, coefficients):
    highest = lax.Precision.HIGHEST
    frames_here, rows_here, cols_here = video.shape
    rank_size = basis.shape[0]
    frame_count = lax.axis_size("frame")
    row_count = lax.axis_size("row")
    col_count = lax.axis_size("col")
    extent = (frames_here * frame_count, rows_here * row_count, cols_here * col_count)
    frame_slot = lax.axis_index("frame")
    corner = (
        frame_slot * frames_here,
        lax.axis_index("row") * rows_here,
        lax.axis_index("col") * cols_here,
    )
    pixels = rows_here * cols_here
    flat_basis = basis.reshape(rank_size, pixels)
    background = jnp.dot(coefficients, flat_basis, precision=highest).reshape(video.shape)
    target = video - background + dual_scale * multiplier
    current = foreground
    for sweep in range(PASSES):
        padded = with_halo(current, (("row", 1), ("col", 2), ("frame", 0)), 1)
        current = descend(padded, target, tuple((start_cell - 1 for start_cell in corner)), extent)
    shrunk = current - jnp.clip(current, -shrink_level, shrink_level)
    residual_target = video + dual_scale * multiplier - shrunk
    flat_target = residual_target.reshape(frames_here, pixels)
    gram_part = jnp.dot(flat_basis, flat_basis.T, precision=highest)
    cross_part = jnp.dot(flat_basis, flat_target.T, precision=highest)
    gram_sum, cross_sum = lax.psum((gram_part, cross_part), ("row", "col"))
    identity_matrix = jnp.eye(rank_size, dtype=gram_sum.dtype)
    pixel_ridge = ridge_share * pixels * row_count * col_count
    coeff_rows = solve_definite(
        gram_sum + pixel_ridge * identity_matrix, cross_sum + pixel_ridge * coefficients.T
    )
    total_part = jnp.dot(coeff_rows, flat_target, precision=highest).reshape(
        rank_size, rows_here, cols_here
    )
    frame_gram_part = jnp.dot(coeff_rows, coeff_rows.T, precision=highest)
    owned_rows = rows_here // frame_count
    owned_sums = lax.psum_scatter(total_part, "frame", scatter_dimension=1, tiled=True)
    frame_gram = lax.psum(frame_gram_part, "frame")
    old_owned = lax.dynamic_slice_in_dim(basis, frame_slot * owned_rows, owned_rows, 1)
    frame_ridge = ridge_share * frames_here * frame_count
    right_side = (owned_sums + frame_ridge * old_owned).reshape(rank_size, owned_rows * cols_here)
    new_basis = solve_definite(frame_gram + frame_ridge * identity_matrix, right_side)
    return (shrunk, coeff_rows.T, new_basis.reshape(rank_size, owned_rows, cols_here))


MESH = pl.DeviceIdType.MESH
CHUNK = 24
SEGMENTS = 4


def eliminate(matrix, size):
    lanes = lax.broadcasted_iota(jnp.int32, matrix.shape, 1)
    rows = lax.broadcasted_iota(jnp.int32, matrix.shape, 0)
    for k in range(size):
        pivot = matrix[k : k + 1, k : k + 1]
        scaled = matrix[k : k + 1, :] / pivot
        column = jnp.sum(jnp.where(lanes == k, matrix, 0.0), axis=1, keepdims=True)
        matrix = jnp.where(rows == k, scaled, matrix - column * scaled)
    return matrix


def kernel(
    sizes, coeff_hbm, video_hbm, mult_hbm, fore_hbm, basis_hbm,
    result, coeff_out, fresh,
    field0, field1, field2, video, mult, basis, anchor, target, owned,
    packed, arrived, corner, edge_next, edge_flux, first_cols, left_now, left_next, bottom_row,
    cross, sums, grams, gram_parts, inverse, parts, shares, square, table, coeff_ref, table_smem,
):
    field = (field0, field1, field2)
    F, H, W, rank, nr, nc, nz = sizes
    r = lax.axis_index("row")
    c = lax.axis_index("col")
    z = lax.axis_index("frame")
    own = H // nz
    pieces = own // CHUNK
    half = H // 2
    flip = lax.rem(r, 2)

    steps = H // CHUNK

    def chunk_at(step):
        return step + flip * (steps - 1 - 2 * step)

    def rows_at(step, offset=0):
        return pl.ds(pl.multiple_of(offset + chunk_at(step) * CHUNK, 8), CHUNK)

    span = H // SEGMENTS
    per = steps // SEGMENTS

    def segment_start(j):
        return pl.multiple_of((j + flip * (SEGMENTS - 1 - 2 * j)) * span, 8)

    def half_start(h):
        return pl.multiple_of((h + flip * (1 - 2 * h)) * half, 8)

    inner = (z > 0) & (z < nz - 1)

    def inside(dr, dc, dz):
        ok = None
        for at, step, count in ((r, dr, nr), (c, dc, nc), (z, dz, nz)):
            if step != 0:
                test = (at + step >= 0) & (at + step < count)
                ok = test if ok is None else ok & test
        return ok

    def work(
        in_sems, halo_send, halo_recv, part_send, part_recv, gram_send, gram_recv,
        total_send, total_recv, share_send, share_recv, small_sem, move_send, move_recv,
    ):
        def take(source, piece):
            rows = pl.ds(pl.multiple_of(z * own + piece * CHUNK, 8), CHUNK)
            spot = pl.ds(pl.multiple_of(piece * CHUNK, 8), CHUNK)
            return pltpu.make_async_remote_copy(
                src_ref=anchor.at[:, rows, :], dst_ref=owned.at[pl.ds(source * F, F), spot, :],
                send_sem=move_send.at[source], recv_sem=move_recv.at[source, piece],
                device_id=(r, c, source), device_id_type=MESH,
            )

        halves = [pl.ds(half_start(h), half) for h in range(2)]
        loads = [
            pltpu.make_async_copy(src, dst, in_sems.at[i])
            for i, (src, dst) in enumerate(
                [
                    (
                        fore_hbm.at[:, halves[h], :],
                        field0.at[1 : F + 1, pl.ds(pl.multiple_of(half_start(h) + 8, 8), half), :],
                    )
                    for h in range(2)
                ]
                + [(coeff_hbm, coeff_ref)]
                + [
                    (src.at[:, rows, :], dst.at[:, rows, :])
                    for rows in halves
                    for src, dst in ((video_hbm, video), (mult_hbm, mult), (basis_hbm, basis))
                ]
            )
        ]
        for load in loads[:2]:
            load.start()

        barrier = pltpu.get_barrier_semaphore()
        beside = ((0, 0, 1), (0, 1, 0), (1, 0, 0), (1, 0, -1), (0, 1, -1), (1, -1, 0))
        beside += tuple(tuple(-s for s in step) for step in beside)
        for step in beside:
            @pl.when(inside(*step))
            def _(step=step):
                pl.semaphore_signal(
                    barrier,
                    inc=1,
                    device_id=(r + step[0], c + step[1], z + step[2]),
                    device_id_type=MESH,
                )
        expected = jnp.int32(0)
        for step in beside:
            expected = expected + inside(*step).astype(jnp.int32)
        for load in loads[2:]:
            load.start()

        pl.semaphore_wait(barrier, expected)

        lane_h = lax.broadcasted_iota(jnp.int32, (span, 128), 1)

        def pack_columns(k, j):
            base = segment_start(j)
            tile = jnp.zeros((span, 128), jnp.float32)
            for f in range(F):
                for lane, at in ((f, 0), (8 + f, W - 1)):
                    lanes = field[k][f + 1, pl.ds(base + 8, span), (at // 128) * 128 : (at // 128) * 128 + 128]
                    tile = jnp.where(lane_h == lane, lanes[:, at % 128 : at % 128 + 1], tile)
            first_cols[pl.ds(base + 8, span), :] = tile
            packed[k, j] = tile.T[:16, :]

        strips = range(4)
        corners = (4, 5)

        def column_list(k, j):
            return (
                (packed.at[k, j, 0:F], arrived.at[k, j, 1 : F + 1], (0, -1, 0)),
                (packed.at[k, j, 8 : 8 + F], arrived.at[k, j, 8 : 8 + F], (0, 1, 0)),
                (packed.at[k, j, F - 1 : F], arrived.at[k, j, 0:1], (0, -1, 1)),
                (packed.at[k, j, 8:9], arrived.at[k, j, 8 + F : 9 + F], (0, 1, -1)),
            )

        def halo_list(k):
            fk = field[k]
            mid = slice(1, F + 1)
            return (
                (fk.at[mid, H : H + 8, :], fk.at[mid, 0:8, :], (1, 0, 0)),
                (fk.at[mid, 8:16, :], fk.at[mid, H + 8 : H + 16, :], (-1, 0, 0)),
                (fk.at[F, 8:9, :], fk.at[0, H + 8 : H + 9, :], (-1, 0, 1)),
                (fk.at[1, H + 7 : H + 8, :], fk.at[F + 1, 7:8, :], (1, 0, -1)),
                (fk.at[mid, H : H + 8, 0:128], corner.at[k, 0], (1, -1, 0)),
                (fk.at[mid, 8:16, W - 128 : W], corner.at[k, 1], (-1, 1, 0)),
            )

        def halo_copy(k, i, leave, src, dst, step):
            return pltpu.make_async_remote_copy(
                src_ref=src, dst_ref=dst,
                send_sem=halo_send.at[k % 2, leave], recv_sem=halo_recv.at[k % 2, i],
                device_id=(r + step[0], c + step[1], z + step[2]), device_id_type=MESH,
            )

        def send_columns(k, j):
            for i, (src, dst, step) in enumerate(column_list(k, j)):
                @pl.when(inside(*step))
                def _(i=i, src=src, dst=dst, step=step):
                    halo_copy(k, 3 + 2 * j + i % 2, 3 + i, src, dst, step).start()

        def wait_columns(k, j):
            for side, step, corner_step, small, large in (
                (0, (0, -1, 0), (0, -1, 1), slice(1, F + 1), slice(0, F + 1)),
                (1, (0, 1, 0), (0, 1, -1), slice(8, 8 + F), slice(8, 9 + F)),
            ):
                near = inside(*(-s for s in step))
                both = inside(*(-s for s in corner_step))
                for turn, rows in ((near & ~both, small), (both, large)):
                    @pl.when(turn)
                    def _(side=side, step=step, rows=rows):
                        ref = arrived.at[k, j, rows]
                        halo_copy(k, 3 + 2 * j + side, 0, ref, ref, step).wait_recv()

        def face(k, step, up):
            fk = field[k]
            rows = rows_at(step, 8)
            at = 3 + 2 * SEGMENTS + step
            mine, theirs = (F, 0) if up else (1, F + 1)
            src = fore_hbm.at[mine - 1, rows_at(step)] if k == 0 else fk.at[mine, rows]
            return halo_copy(
                k, at, 7 if up else 8, src, fk.at[theirs, rows], (0, 0, 1 if up else -1)
            )

        def send_faces(k, low, high):
            @pl.loop(low, high)
            def _(step):
                for up in (True, False):
                    @pl.when(inside(0, 0, 1 if up else -1))
                    def _(up=up):
                        face(k, step, up).start()

        def wait_face(k, step):
            for turn, frames in ((inner, slice(0, 2)), (~inner, slice(0, 1))):
                @pl.when(turn)
                def _(frames=frames):
                    ref = field[k].at[frames, rows_at(step, 8), :]
                    halo_copy(k, 3 + 2 * SEGMENTS + step, 0, ref, ref, (0, 0, 1)).wait_recv()

        def send_halos(k, which):
            every = halo_list(k)
            for i in which:
                src, dst, step = every[i]

                @pl.when(inside(*step))
                def _(i=i, src=src, dst=dst, step=step):
                    halo_copy(k, i // 2, i // 2, src, dst, step).start()

        def wait_halos(k, which):
            every = halo_list(k)
            for i in which:
                src, dst, step = every[i]

                @pl.when(inside(*(-s for s in step)))
                def _(i=i, src=src, dst=dst, step=step):
                    halo_copy(k, i // 2, i // 2, src, dst, step).wait_recv()

        def finish_sends(k):
            for i, (src, dst, step) in enumerate(halo_list(k)):
                @pl.when(inside(*step))
                def _(i=i, src=src, dst=dst, step=step):
                    halo_copy(k, i // 2, i // 2, src, dst, step).wait_send()

            every = (
                (packed.at[k, :, 0:F], arrived.at[k, :, 1 : F + 1], (0, -1, 0)),
                (packed.at[k, :, 8 : 8 + F], arrived.at[k, :, 8 : 8 + F], (0, 1, 0)),
                (packed.at[k, :, F - 1 : F], arrived.at[k, :, 0:1], (0, -1, 1)),
                (packed.at[k, :, 8:9], arrived.at[k, :, 8 + F : 9 + F], (0, 1, -1)),
                (field[k].at[F, 8 : H + 8, :], field[k].at[0, 8 : H + 8, :], (0, 0, 1)),
                (field[k].at[1, 8 : H + 8, :], field[k].at[F + 1, 8 : H + 8, :], (0, 0, -1)),
            )
            for i, (src, dst, step) in enumerate(every):
                @pl.when(inside(*step))
                def _(i=i, src=src, dst=dst, step=step):
                    halo_copy(k, 0, 3 + i, src, dst, step).wait_send()

        def prepare_columns(k, j):
            base = segment_start(j)
            spread = jnp.concatenate(
                [arrived[k, j], jnp.zeros((112, span), jnp.float32)], axis=0
            ).T
            edge_next[pl.ds(base + 8, span), :] = spread
            left_now[pl.ds(base + 8, span), :] = pltpu.roll(spread, 120, 1)
            left_next[pl.ds(base + 8, span), :] = pltpu.roll(spread, 119, 1)
            low, count = pl.multiple_of(base + 8 * flip, 8), span + 8
            here = left_now[pl.ds(low, count), :]
            ahead = left_next[pl.ds(low, count), :]
            lane = lax.broadcasted_iota(jnp.int32, (count, 128), 1)
            row = lax.broadcasted_iota(jnp.int32, (count, 128), 0) + (low - 8)
            slope0 = jnp.where((lane == F - 1) & (z == nz - 1), 0.0, ahead - here)
            after = left_now[pl.ds(low, count + 8), :]
            below = jnp.where(
                row == H - 1, bottom_row[0:1, :], pltpu.roll(after, count + 7, 0)[:count]
            )
            slope1 = jnp.where((row == H - 1) & (r == nr - 1), 0.0, below - here)
            slope2 = first_cols[pl.ds(low, count), :] - here
            weight = lax.rsqrt(smooth_floor + slope0 * slope0 + slope1 * slope1 + slope2 * slope2)
            edge_flux[pl.ds(low, count), :] = jnp.where(c == 0, 0.0, slope2 * weight)

        def take_corners(k):
            wait_halos(k, corners)
            lane8 = lax.broadcasted_iota(jnp.int32, (8, 128), 1)
            top = jnp.zeros((8, 128), jnp.float32)
            bottom = jnp.zeros((8, 128), jnp.float32)
            for f in range(F):
                top = jnp.where(lane8 == f + 1, corner[k, 0, f][:, 0:1], top)
                bottom = jnp.where(lane8 == f, corner[k, 1, f][:, 127:128], bottom)
            edge_next[0:8, :] = top
            bottom_row[...] = bottom

        def sweep(k, last, start):
            R = CHUNK
            tiles = W // 128
            row_8 = lax.broadcasted_iota(jnp.int32, (8, 128), 0) + (r * H + start)
            above_image = row_8 - 8 < 0
            last_image_row = row_8 + (R - 8) >= nr * H - 1
            columns = edge_next[pl.ds(start, R + 8), :]
            fluxes_in = edge_flux[pl.ds(start + 8, R), :]
            at = pl.ds(start, R)

            def frame(f):
                return [
                    field[k][f, pl.ds(start, R + 16), w * 128 : w * 128 + 128] for w in range(tiles)
                ]

            now = frame(0)
            flux0_before = None
            for f in range(-1, F):
                after = frame(f + 2)
                skip = 8 if f < 0 else 0
                n = R + 8 - skip
                lane = lax.broadcasted_iota(jnp.int32, (n, 128), 1)
                here = [t[skip : R + 8] for t in now]
                turned = [pltpu.roll(t, 127, 1) for t in here]
                wall = jnp.broadcast_to(columns[skip:, f + 1 : f + 2], (n, 128))
                flux0, flux1, flux2 = [], [], []
                for w in range(tiles):
                    slope0 = after[w][skip : R + 8] - here[w]
                    if f == F - 1:
                        slope0 = jnp.where(z == nz - 1, 0.0, slope0)
                    slope1 = pltpu.roll(now[w][skip:], n + 7, 0)[:n] - here[w]
                    slope1 = jnp.concatenate(
                        [slope1[: n - 8], jnp.where(last_image_row, 0.0, slope1[n - 8 :])], axis=0
                    )
                    beyond = turned[w + 1] if w + 1 < tiles else wall
                    slope2 = jnp.where(lane == 127, beyond, turned[w]) - here[w]
                    if w + 1 == tiles:
                        slope2 = jnp.where((lane == 127) & (c == nc - 1), 0.0, slope2)
                    weight = lax.rsqrt(
                        smooth_floor + slope0 * slope0 + slope1 * slope1 + slope2 * slope2
                    )
                    flux0.append((slope0 * weight)[8 - skip :])
                    if f >= 0:
                        flux = slope1 * weight
                        flux1.append(
                            jnp.concatenate(
                                [jnp.where(above_image, 0.0, flux[:8]), flux[8:]], axis=0
                            )
                        )
                        flux2.append((slope2 * weight)[8:])
                if f < 0:
                    flux0 = [jnp.where(z == 0, 0.0, t) for t in flux0]
                else:
                    moved = [pltpu.roll(t, 1, 1) for t in flux2]
                    entry = jnp.broadcast_to(fluxes_in[:, f : f + 1], (R, 128))
                    lane = lax.broadcasted_iota(jnp.int32, (R, 128), 1)
                    for w in range(tiles):
                        left = jnp.where(lane == 0, moved[w - 1] if w > 0 else entry, moved[w])
                        above = pltpu.roll(flux1[w], 1, 0)[8:]
                        spread = (flux0[w] - flux0_before[w]) + (flux1[w][8:] - above) + (flux2[w] - left)
                        lanes = slice(w * 128, w * 128 + 128)
                        value = (1.0 - relax_rate) * here[w][8:] + (
                            target[f, at, lanes] + (relax_rate * smooth_weight) * spread
                        )
                        if last:
                            shrunk = value - jnp.clip(value, -shrink_level, shrink_level)
                            result[f, at, lanes] = shrunk
                            anchor[f, at, lanes] = anchor[f, at, lanes] - shrunk
                        else:
                            field[k + 1][f + 1, pl.ds(start + 8, R), lanes] = value
                flux0_before = flux0
                now = after

        def products(left_of, right_of, lefts, rights, first, count, start, store):
            def body(step, totals):
                rows = pl.ds(pl.multiple_of(first + step * 8, 8), 8)
                a = [left_of[i, rows, :] for i in lefts]
                b = [right_of[j, rows, :] for j in rights]
                out = []
                for x in range(len(lefts)):
                    for y in range(len(rights)):
                        prod = a[x] * b[y]
                        total = totals[len(out)]
                        for w in range(W // 128):
                            total = total + prod[:, w * 128 : w * 128 + 128]
                        out.append(total)
                return tuple(out)

            totals = lax.fori_loop(
                0, count // 8, body, tuple(start(i, j) for i in lefts for j in rights), unroll=3 if count % 24 == 0 else 1
            )
            n = 0
            for i in lefts:
                for j in rights:
                    store(i, j, totals[n])
                    n += 1

        def held(block):
            return (block - z >= 2) | (z - block >= 2)

        def move(block, piece):
            rows = pl.ds(pl.multiple_of(block * own + piece * CHUNK, 8), CHUNK)
            spot = pl.ds(pl.multiple_of(piece * CHUNK, 8), CHUNK)
            return pltpu.make_async_remote_copy(
                src_ref=anchor.at[:, rows, :], dst_ref=owned.at[pl.ds(z * F, F), spot, :],
                send_sem=move_send.at[block], recv_sem=move_recv.at[z, piece],
                device_id=(r, c, block), device_id_type=MESH,
            )

        send_faces(0, 0, 1)
        for j in range(SEGMENTS):
            if j % (SEGMENTS // 2) == 0:
                loads[j // (SEGMENTS // 2)].wait()
            pack_columns(0, j)
            send_columns(0, j)
            if j == SEGMENTS // 2:
                send_halos(0, strips)
                send_halos(0, corners)
            send_faces(0, max(1, j * per), (j + 1) * per)

        zero_tile = jnp.zeros((8, 128), jnp.float32)

        def store_gram(i, j, value):
            row = jnp.sum(value, axis=0, keepdims=True)
            sums[j, i : i + 1, :] = row
            if i // 4 != j // 4:
                sums[i, j : j + 1, :] = row

        lane_r = lax.broadcasted_iota(jnp.int32, (rank, 128), 1)
        row_r = lax.broadcasted_iota(jnp.int32, (rank, 128), 0)

        def gram_share():
            for i in range(0, rank, 4):
                for j in range(i, rank, 4):
                    products(
                        basis, basis, range(i, i + 4), range(j, j + 4), z * own, own,
                        lambda i, j: zero_tile, store_gram,
                    )
            tile = jnp.zeros((rank, 128), jnp.float32)
            for q in range(rank):
                tile = jnp.where(lane_r == q, jnp.sum(sums[q], axis=1, keepdims=True), tile)
            lane = lax.broadcasted_iota(jnp.int32, (8, 128), 1)
            tile = jnp.where(lane < rank, tile[:8], pltpu.roll(tile[8:], rank, 1))
            tile = jnp.where(lane < 2 * rank, tile, pltpu.roll(pltpu.roll(tile, 4, 0), 2 * rank, 1))
            tile = jnp.where(lane < 4 * rank, tile, pltpu.roll(pltpu.roll(tile, 6, 0), 4 * rank, 1))
            grams[z] = tile

        def unfold(tile):
            row = lax.broadcasted_iota(jnp.int32, (8, 128), 0)
            tile = jnp.where(row < 2, tile, pltpu.roll(pltpu.roll(tile, 2, 0), 128 - 4 * rank, 1))
            tile = jnp.where(row < 4, tile, pltpu.roll(pltpu.roll(tile, 4, 0), 128 - 2 * rank, 1))
            tile = jnp.concatenate([tile, pltpu.roll(tile, 128 - rank, 1)], axis=0)
            return jnp.where(lane_r < rank, tile, 0.0)

        def all_sent(block, sem):
            return pltpu.make_async_remote_copy(
                src_ref=block, dst_ref=block, send_sem=sem.at[0], recv_sem=sem.at[0],
                device_id=(r, c, lax.rem(z + 1, nz)), device_id_type=MESH,
            )

        def all_here(block, sem):
            return pltpu.make_async_remote_copy(
                src_ref=block, dst_ref=block, send_sem=sem.at[0], recv_sem=sem.at[0],
                device_id=(r, c, lax.rem(z + 1, nz)), device_id_type=MESH,
            )

        def share_gram(d):
            return pltpu.make_async_remote_copy(
                src_ref=grams.at[z, 0:2], dst_ref=grams.at[z, 0:2],
                send_sem=gram_send.at[0], recv_sem=gram_recv.at[0],
                device_id=(r, c, lax.rem(z + d, nz)), device_id_type=MESH,
            )

        group = nr * nc
        me = r * nc + c

        def share_total(d):
            other = lax.rem(me + d, group)
            return pltpu.make_async_remote_copy(
                src_ref=gram_parts.at[me, 0:2], dst_ref=gram_parts.at[me, 0:2],
                send_sem=total_send.at[0], recv_sem=total_recv.at[0],
                device_id=(other // nc, lax.rem(other, nc), z), device_id_type=MESH,
            )

        def store_cross(i, j, value):
            cross[j, i] = value

        def find_target(h):
            for load in loads[3 + 3 * h : 6 + 3 * h]:
                load.wait()

            @pl.loop(0, half // 8)
            def _(step):
                rows = pl.ds(pl.multiple_of(half_start(h) + step * 8, 8), 8)
                totals = [None] * F
                for q in range(rank):
                    plane = basis[q, rows, :]
                    for f in range(F):
                        term = coeff_ref[f, q] * plane
                        totals[f] = term if totals[f] is None else totals[f] + term
                for f in range(F):
                    lifted = dual_scale * mult[f, rows, :]
                    anchor[f, rows, :] = video[f, rows, :] + lifted
                    target[f, rows, :] = relax_rate * (video[f, rows, :] - totals[f] + lifted)

        loads[2].wait()
        find_target(0)
        find_target(1)
        gram_share()

        def advance(k, step):
            start = pl.multiple_of(chunk_at(step) * CHUNK, 8)
            sweep(k, k == PASSES - 1, start)
            if k == PASSES - 1:
                place, piece = chunk_at(step) // pieces, lax.rem(chunk_at(step), pieces)

                @pl.when((place - z == 1) | (z - place == 1))
                def _():
                    move(place, piece).start()

                for i in range(0, rank, 4):
                    products(
                        basis, anchor, range(i, i + 4), range(F), start, CHUNK,
                        lambda i, j: cross[j, i], store_cross,
                    )

        cross[...] = jnp.zeros_like(cross)
        bottom_row[...] = jnp.zeros_like(bottom_row)
        for k in range(PASSES):
            last = k == PASSES - 1
            if k > 0 and not last:
                finish_sends(k - 1)
            wait_columns(k, 0)
            prepare_columns(k, 0)
            wait_face(k, 0)

            @pl.loop(0, SEGMENTS)
            def _(j, k=k, last=last):
                @pl.loop(j * per, (j + 1) * per - 1)
                def _(step):
                    wait_face(k, step + 1)
                    advance(k, step)

                final = j == SEGMENTS - 1
                if k == PASSES - 2:
                    @pl.when(j == 1)
                    def _():
                        for d in range(1, nz):
                            share_gram(d).start()
                if k == PASSES - 1:
                    @pl.when(j == 1)
                    def _():
                        all_here(grams.at[0 : nz - 1, 0:2], gram_recv).wait_recv()
                        total = grams[0]
                        for i in range(1, nz):
                            total = total + grams[i]
                        gram_parts[me] = total
                        for d in range(1, group):
                            share_total(d).start()

                @pl.when(j == SEGMENTS - 2)
                def _():
                    take_corners(k)

                @pl.when(~final)
                def _():
                    wait_columns(k, j + 1)
                    prepare_columns(k, j + 1)
                    wait_face(k, (j + 1) * per)

                @pl.when(final)
                def _():
                    wait_halos(k, strips)

                advance(k, (j + 1) * per - 1)
                if not last:
                    @pl.when(final)
                    def _():
                        send_halos(k + 1, strips)
                        send_halos(k + 1, corners)

                    pack_columns(k + 1, j)
                    send_columns(k + 1, j)
                    send_faces(k + 1, j * per, (j + 1) * per)


        def send_held(turn, low, high):
            for b in range(nz):
                @pl.when(held(b) & turn)
                def _(b=b):
                    for p in range(low, high):
                        move(b, p).start()

        for far, near in ((nz - 1, 0), (0, nz - 1)):
            place = far - 1 if far > near else far + 1

            @pl.when((z == near) & held(jnp.int32(place)))
            def _(place=place):
                move(place, 0).start()

        for j in range(F):
            for i in range(rank):
                sums[rank + j, i : i + 1, :] = jnp.sum(cross[j, i], axis=0, keepdims=True)

        part = jnp.zeros((rank, 128), jnp.float32)
        for q in range(rank, rank + F):
            part = jnp.where(lane_r == q, jnp.sum(sums[q], axis=1, keepdims=True), part)
        parts[me] = part

        def share_part(d):
            other = lax.rem(me + d, group)
            return pltpu.make_async_remote_copy(
                src_ref=parts.at[me], dst_ref=parts.at[me],
                send_sem=part_send.at[0], recv_sem=part_recv.at[0],
                device_id=(other // nc, lax.rem(other, nc), z), device_id_type=MESH,
            )

        for d in range(1, group):
            share_part(d).start()
        pixel_ridge = ridge_share * H * W * group
        diagonal = lane_r == row_r
        before = jnp.zeros((rank, 128), jnp.float32)
        for q in range(rank):
            for f in range(F):
                before = jnp.where((row_r == q) & (lane_r == rank + f), coeff_ref[f, q], before)
        all_here(gram_parts.at[0 : group - 1, 0:2], total_recv).wait_recv()
        total = gram_parts[0]
        for i in range(1, group):
            total = total + gram_parts[i]
        diagonal = lane_r == row_r
        system = unfold(total) + jnp.where(
            diagonal, pixel_ridge, jnp.where(lane_r == row_r + rank, 1.0, 0.0)
        )
        system = eliminate(system, rank)
        for q in range(rank):
            inverse[q] = jnp.broadcast_to(system[:, rank + q : rank + q + 1], (rank, 128))
        all_here(parts.at[0 : group - 1], part_recv).wait_recv()
        total = parts[0]
        for i in range(1, group):
            total = total + parts[i]
        total = total + pixel_ridge * before
        solved = inverse[0] * total[0:1, :]
        for q in range(1, rank):
            solved = solved + inverse[q] * total[q : q + 1, :]
        square[...] = jnp.zeros_like(square)
        square[0:rank, :] = solved
        mine = square[...].T[rank : rank + F, :]
        shares[pl.ds(z * F, F), :] = mine

        def share_rows(d):
            return pltpu.make_async_remote_copy(
                src_ref=shares.at[pl.ds(z * F, F)], dst_ref=shares.at[pl.ds(z * F, F)],
                send_sem=share_send.at[0], recv_sem=share_recv.at[0],
                device_id=(r, c, lax.rem(z + d, nz)), device_id_type=MESH,
            )

        for d in range(1, nz):
            share_rows(d).start()

        send_held(inner, 0, pieces)
        coeff_out[...] = mine[:, 0:rank]
        all_here(shares.at[0 : (nz - 1) * F], share_recv).wait_recv()
        for b in range(nz):
            @pl.when(held(b) & ~inner)
            def _(b=b):
                first = jnp.where(((z == 0) & (b == nz - 2)) | ((z == nz - 1) & (b == 1)), 1, 0)

                @pl.loop(first, pieces)
                def _(p):
                    move(b, p).start()

        frames = F * nz
        square[0:frames, :] = shares[...]
        wide = pltpu.roll(square[...].T[0:rank, :], rank, 1)
        square[0:rank, :] = wide
        gram = lax.dot_general(
            wide, square[...], (((1,), (1,)), ((), ())),
            precision=lax.Precision.HIGHEST, preferred_element_type=jnp.float32,
        )
        frame_ridge = ridge_share * frames
        system = jnp.where(diagonal, gram + frame_ridge, gram) + wide
        system = system + jnp.where(lane_r == row_r + rank + frames, frame_ridge, 0.0)
        table[...] = eliminate(system, rank)
        to_scalar = pltpu.make_async_copy(table, table_smem, small_sem.at[0])
        to_scalar.start()
        to_scalar.wait()
        my_base = z * own

        @pl.loop(0, own // 8)
        def _(step):
            rows = pl.ds(pl.multiple_of(step * 8, 8), 8)
            old = pl.ds(pl.multiple_of(my_base + step * 8, 8), 8)
            for half in range(0, rank, 8):
                totals = [None] * 8
                for f in range(F + rank):
                    plane = anchor[f, old, :] if f < F else basis[f - F, old, :]
                    place = rank + z * F + f if f < F else rank + frames + f - F
                    for q in range(8):
                        term = table_smem[half + q, place] * plane
                        totals[q] = term if totals[q] is None else totals[q] + term
                for q in range(8):
                    fresh[half + q, rows, :] = totals[q]

        for k in range(PASSES - 2, PASSES):
            finish_sends(k)
        all_sent(shares.at[0 : (nz - 1) * F], share_send).wait_send()
        all_sent(grams.at[0 : nz - 1, 0:2], gram_send).wait_send()
        all_sent(gram_parts.at[0 : group - 1, 0:2], total_send).wait_send()
        all_sent(parts.at[0 : group - 1], part_send).wait_send()

        for n in range(nz - 1):
            near = n + (n >= z).astype(jnp.int32)
            far = nz - 1 - (n + (n >= nz - 1 - z).astype(jnp.int32))
            distance = 1 if n == 0 else nz - n
            source = jnp.where(2 * z < nz, near, far)
            source = jnp.where(z == 0, distance, jnp.where(z == nz - 1, nz - 1 - distance, source))

            @pl.loop(0, pieces)
            def _(piece, source=source):
                take(source, piece).wait_recv()
                for step in range(CHUNK // 8):
                    rows = pl.ds(pl.multiple_of(piece * CHUNK + step * 8, 8), 8)
                    planes = [owned[source * F + f, rows, :] for f in range(F)]
                    for q in range(rank):
                        value = fresh[q, rows, :]
                        for f in range(F):
                            value = value + table_smem[q, rank + source * F + f] * planes[f]
                        fresh[q, rows, :] = value

        for b in range(nz):
            @pl.when(z != b)
            def _(b=b):
                rows = pl.ds(b * own, own)
                pltpu.make_async_remote_copy(
                    src_ref=anchor.at[:, rows, :], dst_ref=owned.at[pl.ds(z * F, F)],
                    send_sem=move_send.at[b], recv_sem=move_recv.at[z, 0],
                    device_id=(r, c, b), device_id_type=MESH,
                ).wait_send()

    dma = pltpu.SemaphoreType.DMA
    one = dma((1,))
    pl.run_scoped(
        work,
        dma((9,)),
        dma((2, 9)),
        dma((2, 3 + 2 * SEGMENTS + steps)),
        *(one,) * 9,
        dma((nz,)),
        dma((nz, pieces)),
    )


def deliver(shrunk, coeff, fresh, shrunk_hbm, coeff_hbm, fresh_hbm):
    def work(sems):
        copies = [pltpu.make_async_copy(coeff, coeff_hbm, sems.at[0])]
        for source, place in ((fresh, fresh_hbm), (shrunk, shrunk_hbm)):
            share = source.shape[0] // 1
            for i in range(1):
                part = pl.ds(i * share, share)
                copies.append(
                    pltpu.make_async_copy(source.at[part], place.at[part], sems.at[len(copies)])
                )
        for copy in copies:
            copy.start()
        for copy in copies:
            copy.wait()

    pl.run_scoped(work, pltpu.SemaphoreType.DMA((3,)))


def whole_kernel(video, multiplier, foreground, basis, coefficients):
    F, H, W = video.shape
    rank = basis.shape[0]
    nr, nc, nz = (lax.axis_size(name) for name in ("row", "col", "frame"))
    f32 = jnp.float32
    own = H // nz
    group = nr * nc
    vmem = pltpu.VMEM
    dma = pltpu.SemaphoreType.DMA
    pieces = own // CHUNK
    hbm = pl.BlockSpec(memory_space=pl.ANY)
    on_chip = pl.BlockSpec(memory_space=pltpu.VMEM)
    found = pl.pallas_call(
        functools.partial(kernel, (F, H, W, rank, nr, nc, nz)),
        out_shape=(vmem((F, H, W), f32), vmem((F, rank), f32), vmem((rank, own, W), f32)),
        in_specs=[hbm] * 5,
        out_specs=[on_chip] * 3,
        scratch_shapes=[vmem((F + 2, H + 16, W), f32)] * PASSES
        + [
            vmem((F, H, W), f32),
            vmem((F, H, W), f32),
            vmem((rank, H, W), f32),
            vmem((F, H, W), f32),
            vmem((F, H, W), f32),
            vmem((F * nz, own, W), f32),
            vmem((PASSES, SEGMENTS, 16, H // SEGMENTS), f32),
            vmem((PASSES, SEGMENTS, 16, H // SEGMENTS), f32),
            vmem((PASSES, 2, F, 8, 128), f32),
            vmem((H + 8, 128), f32),
            vmem((H + 16, 128), f32),
            vmem((H + 16, 128), f32),
            vmem((H + 24, 128), f32),
            vmem((H + 24, 128), f32),
            vmem((8, 128), f32),
            vmem((F, rank, 8, 128), f32),
            vmem((rank + F, rank, 128), f32),
            vmem((nz, 8, 128), f32),
            vmem((group, 8, 128), f32),
            vmem((rank, rank, 128), f32),
            vmem((group, rank, 128), f32),
            vmem((nz * F, 128), f32),
            vmem((128, 128), f32),
            vmem((rank, 128), f32),
            pltpu.SMEM((F, rank), f32),
            pltpu.SMEM((rank, 128), f32),
        ],
        compiler_params=pltpu.CompilerParams(
            collective_id=0, has_side_effects=True, vmem_limit_bytes=32 * 1024 * 1024
        ),
    )(
        *(
            pltpu.with_memory_space_constraint(x, pltpu.HBM)
            for x in (coefficients, video, multiplier, foreground, basis)
        )
    )
    return pl.pallas_call(
        deliver,
        out_shape=(
            jax.ShapeDtypeStruct((F, H, W), f32),
            jax.ShapeDtypeStruct((F, rank), f32),
            jax.ShapeDtypeStruct((rank, own, W), f32),
        ),
        in_specs=[on_chip] * 3,
        out_specs=[hbm] * 3,
    )(*(pltpu.with_memory_space_constraint(x, pltpu.VMEM) for x in found))


def body(video, multiplier, foreground, basis, coefficients):
    F, H, W = video.shape
    rank = basis.shape[0]
    nz = lax.axis_size("frame")
    fits = (
        H % nz == 0 and (H // nz) % 8 == 0 and (H // nz) % CHUNK == 0 and W % 128 == 0
        and H % 16 == 0 and H % (SEGMENTS * CHUNK) == 0 and lax.axis_size("row") <= 2
        and F % 4 == 0 and F < 8 and rank == 16 and nz >= 2 and F * nz == rank and 2 * rank + F * nz <= 128
    )
    run = whole_kernel if fits else local
    return run(video, multiplier, foreground, basis, coefficients)


def solution(mesh):
    placed = (
        P("frame", "row", "col"),
        P("frame", "row", "col"),
        P("frame", "row", "col"),
        P(None, "row", "col"),
        P("frame", None),
    )
    return jax.shard_map(
        body,
        mesh=mesh,
        in_specs=placed,
        out_specs=(P("frame", "row", "col"), P("frame", None), P(None, ("row", "frame"), "col")),
        check_vma=False,
    )
```

```python
import functools

import jax
import jax.numpy as jnp
from jax import lax
from jax.experimental import pallas as pl
from jax.experimental.pallas import tpu as pltpu
from jax.sharding import PartitionSpec as P

PASSES = 3


relax_rate = 0.8
smooth_weight = 0.5
smooth_floor = 0.25
shrink_level = 0.4
dual_scale = 0.8
ridge_share = 0.1


def with_halo(block, sides, width):
    for axis, dim in sides:
        count = lax.axis_size(axis)
        forward = [(i, i + 1) for i in range(count - 1)]
        backward = [(target, source) for source, target in forward]
        low = lax.ppermute(
            lax.slice_in_dim(block, block.shape[dim] - width, None, axis=dim), axis, forward
        )
        high = lax.ppermute(lax.slice_in_dim(block, 0, width, axis=dim), axis, backward)
        block = jnp.concatenate([low, block, high], axis=dim)
    return block


def forward_cells(padded, direction, shape):
    starts = [0, 0, 0]
    starts[direction] = 1
    limits = [starts[axis_dim] + shape[axis_dim] for axis_dim in range(3)]
    return lax.slice(padded, starts, limits)


def descend(padded, source, anchor, extent):
    shape = tuple((int(length) - 1 for length in padded.shape))
    here_cells = padded[:-1, :-1, :-1]
    slopes = []
    for direction in range(3):
        ahead_cells = forward_cells(padded, direction, shape)
        places = anchor[direction] + jnp.arange(shape[direction], dtype=jnp.int32)
        inside = (places >= 0) & (places < extent[direction] - 1)
        layout = [1, 1, 1]
        layout[direction] = shape[direction]
        inside = inside.reshape(layout)
        slopes.append(jnp.where(inside, ahead_cells - here_cells, jnp.zeros_like(here_cells)))
    weight = lax.rsqrt(
        smooth_floor + slopes[0] * slopes[0] + slopes[1] * slopes[1] + slopes[2] * slopes[2]
    )
    fluxes = [slope_part * weight for slope_part in slopes]
    spread = (
        fluxes[0][1:, 1:, 1:]
        - fluxes[0][:-1, 1:, 1:]
        + (fluxes[1][1:, 1:, 1:] - fluxes[1][1:, :-1, 1:])
        + (fluxes[2][1:, 1:, 1:] - fluxes[2][1:, 1:, :-1])
    )
    center = padded[1:-1, 1:-1, 1:-1]
    return center + relax_rate * (source - center + smooth_weight * spread)


def solve_definite(matrix, right_side):
    factor_lower = jnp.linalg.cholesky(matrix)
    half_solved = lax.linalg.triangular_solve(factor_lower, right_side, left_side=True, lower=True)
    return lax.linalg.triangular_solve(
        factor_lower, half_solved, left_side=True, lower=True, transpose_a=True
    )


def local(video, multiplier, foreground, basis, coefficients):
    highest = lax.Precision.HIGHEST
    frames_here, rows_here, cols_here = video.shape
    rank_size = basis.shape[0]
    frame_count = lax.axis_size("frame")
    row_count = lax.axis_size("row")
    col_count = lax.axis_size("col")
    extent = (frames_here * frame_count, rows_here * row_count, cols_here * col_count)
    frame_slot = lax.axis_index("frame")
    corner = (
        frame_slot * frames_here,
        lax.axis_index("row") * rows_here,
        lax.axis_index("col") * cols_here,
    )
    pixels = rows_here * cols_here
    flat_basis = basis.reshape(rank_size, pixels)
    background = jnp.dot(coefficients, flat_basis, precision=highest).reshape(video.shape)
    target = video - background + dual_scale * multiplier
    current = foreground
    for sweep in range(PASSES):
        padded = with_halo(current, (("row", 1), ("col", 2), ("frame", 0)), 1)
        current = descend(padded, target, tuple((start_cell - 1 for start_cell in corner)), extent)
    shrunk = current - jnp.clip(current, -shrink_level, shrink_level)
    residual_target = video + dual_scale * multiplier - shrunk
    flat_target = residual_target.reshape(frames_here, pixels)
    gram_part = jnp.dot(flat_basis, flat_basis.T, precision=highest)
    cross_part = jnp.dot(flat_basis, flat_target.T, precision=highest)
    gram_sum, cross_sum = lax.psum((gram_part, cross_part), ("row", "col"))
    identity_matrix = jnp.eye(rank_size, dtype=gram_sum.dtype)
    pixel_ridge = ridge_share * pixels * row_count * col_count
    coeff_rows = solve_definite(
        gram_sum + pixel_ridge * identity_matrix, cross_sum + pixel_ridge * coefficients.T
    )
    total_part = jnp.dot(coeff_rows, flat_target, precision=highest).reshape(
        rank_size, rows_here, cols_here
    )
    frame_gram_part = jnp.dot(coeff_rows, coeff_rows.T, precision=highest)
    owned_rows = rows_here // frame_count
    owned_sums = lax.psum_scatter(total_part, "frame", scatter_dimension=1, tiled=True)
    frame_gram = lax.psum(frame_gram_part, "frame")
    old_owned = lax.dynamic_slice_in_dim(basis, frame_slot * owned_rows, owned_rows, 1)
    frame_ridge = ridge_share * frames_here * frame_count
    right_side = (owned_sums + frame_ridge * old_owned).reshape(rank_size, owned_rows * cols_here)
    new_basis = solve_definite(frame_gram + frame_ridge * identity_matrix, right_side)
    return (shrunk, coeff_rows.T, new_basis.reshape(rank_size, owned_rows, cols_here))


MESH = pl.DeviceIdType.MESH
CHUNK = 24
SEGMENTS = 4


def eliminate(matrix, size):
    lanes = lax.broadcasted_iota(jnp.int32, matrix.shape, 1)
    rows = lax.broadcasted_iota(jnp.int32, matrix.shape, 0)
    for k in range(size):
        pivot = matrix[k : k + 1, k : k + 1]
        scaled = matrix[k : k + 1, :] / pivot
        column = jnp.sum(jnp.where(lanes == k, matrix, 0.0), axis=1, keepdims=True)
        matrix = jnp.where(rows == k, scaled, matrix - column * scaled)
    return matrix


def kernel(
    sizes, coeff_hbm, video_hbm, mult_hbm, fore_hbm, basis_hbm,
    result, coeff_out, fresh,
    field0, field1, field2, video, mult, basis, anchor, target, owned,
    packed, arrived, corner, edge_next, edge_flux, first_cols, left_now, left_next, bottom_row,
    cross, sums, grams, gram_parts, inverse, parts, shares, square, table, coeff_ref, table_smem,
):
    field = (field0, field1, field2)
    F, H, W, rank, nr, nc, nz = sizes
    r = lax.axis_index("row")
    c = lax.axis_index("col")
    z = lax.axis_index("frame")
    own = H // nz
    pieces = own // CHUNK
    half = H // 2
    flip = lax.rem(r, 2)

    steps = H // CHUNK

    def chunk_at(step):
        return step + flip * (steps - 1 - 2 * step)

    def rows_at(step, offset=0):
        return pl.ds(pl.multiple_of(offset + chunk_at(step) * CHUNK, 8), CHUNK)

    span = H // SEGMENTS
    per = steps // SEGMENTS

    def segment_start(j):
        return pl.multiple_of((j + flip * (SEGMENTS - 1 - 2 * j)) * span, 8)

    def half_start(h):
        return pl.multiple_of((h + flip * (1 - 2 * h)) * half, 8)

    inner = (z > 0) & (z < nz - 1)

    def inside(dr, dc, dz):
        ok = None
        for at, step, count in ((r, dr, nr), (c, dc, nc), (z, dz, nz)):
            if step != 0:
                test = (at + step >= 0) & (at + step < count)
                ok = test if ok is None else ok & test
        return ok

    def work(
        in_sems, halo_send, halo_recv, part_send, part_recv, gram_send, gram_recv,
        total_send, total_recv, share_send, share_recv, small_sem, move_send, move_recv,
    ):
        def take(source, piece):
            rows = pl.ds(pl.multiple_of(z * own + piece * CHUNK, 8), CHUNK)
            spot = pl.ds(pl.multiple_of(piece * CHUNK, 8), CHUNK)
            return pltpu.make_async_remote_copy(
                src_ref=anchor.at[:, rows, :], dst_ref=owned.at[pl.ds(source * F, F), spot, :],
                send_sem=move_send.at[source], recv_sem=move_recv.at[source, piece],
                device_id=(r, c, source), device_id_type=MESH,
            )

        halves = [pl.ds(half_start(h), half) for h in range(2)]
        loads = [
            pltpu.make_async_copy(src, dst, in_sems.at[i])
            for i, (src, dst) in enumerate(
                [
                    (
                        fore_hbm.at[:, halves[h], :],
                        field0.at[1 : F + 1, pl.ds(pl.multiple_of(half_start(h) + 8, 8), half), :],
                    )
                    for h in range(2)
                ]
                + [(coeff_hbm, coeff_ref)]
                + [
                    (src.at[:, rows, :], dst.at[:, rows, :])
                    for rows in halves
                    for src, dst in ((video_hbm, video), (mult_hbm, mult), (basis_hbm, basis))
                ]
            )
        ]
        barrier = pltpu.get_barrier_semaphore()
        beside = ((0, 0, 1), (0, 1, 0), (1, 0, 0), (1, 0, -1), (0, 1, -1), (1, -1, 0))
        beside += tuple(tuple(-s for s in step) for step in beside)
        for step in beside:
            @pl.when(inside(*step))
            def _(step=step):
                pl.semaphore_signal(
                    barrier,
                    inc=1,
                    device_id=(r + step[0], c + step[1], z + step[2]),
                    device_id_type=MESH,
                )
        expected = jnp.int32(0)
        for step in beside:
            expected = expected + inside(*step).astype(jnp.int32)
        for load in loads:
            load.start()

        pl.semaphore_wait(barrier, expected)

        lane_h = lax.broadcasted_iota(jnp.int32, (span, 128), 1)

        def pack_columns(k, j):
            base = segment_start(j)
            tile = jnp.zeros((span, 128), jnp.float32)
            for f in range(F):
                for lane, at in ((f, 0), (8 + f, W - 1)):
                    lanes = field[k][f + 1, pl.ds(base + 8, span), (at // 128) * 128 : (at // 128) * 128 + 128]
                    tile = jnp.where(lane_h == lane, lanes[:, at % 128 : at % 128 + 1], tile)
            first_cols[pl.ds(base + 8, span), :] = tile
            packed[k, j] = tile.T[:16, :]

        strips = range(4)
        corners = (4, 5)

        def column_list(k, j):
            return (
                (packed.at[k, j, 0:F], arrived.at[k, j, 1 : F + 1], (0, -1, 0)),
                (packed.at[k, j, 8 : 8 + F], arrived.at[k, j, 8 : 8 + F], (0, 1, 0)),
                (packed.at[k, j, F - 1 : F], arrived.at[k, j, 0:1], (0, -1, 1)),
                (packed.at[k, j, 8:9], arrived.at[k, j, 8 + F : 9 + F], (0, 1, -1)),
            )

        def halo_list(k):
            fk = field[k]
            mid = slice(1, F + 1)
            return (
                (fk.at[mid, H : H + 8, :], fk.at[mid, 0:8, :], (1, 0, 0)),
                (fk.at[mid, 8:16, :], fk.at[mid, H + 8 : H + 16, :], (-1, 0, 0)),
                (fk.at[F, 8:9, :], fk.at[0, H + 8 : H + 9, :], (-1, 0, 1)),
                (fk.at[1, H + 7 : H + 8, :], fk.at[F + 1, 7:8, :], (1, 0, -1)),
                (fk.at[mid, H : H + 8, 0:128], corner.at[k, 0], (1, -1, 0)),
                (fk.at[mid, 8:16, W - 128 : W], corner.at[k, 1], (-1, 1, 0)),
            )

        def halo_copy(k, i, leave, src, dst, step):
            return pltpu.make_async_remote_copy(
                src_ref=src, dst_ref=dst,
                send_sem=halo_send.at[k % 2, leave], recv_sem=halo_recv.at[k % 2, i],
                device_id=(r + step[0], c + step[1], z + step[2]), device_id_type=MESH,
            )

        def send_columns(k, j):
            for i, (src, dst, step) in enumerate(column_list(k, j)):
                @pl.when(inside(*step))
                def _(i=i, src=src, dst=dst, step=step):
                    halo_copy(k, 3 + 2 * j + i % 2, 3 + i, src, dst, step).start()

        def wait_columns(k, j):
            for side, step, corner_step, small, large in (
                (0, (0, -1, 0), (0, -1, 1), slice(1, F + 1), slice(0, F + 1)),
                (1, (0, 1, 0), (0, 1, -1), slice(8, 8 + F), slice(8, 9 + F)),
            ):
                near = inside(*(-s for s in step))
                both = inside(*(-s for s in corner_step))
                for turn, rows in ((near & ~both, small), (both, large)):
                    @pl.when(turn)
                    def _(side=side, step=step, rows=rows):
                        ref = arrived.at[k, j, rows]
                        halo_copy(k, 3 + 2 * j + side, 0, ref, ref, step).wait_recv()

        def face(k, step, up):
            fk = field[k]
            rows = rows_at(step, 8)
            at = 3 + 2 * SEGMENTS + step
            mine, theirs = (F, 0) if up else (1, F + 1)
            src = fore_hbm.at[mine - 1, rows_at(step)] if k == 0 else fk.at[mine, rows]
            return halo_copy(
                k, at, 7 if up else 8, src, fk.at[theirs, rows], (0, 0, 1 if up else -1)
            )

        def send_faces(k, low, high):
            @pl.loop(low, high)
            def _(step):
                for up in (True, False):
                    @pl.when(inside(0, 0, 1 if up else -1))
                    def _(up=up):
                        face(k, step, up).start()

        def wait_face(k, step):
            for turn, frames in ((inner, slice(0, 2)), (~inner, slice(0, 1))):
                @pl.when(turn)
                def _(frames=frames):
                    ref = field[k].at[frames, rows_at(step, 8), :]
                    halo_copy(k, 3 + 2 * SEGMENTS + step, 0, ref, ref, (0, 0, 1)).wait_recv()

        def send_halos(k, which):
            every = halo_list(k)
            for i in which:
                src, dst, step = every[i]

                @pl.when(inside(*step))
                def _(i=i, src=src, dst=dst, step=step):
                    halo_copy(k, i // 2, i // 2, src, dst, step).start()

        def wait_halos(k, which):
            every = halo_list(k)
            for i in which:
                src, dst, step = every[i]

                @pl.when(inside(*(-s for s in step)))
                def _(i=i, src=src, dst=dst, step=step):
                    halo_copy(k, i // 2, i // 2, src, dst, step).wait_recv()

        def finish_sends(k):
            for i, (src, dst, step) in enumerate(halo_list(k)):
                @pl.when(inside(*step))
                def _(i=i, src=src, dst=dst, step=step):
                    halo_copy(k, i // 2, i // 2, src, dst, step).wait_send()

            every = (
                (packed.at[k, :, 0:F], arrived.at[k, :, 1 : F + 1], (0, -1, 0)),
                (packed.at[k, :, 8 : 8 + F], arrived.at[k, :, 8 : 8 + F], (0, 1, 0)),
                (packed.at[k, :, F - 1 : F], arrived.at[k, :, 0:1], (0, -1, 1)),
                (packed.at[k, :, 8:9], arrived.at[k, :, 8 + F : 9 + F], (0, 1, -1)),
                (field[k].at[F, 8 : H + 8, :], field[k].at[0, 8 : H + 8, :], (0, 0, 1)),
                (field[k].at[1, 8 : H + 8, :], field[k].at[F + 1, 8 : H + 8, :], (0, 0, -1)),
            )
            for i, (src, dst, step) in enumerate(every):
                @pl.when(inside(*step))
                def _(i=i, src=src, dst=dst, step=step):
                    halo_copy(k, 0, 3 + i, src, dst, step).wait_send()

        def prepare_columns(k, j):
            base = segment_start(j)
            spread = jnp.concatenate(
                [arrived[k, j], jnp.zeros((112, span), jnp.float32)], axis=0
            ).T
            edge_next[pl.ds(base + 8, span), :] = spread
            left_now[pl.ds(base + 8, span), :] = pltpu.roll(spread, 120, 1)
            left_next[pl.ds(base + 8, span), :] = pltpu.roll(spread, 119, 1)
            low, count = pl.multiple_of(base + 8 * flip, 8), span + 8
            here = left_now[pl.ds(low, count), :]
            ahead = left_next[pl.ds(low, count), :]
            lane = lax.broadcasted_iota(jnp.int32, (count, 128), 1)
            row = lax.broadcasted_iota(jnp.int32, (count, 128), 0) + (low - 8)
            slope0 = jnp.where((lane == F - 1) & (z == nz - 1), 0.0, ahead - here)
            after = left_now[pl.ds(low, count + 8), :]
            below = jnp.where(
                row == H - 1, bottom_row[0:1, :], pltpu.roll(after, count + 7, 0)[:count]
            )
            slope1 = jnp.where((row == H - 1) & (r == nr - 1), 0.0, below - here)
            slope2 = first_cols[pl.ds(low, count), :] - here
            weight = lax.rsqrt(smooth_floor + slope0 * slope0 + slope1 * slope1 + slope2 * slope2)
            edge_flux[pl.ds(low, count), :] = jnp.where(c == 0, 0.0, slope2 * weight)

        def take_corners(k):
            wait_halos(k, corners)
            lane8 = lax.broadcasted_iota(jnp.int32, (8, 128), 1)
            top = jnp.zeros((8, 128), jnp.float32)
            bottom = jnp.zeros((8, 128), jnp.float32)
            for f in range(F):
                top = jnp.where(lane8 == f + 1, corner[k, 0, f][:, 0:1], top)
                bottom = jnp.where(lane8 == f, corner[k, 1, f][:, 127:128], bottom)
            edge_next[0:8, :] = top
            bottom_row[...] = bottom

        def sweep(k, last, start):
            R = CHUNK
            tiles = W // 128
            row_8 = lax.broadcasted_iota(jnp.int32, (8, 128), 0) + (r * H + start)
            above_image = row_8 - 8 < 0
            last_image_row = row_8 + (R - 8) >= nr * H - 1
            columns = edge_next[pl.ds(start, R + 8), :]
            fluxes_in = edge_flux[pl.ds(start + 8, R), :]
            at = pl.ds(start, R)

            def frame(f):
                return [
                    field[k][f, pl.ds(start, R + 16), w * 128 : w * 128 + 128] for w in range(tiles)
                ]

            now = frame(0)
            flux0_before = None
            for f in range(-1, F):
                after = frame(f + 2)
                skip = 8 if f < 0 else 0
                n = R + 8 - skip
                lane = lax.broadcasted_iota(jnp.int32, (n, 128), 1)
                here = [t[skip : R + 8] for t in now]
                turned = [pltpu.roll(t, 127, 1) for t in here]
                wall = jnp.broadcast_to(columns[skip:, f + 1 : f + 2], (n, 128))
                flux0, flux1, flux2 = [], [], []
                for w in range(tiles):
                    slope0 = after[w][skip : R + 8] - here[w]
                    if f == F - 1:
                        slope0 = jnp.where(z == nz - 1, 0.0, slope0)
                    slope1 = pltpu.roll(now[w][skip:], n + 7, 0)[:n] - here[w]
                    slope1 = jnp.concatenate(
                        [slope1[: n - 8], jnp.where(last_image_row, 0.0, slope1[n - 8 :])], axis=0
                    )
                    beyond = turned[w + 1] if w + 1 < tiles else wall
                    slope2 = jnp.where(lane == 127, beyond, turned[w]) - here[w]
                    if w + 1 == tiles:
                        slope2 = jnp.where((lane == 127) & (c == nc - 1), 0.0, slope2)
                    weight = lax.rsqrt(
                        smooth_floor + slope0 * slope0 + slope1 * slope1 + slope2 * slope2
                    )
                    flux0.append((slope0 * weight)[8 - skip :])
                    if f >= 0:
                        flux = slope1 * weight
                        flux1.append(
                            jnp.concatenate(
                                [jnp.where(above_image, 0.0, flux[:8]), flux[8:]], axis=0
                            )
                        )
                        flux2.append((slope2 * weight)[8:])
                if f < 0:
                    flux0 = [jnp.where(z == 0, 0.0, t) for t in flux0]
                else:
                    moved = [pltpu.roll(t, 1, 1) for t in flux2]
                    entry = jnp.broadcast_to(fluxes_in[:, f : f + 1], (R, 128))
                    lane = lax.broadcasted_iota(jnp.int32, (R, 128), 1)
                    for w in range(tiles):
                        left = jnp.where(lane == 0, moved[w - 1] if w > 0 else entry, moved[w])
                        above = pltpu.roll(flux1[w], 1, 0)[8:]
                        spread = (flux0[w] - flux0_before[w]) + (flux1[w][8:] - above) + (flux2[w] - left)
                        lanes = slice(w * 128, w * 128 + 128)
                        value = (1.0 - relax_rate) * here[w][8:] + (
                            target[f, at, lanes] + (relax_rate * smooth_weight) * spread
                        )
                        if last:
                            shrunk = value - jnp.clip(value, -shrink_level, shrink_level)
                            result[f, at, lanes] = shrunk
                            anchor[f, at, lanes] = anchor[f, at, lanes] - shrunk
                        else:
                            field[k + 1][f + 1, pl.ds(start + 8, R), lanes] = value
                flux0_before = flux0
                now = after

        def products(left_of, right_of, lefts, rights, first, count, start, store):
            def body(step, totals):
                rows = pl.ds(pl.multiple_of(first + step * 8, 8), 8)
                a = [left_of[i, rows, :] for i in lefts]
                b = [right_of[j, rows, :] for j in rights]
                out = []
                for x in range(len(lefts)):
                    for y in range(len(rights)):
                        prod = a[x] * b[y]
                        total = totals[len(out)]
                        for w in range(W // 128):
                            total = total + prod[:, w * 128 : w * 128 + 128]
                        out.append(total)
                return tuple(out)

            totals = lax.fori_loop(
                0, count // 8, body, tuple(start(i, j) for i in lefts for j in rights), unroll=3 if count % 24 == 0 else 1
            )
            n = 0
            for i in lefts:
                for j in rights:
                    store(i, j, totals[n])
                    n += 1

        def held(block):
            return (block - z >= 2) | (z - block >= 2)

        def move(block, piece):
            rows = pl.ds(pl.multiple_of(block * own + piece * CHUNK, 8), CHUNK)
            spot = pl.ds(pl.multiple_of(piece * CHUNK, 8), CHUNK)
            return pltpu.make_async_remote_copy(
                src_ref=anchor.at[:, rows, :], dst_ref=owned.at[pl.ds(z * F, F), spot, :],
                send_sem=move_send.at[block], recv_sem=move_recv.at[z, piece],
                device_id=(r, c, block), device_id_type=MESH,
            )

        send_faces(0, 0, 1)
        for j in range(SEGMENTS):
            if j % (SEGMENTS // 2) == 0:
                loads[j // (SEGMENTS // 2)].wait()
            pack_columns(0, j)
            send_columns(0, j)
            if j == SEGMENTS // 2:
                send_halos(0, strips)
                send_halos(0, corners)
            send_faces(0, max(1, j * per), (j + 1) * per)

        zero_tile = jnp.zeros((8, 128), jnp.float32)

        def store_gram(i, j, value):
            row = jnp.sum(value, axis=0, keepdims=True)
            sums[j, i : i + 1, :] = row
            if i // 4 != j // 4:
                sums[i, j : j + 1, :] = row

        lane_r = lax.broadcasted_iota(jnp.int32, (rank, 128), 1)
        row_r = lax.broadcasted_iota(jnp.int32, (rank, 128), 0)

        def gram_share():
            for i in range(0, rank, 4):
                for j in range(i, rank, 4):
                    products(
                        basis, basis, range(i, i + 4), range(j, j + 4), z * own, own,
                        lambda i, j: zero_tile, store_gram,
                    )
            tile = jnp.zeros((rank, 128), jnp.float32)
            for q in range(rank):
                tile = jnp.where(lane_r == q, jnp.sum(sums[q], axis=1, keepdims=True), tile)
            lane = lax.broadcasted_iota(jnp.int32, (8, 128), 1)
            tile = jnp.where(lane < rank, tile[:8], pltpu.roll(tile[8:], rank, 1))
            tile = jnp.where(lane < 2 * rank, tile, pltpu.roll(pltpu.roll(tile, 4, 0), 2 * rank, 1))
            tile = jnp.where(lane < 4 * rank, tile, pltpu.roll(pltpu.roll(tile, 6, 0), 4 * rank, 1))
            grams[z] = tile

        def unfold(tile):
            row = lax.broadcasted_iota(jnp.int32, (8, 128), 0)
            tile = jnp.where(row < 2, tile, pltpu.roll(pltpu.roll(tile, 2, 0), 128 - 4 * rank, 1))
            tile = jnp.where(row < 4, tile, pltpu.roll(pltpu.roll(tile, 4, 0), 128 - 2 * rank, 1))
            tile = jnp.concatenate([tile, pltpu.roll(tile, 128 - rank, 1)], axis=0)
            return jnp.where(lane_r < rank, tile, 0.0)

        def all_sent(block, sem):
            return pltpu.make_async_remote_copy(
                src_ref=block, dst_ref=block, send_sem=sem.at[0], recv_sem=sem.at[0],
                device_id=(r, c, lax.rem(z + 1, nz)), device_id_type=MESH,
            )

        def all_here(block, sem):
            return pltpu.make_async_remote_copy(
                src_ref=block, dst_ref=block, send_sem=sem.at[0], recv_sem=sem.at[0],
                device_id=(r, c, lax.rem(z + 1, nz)), device_id_type=MESH,
            )

        def share_gram(d):
            return pltpu.make_async_remote_copy(
                src_ref=grams.at[z, 0:2], dst_ref=grams.at[z, 0:2],
                send_sem=gram_send.at[0], recv_sem=gram_recv.at[0],
                device_id=(r, c, lax.rem(z + d, nz)), device_id_type=MESH,
            )

        group = nr * nc
        me = r * nc + c

        def share_total(d):
            other = lax.rem(me + d, group)
            return pltpu.make_async_remote_copy(
                src_ref=gram_parts.at[me, 0:2], dst_ref=gram_parts.at[me, 0:2],
                send_sem=total_send.at[0], recv_sem=total_recv.at[0],
                device_id=(other // nc, lax.rem(other, nc), z), device_id_type=MESH,
            )

        def store_cross(i, j, value):
            cross[j, i] = value

        def find_target(h):
            for load in loads[3 + 3 * h : 6 + 3 * h]:
                load.wait()

            @pl.loop(0, half // 8)
            def _(step):
                rows = pl.ds(pl.multiple_of(half_start(h) + step * 8, 8), 8)
                totals = [None] * F
                for q in range(rank):
                    plane = basis[q, rows, :]
                    for f in range(F):
                        term = coeff_ref[f, q] * plane
                        totals[f] = term if totals[f] is None else totals[f] + term
                for f in range(F):
                    lifted = dual_scale * mult[f, rows, :]
                    anchor[f, rows, :] = video[f, rows, :] + lifted
                    target[f, rows, :] = relax_rate * (video[f, rows, :] - totals[f] + lifted)

        loads[2].wait()
        find_target(0)
        find_target(1)
        gram_share()

        def advance(k, step):
            start = pl.multiple_of(chunk_at(step) * CHUNK, 8)
            sweep(k, k == PASSES - 1, start)
            if k == PASSES - 1:
                place, piece = chunk_at(step) // pieces, lax.rem(chunk_at(step), pieces)

                @pl.when((place - z == 1) | (z - place == 1))
                def _():
                    move(place, piece).start()

                for i in range(0, rank, 4):
                    products(
                        basis, anchor, range(i, i + 4), range(F), start, CHUNK,
                        lambda i, j: cross[j, i], store_cross,
                    )

        cross[...] = jnp.zeros_like(cross)
        bottom_row[...] = jnp.zeros_like(bottom_row)
        for k in range(PASSES):
            last = k == PASSES - 1
            if k > 0 and not last:
                finish_sends(k - 1)
            wait_columns(k, 0)
            prepare_columns(k, 0)
            wait_face(k, 0)

            @pl.loop(0, SEGMENTS)
            def _(j, k=k, last=last):
                @pl.loop(j * per, (j + 1) * per - 1)
                def _(step):
                    wait_face(k, step + 1)
                    advance(k, step)

                final = j == SEGMENTS - 1
                if k == PASSES - 2:
                    @pl.when(j == 1)
                    def _():
                        for d in range(1, nz):
                            share_gram(d).start()
                if k == PASSES - 1:
                    @pl.when(j == 1)
                    def _():
                        all_here(grams.at[0 : nz - 1, 0:2], gram_recv).wait_recv()
                        total = grams[0]
                        for i in range(1, nz):
                            total = total + grams[i]
                        gram_parts[me] = total
                        for d in range(1, group):
                            share_total(d).start()

                @pl.when(j == SEGMENTS - 2)
                def _():
                    take_corners(k)

                @pl.when(~final)
                def _():
                    wait_columns(k, j + 1)
                    prepare_columns(k, j + 1)
                    wait_face(k, (j + 1) * per)

                @pl.when(final)
                def _():
                    wait_halos(k, strips)

                advance(k, (j + 1) * per - 1)
                if not last:
                    @pl.when(final)
                    def _():
                        send_halos(k + 1, strips)
                        send_halos(k + 1, corners)

                    pack_columns(k + 1, j)
                    send_columns(k + 1, j)
                    send_faces(k + 1, j * per, (j + 1) * per)


        def send_held(turn, low, high):
            for b in range(nz):
                @pl.when(held(b) & turn)
                def _(b=b):
                    for p in range(low, high):
                        move(b, p).start()

        for far, near in ((nz - 1, 0), (0, nz - 1)):
            place = far - 1 if far > near else far + 1

            @pl.when((z == near) & held(jnp.int32(place)))
            def _(place=place):
                move(place, 0).start()

        for j in range(F):
            for i in range(rank):
                sums[rank + j, i : i + 1, :] = jnp.sum(cross[j, i], axis=0, keepdims=True)

        part = jnp.zeros((rank, 128), jnp.float32)
        for q in range(rank, rank + F):
            part = jnp.where(lane_r == q, jnp.sum(sums[q], axis=1, keepdims=True), part)
        parts[me] = part

        def share_part(d):
            other = lax.rem(me + d, group)
            return pltpu.make_async_remote_copy(
                src_ref=parts.at[me], dst_ref=parts.at[me],
                send_sem=part_send.at[0], recv_sem=part_recv.at[0],
                device_id=(other // nc, lax.rem(other, nc), z), device_id_type=MESH,
            )

        for d in range(1, group):
            share_part(d).start()
        pixel_ridge = ridge_share * H * W * group
        diagonal = lane_r == row_r
        before = jnp.zeros((rank, 128), jnp.float32)
        for q in range(rank):
            for f in range(F):
                before = jnp.where((row_r == q) & (lane_r == rank + f), coeff_ref[f, q], before)
        all_here(gram_parts.at[0 : group - 1, 0:2], total_recv).wait_recv()
        total = gram_parts[0]
        for i in range(1, group):
            total = total + gram_parts[i]
        diagonal = lane_r == row_r
        system = unfold(total) + jnp.where(
            diagonal, pixel_ridge, jnp.where(lane_r == row_r + rank, 1.0, 0.0)
        )
        system = eliminate(system, rank)
        for q in range(rank):
            inverse[q] = jnp.broadcast_to(system[:, rank + q : rank + q + 1], (rank, 128))
        all_here(parts.at[0 : group - 1], part_recv).wait_recv()
        total = parts[0]
        for i in range(1, group):
            total = total + parts[i]
        total = total + pixel_ridge * before
        solved = inverse[0] * total[0:1, :]
        for q in range(1, rank):
            solved = solved + inverse[q] * total[q : q + 1, :]
        square[...] = jnp.zeros_like(square)
        square[0:rank, :] = solved
        mine = square[...].T[rank : rank + F, :]
        shares[pl.ds(z * F, F), :] = mine

        def share_rows(d):
            return pltpu.make_async_remote_copy(
                src_ref=shares.at[pl.ds(z * F, F)], dst_ref=shares.at[pl.ds(z * F, F)],
                send_sem=share_send.at[0], recv_sem=share_recv.at[0],
                device_id=(r, c, lax.rem(z + d, nz)), device_id_type=MESH,
            )

        for d in range(1, nz):
            share_rows(d).start()

        send_held(inner, 0, pieces)
        coeff_out[...] = mine[:, 0:rank]
        all_here(shares.at[0 : (nz - 1) * F], share_recv).wait_recv()
        for b in range(nz):
            @pl.when(held(b) & ~inner)
            def _(b=b):
                first = jnp.where(((z == 0) & (b == nz - 2)) | ((z == nz - 1) & (b == 1)), 1, 0)

                @pl.loop(first, pieces)
                def _(p):
                    move(b, p).start()

        frames = F * nz
        square[0:frames, :] = shares[...]
        wide = pltpu.roll(square[...].T[0:rank, :], rank, 1)
        square[0:rank, :] = wide
        gram = lax.dot_general(
            wide, square[...], (((1,), (1,)), ((), ())),
            precision=lax.Precision.HIGHEST, preferred_element_type=jnp.float32,
        )
        frame_ridge = ridge_share * frames
        system = jnp.where(diagonal, gram + frame_ridge, gram) + wide
        system = system + jnp.where(lane_r == row_r + rank + frames, frame_ridge, 0.0)
        table[...] = eliminate(system, rank)
        to_scalar = pltpu.make_async_copy(table, table_smem, small_sem.at[0])
        to_scalar.start()
        to_scalar.wait()
        my_base = z * own

        @pl.loop(0, own // 8)
        def _(step):
            rows = pl.ds(pl.multiple_of(step * 8, 8), 8)
            old = pl.ds(pl.multiple_of(my_base + step * 8, 8), 8)
            for half in range(0, rank, 8):
                totals = [None] * 8
                for f in range(F + rank):
                    plane = anchor[f, old, :] if f < F else basis[f - F, old, :]
                    place = rank + z * F + f if f < F else rank + frames + f - F
                    for q in range(8):
                        term = table_smem[half + q, place] * plane
                        totals[q] = term if totals[q] is None else totals[q] + term
                for q in range(8):
                    fresh[half + q, rows, :] = totals[q]

        for k in range(PASSES - 2, PASSES):
            finish_sends(k)
        all_sent(shares.at[0 : (nz - 1) * F], share_send).wait_send()
        all_sent(grams.at[0 : nz - 1, 0:2], gram_send).wait_send()
        all_sent(gram_parts.at[0 : group - 1, 0:2], total_send).wait_send()
        all_sent(parts.at[0 : group - 1], part_send).wait_send()

        for n in range(nz - 1):
            near = n + (n >= z).astype(jnp.int32)
            far = nz - 1 - (n + (n >= nz - 1 - z).astype(jnp.int32))
            distance = 1 if n == 0 else nz - n
            source = jnp.where(2 * z < nz, near, far)
            source = jnp.where(z == 0, distance, jnp.where(z == nz - 1, nz - 1 - distance, source))

            @pl.loop(0, pieces)
            def _(piece, source=source):
                take(source, piece).wait_recv()
                for step in range(CHUNK // 8):
                    rows = pl.ds(pl.multiple_of(piece * CHUNK + step * 8, 8), 8)
                    planes = [owned[source * F + f, rows, :] for f in range(F)]
                    for q in range(rank):
                        value = fresh[q, rows, :]
                        for f in range(F):
                            value = value + table_smem[q, rank + source * F + f] * planes[f]
                        fresh[q, rows, :] = value

        for b in range(nz):
            @pl.when(z != b)
            def _(b=b):
                rows = pl.ds(b * own, own)
                pltpu.make_async_remote_copy(
                    src_ref=anchor.at[:, rows, :], dst_ref=owned.at[pl.ds(z * F, F)],
                    send_sem=move_send.at[b], recv_sem=move_recv.at[z, 0],
                    device_id=(r, c, b), device_id_type=MESH,
                ).wait_send()

    dma = pltpu.SemaphoreType.DMA
    one = dma((1,))
    pl.run_scoped(
        work,
        dma((9,)),
        dma((2, 9)),
        dma((2, 3 + 2 * SEGMENTS + steps)),
        *(one,) * 9,
        dma((nz,)),
        dma((nz, pieces)),
    )


def deliver(shrunk, coeff, fresh, shrunk_hbm, coeff_hbm, fresh_hbm):
    def work(sems):
        copies = [pltpu.make_async_copy(coeff, coeff_hbm, sems.at[0])]
        for source, place in ((fresh, fresh_hbm), (shrunk, shrunk_hbm)):
            share = source.shape[0] // 1
            for i in range(1):
                part = pl.ds(i * share, share)
                copies.append(
                    pltpu.make_async_copy(source.at[part], place.at[part], sems.at[len(copies)])
                )
        for copy in copies:
            copy.start()
        for copy in copies:
            copy.wait()

    pl.run_scoped(work, pltpu.SemaphoreType.DMA((3,)))


def whole_kernel(video, multiplier, foreground, basis, coefficients):
    F, H, W = video.shape
    rank = basis.shape[0]
    nr, nc, nz = (lax.axis_size(name) for name in ("row", "col", "frame"))
    f32 = jnp.float32
    own = H // nz
    group = nr * nc
    vmem = pltpu.VMEM
    dma = pltpu.SemaphoreType.DMA
    pieces = own // CHUNK
    hbm = pl.BlockSpec(memory_space=pl.ANY)
    on_chip = pl.BlockSpec(memory_space=pltpu.VMEM)
    found = pl.pallas_call(
        functools.partial(kernel, (F, H, W, rank, nr, nc, nz)),
        out_shape=(vmem((F, H, W), f32), vmem((F, rank), f32), vmem((rank, own, W), f32)),
        in_specs=[hbm] * 5,
        out_specs=[on_chip] * 3,
        scratch_shapes=[vmem((F + 2, H + 16, W), f32)] * PASSES
        + [
            vmem((F, H, W), f32),
            vmem((F, H, W), f32),
            vmem((rank, H, W), f32),
            vmem((F, H, W), f32),
            vmem((F, H, W), f32),
            vmem((F * nz, own, W), f32),
            vmem((PASSES, SEGMENTS, 16, H // SEGMENTS), f32),
            vmem((PASSES, SEGMENTS, 16, H // SEGMENTS), f32),
            vmem((PASSES, 2, F, 8, 128), f32),
            vmem((H + 8, 128), f32),
            vmem((H + 16, 128), f32),
            vmem((H + 16, 128), f32),
            vmem((H + 24, 128), f32),
            vmem((H + 24, 128), f32),
            vmem((8, 128), f32),
            vmem((F, rank, 8, 128), f32),
            vmem((rank + F, rank, 128), f32),
            vmem((nz, 8, 128), f32),
            vmem((group, 8, 128), f32),
            vmem((rank, rank, 128), f32),
            vmem((group, rank, 128), f32),
            vmem((nz * F, 128), f32),
            vmem((128, 128), f32),
            vmem((rank, 128), f32),
            pltpu.SMEM((F, rank), f32),
            pltpu.SMEM((rank, 128), f32),
        ],
        compiler_params=pltpu.CompilerParams(
            collective_id=0, has_side_effects=True, vmem_limit_bytes=32 * 1024 * 1024
        ),
    )(
        *(
            pltpu.with_memory_space_constraint(x, pltpu.HBM)
            for x in (coefficients, video, multiplier, foreground, basis)
        )
    )
    return pl.pallas_call(
        deliver,
        out_shape=(
            jax.ShapeDtypeStruct((F, H, W), f32),
            jax.ShapeDtypeStruct((F, rank), f32),
            jax.ShapeDtypeStruct((rank, own, W), f32),
        ),
        in_specs=[on_chip] * 3,
        out_specs=[hbm] * 3,
    )(*(pltpu.with_memory_space_constraint(x, pltpu.VMEM) for x in found))


def body(video, multiplier, foreground, basis, coefficients):
    F, H, W = video.shape
    rank = basis.shape[0]
    nz = lax.axis_size("frame")
    fits = (
        H % nz == 0 and (H // nz) % 8 == 0 and (H // nz) % CHUNK == 0 and W % 128 == 0
        and H % 16 == 0 and H % (SEGMENTS * CHUNK) == 0 and lax.axis_size("row") <= 2
        and F % 4 == 0 and F < 8 and rank == 16 and nz >= 2 and F * nz == rank and 2 * rank + F * nz <= 128
    )
    run = whole_kernel if fits else local
    return run(video, multiplier, foreground, basis, coefficients)


def solution(mesh):
    placed = (
        P("frame", "row", "col"),
        P("frame", "row", "col"),
        P("frame", "row", "col"),
        P(None, "row", "col"),
        P("frame", None),
    )
    return jax.shard_map(
        body,
        mesh=mesh,
        in_specs=placed,
        out_specs=(P("frame", "row", "col"), P("frame", None), P(None, ("row", "frame"), "col")),
        check_vma=False,
    )
```

```python
import functools

import jax
import jax.numpy as jnp
from jax import lax
from jax.experimental import pallas as pl
from jax.experimental.pallas import tpu as pltpu
from jax.sharding import PartitionSpec as P

PASSES = 3


relax_rate = 0.8
smooth_weight = 0.5
smooth_floor = 0.25
shrink_level = 0.4
dual_scale = 0.8
ridge_share = 0.1


def with_halo(block, sides, width):
    for axis, dim in sides:
        count = lax.axis_size(axis)
        forward = [(i, i + 1) for i in range(count - 1)]
        backward = [(target, source) for source, target in forward]
        low = lax.ppermute(
            lax.slice_in_dim(block, block.shape[dim] - width, None, axis=dim), axis, forward
        )
        high = lax.ppermute(lax.slice_in_dim(block, 0, width, axis=dim), axis, backward)
        block = jnp.concatenate([low, block, high], axis=dim)
    return block


def forward_cells(padded, direction, shape):
    starts = [0, 0, 0]
    starts[direction] = 1
    limits = [starts[axis_dim] + shape[axis_dim] for axis_dim in range(3)]
    return lax.slice(padded, starts, limits)


def descend(padded, source, anchor, extent):
    shape = tuple((int(length) - 1 for length in padded.shape))
    here_cells = padded[:-1, :-1, :-1]
    slopes = []
    for direction in range(3):
        ahead_cells = forward_cells(padded, direction, shape)
        places = anchor[direction] + jnp.arange(shape[direction], dtype=jnp.int32)
        inside = (places >= 0) & (places < extent[direction] - 1)
        layout = [1, 1, 1]
        layout[direction] = shape[direction]
        inside = inside.reshape(layout)
        slopes.append(jnp.where(inside, ahead_cells - here_cells, jnp.zeros_like(here_cells)))
    weight = lax.rsqrt(
        smooth_floor + slopes[0] * slopes[0] + slopes[1] * slopes[1] + slopes[2] * slopes[2]
    )
    fluxes = [slope_part * weight for slope_part in slopes]
    spread = (
        fluxes[0][1:, 1:, 1:]
        - fluxes[0][:-1, 1:, 1:]
        + (fluxes[1][1:, 1:, 1:] - fluxes[1][1:, :-1, 1:])
        + (fluxes[2][1:, 1:, 1:] - fluxes[2][1:, 1:, :-1])
    )
    center = padded[1:-1, 1:-1, 1:-1]
    return center + relax_rate * (source - center + smooth_weight * spread)


def solve_definite(matrix, right_side):
    factor_lower = jnp.linalg.cholesky(matrix)
    half_solved = lax.linalg.triangular_solve(factor_lower, right_side, left_side=True, lower=True)
    return lax.linalg.triangular_solve(
        factor_lower, half_solved, left_side=True, lower=True, transpose_a=True
    )


def local(video, multiplier, foreground, basis, coefficients):
    highest = lax.Precision.HIGHEST
    frames_here, rows_here, cols_here = video.shape
    rank_size = basis.shape[0]
    frame_count = lax.axis_size("frame")
    row_count = lax.axis_size("row")
    col_count = lax.axis_size("col")
    extent = (frames_here * frame_count, rows_here * row_count, cols_here * col_count)
    frame_slot = lax.axis_index("frame")
    corner = (
        frame_slot * frames_here,
        lax.axis_index("row") * rows_here,
        lax.axis_index("col") * cols_here,
    )
    pixels = rows_here * cols_here
    flat_basis = basis.reshape(rank_size, pixels)
    background = jnp.dot(coefficients, flat_basis, precision=highest).reshape(video.shape)
    target = video - background + dual_scale * multiplier
    current = foreground
    for sweep in range(PASSES):
        padded = with_halo(current, (("row", 1), ("col", 2), ("frame", 0)), 1)
        current = descend(padded, target, tuple((start_cell - 1 for start_cell in corner)), extent)
    shrunk = current - jnp.clip(current, -shrink_level, shrink_level)
    residual_target = video + dual_scale * multiplier - shrunk
    flat_target = residual_target.reshape(frames_here, pixels)
    gram_part = jnp.dot(flat_basis, flat_basis.T, precision=highest)
    cross_part = jnp.dot(flat_basis, flat_target.T, precision=highest)
    gram_sum, cross_sum = lax.psum((gram_part, cross_part), ("row", "col"))
    identity_matrix = jnp.eye(rank_size, dtype=gram_sum.dtype)
    pixel_ridge = ridge_share * pixels * row_count * col_count
    coeff_rows = solve_definite(
        gram_sum + pixel_ridge * identity_matrix, cross_sum + pixel_ridge * coefficients.T
    )
    total_part = jnp.dot(coeff_rows, flat_target, precision=highest).reshape(
        rank_size, rows_here, cols_here
    )
    frame_gram_part = jnp.dot(coeff_rows, coeff_rows.T, precision=highest)
    owned_rows = rows_here // frame_count
    owned_sums = lax.psum_scatter(total_part, "frame", scatter_dimension=1, tiled=True)
    frame_gram = lax.psum(frame_gram_part, "frame")
    old_owned = lax.dynamic_slice_in_dim(basis, frame_slot * owned_rows, owned_rows, 1)
    frame_ridge = ridge_share * frames_here * frame_count
    right_side = (owned_sums + frame_ridge * old_owned).reshape(rank_size, owned_rows * cols_here)
    new_basis = solve_definite(frame_gram + frame_ridge * identity_matrix, right_side)
    return (shrunk, coeff_rows.T, new_basis.reshape(rank_size, owned_rows, cols_here))


MESH = pl.DeviceIdType.MESH
CHUNK = 24
SEGMENTS = 4


def eliminate(matrix, size):
    lanes = lax.broadcasted_iota(jnp.int32, matrix.shape, 1)
    rows = lax.broadcasted_iota(jnp.int32, matrix.shape, 0)
    for k in range(size):
        pivot = matrix[k : k + 1, k : k + 1]
        scaled = matrix[k : k + 1, :] / pivot
        column = jnp.sum(jnp.where(lanes == k, matrix, 0.0), axis=1, keepdims=True)
        matrix = jnp.where(rows == k, scaled, matrix - column * scaled)
    return matrix


def kernel(
    sizes, coeff_hbm, video_hbm, mult_hbm, fore_hbm, basis_hbm,
    result, coeff_out, fresh,
    field0, field1, field2, video, mult, basis, anchor, target, owned,
    packed, arrived, corner, edge_next, edge_flux, first_cols, left_now, left_next, bottom_row,
    cross, sums, grams, gram_parts, inverse, parts, shares, square, table, coeff_ref, table_smem,
):
    field = (field0, field1, field2)
    F, H, W, rank, nr, nc, nz = sizes
    r = lax.axis_index("row")
    c = lax.axis_index("col")
    z = lax.axis_index("frame")
    own = H // nz
    pieces = own // CHUNK
    half = H // 2
    flip = lax.rem(r, 2)

    steps = H // CHUNK

    def chunk_at(step):
        return step + flip * (steps - 1 - 2 * step)

    def rows_at(step, offset=0):
        return pl.ds(pl.multiple_of(offset + chunk_at(step) * CHUNK, 8), CHUNK)

    span = H // SEGMENTS
    per = steps // SEGMENTS

    def segment_start(j):
        return pl.multiple_of((j + flip * (SEGMENTS - 1 - 2 * j)) * span, 8)

    def half_start(h):
        return pl.multiple_of((h + flip * (1 - 2 * h)) * half, 8)

    inner = (z > 0) & (z < nz - 1)

    def inside(dr, dc, dz):
        ok = None
        for at, step, count in ((r, dr, nr), (c, dc, nc), (z, dz, nz)):
            if step != 0:
                test = (at + step >= 0) & (at + step < count)
                ok = test if ok is None else ok & test
        return ok

    def work(
        in_sems, halo_send, halo_recv, part_send, part_recv, gram_send, gram_recv,
        total_send, total_recv, share_send, share_recv, small_sem, move_send, move_recv,
    ):
        def take(source, piece):
            rows = pl.ds(pl.multiple_of(z * own + piece * CHUNK, 8), CHUNK)
            spot = pl.ds(pl.multiple_of(piece * CHUNK, 8), CHUNK)
            return pltpu.make_async_remote_copy(
                src_ref=anchor.at[:, rows, :], dst_ref=owned.at[pl.ds(source * F, F), spot, :],
                send_sem=move_send.at[source], recv_sem=move_recv.at[source, piece],
                device_id=(r, c, source), device_id_type=MESH,
            )

        halves = [pl.ds(half_start(h), half) for h in range(2)]
        loads = [
            pltpu.make_async_copy(src, dst, in_sems.at[i])
            for i, (src, dst) in enumerate(
                [
                    (
                        fore_hbm.at[:, halves[h], :],
                        field0.at[1 : F + 1, pl.ds(pl.multiple_of(half_start(h) + 8, 8), half), :],
                    )
                    for h in range(2)
                ]
                + [(coeff_hbm, coeff_ref)]
                + [
                    (src.at[:, rows, :], dst.at[:, rows, :])
                    for rows in halves
                    for src, dst in ((video_hbm, video), (mult_hbm, mult), (basis_hbm, basis))
                ]
            )
        ]
        for load in loads[:2]:
            load.start()

        barrier = pltpu.get_barrier_semaphore()
        beside = ((0, 0, 1), (0, 1, 0), (1, 0, 0), (1, 0, -1), (0, 1, -1), (1, -1, 0))
        beside += tuple(tuple(-s for s in step) for step in beside)
        for step in beside:
            @pl.when(inside(*step))
            def _(step=step):
                pl.semaphore_signal(
                    barrier,
                    inc=1,
                    device_id=(r + step[0], c + step[1], z + step[2]),
                    device_id_type=MESH,
                )
        expected = jnp.int32(0)
        for step in beside:
            expected = expected + inside(*step).astype(jnp.int32)
        for load in loads[2:]:
            load.start()

        pl.semaphore_wait(barrier, expected)

        lane_h = lax.broadcasted_iota(jnp.int32, (span, 128), 1)

        def pack_columns(k, j):
            base = segment_start(j)
            tile = jnp.zeros((span, 128), jnp.float32)
            for f in range(F):
                for lane, at in ((f, 0), (8 + f, W - 1)):
                    lanes = field[k][f + 1, pl.ds(base + 8, span), (at // 128) * 128 : (at // 128) * 128 + 128]
                    tile = jnp.where(lane_h == lane, lanes[:, at % 128 : at % 128 + 1], tile)
            first_cols[pl.ds(base + 8, span), :] = tile
            packed[k, j] = tile.T[:16, :]

        strips = range(4)
        corners = (4, 5)

        def column_list(k, j):
            return (
                (packed.at[k, j, 0:F], arrived.at[k, j, 1 : F + 1], (0, -1, 0)),
                (packed.at[k, j, 8 : 8 + F], arrived.at[k, j, 8 : 8 + F], (0, 1, 0)),
                (packed.at[k, j, F - 1 : F], arrived.at[k, j, 0:1], (0, -1, 1)),
                (packed.at[k, j, 8:9], arrived.at[k, j, 8 + F : 9 + F], (0, 1, -1)),
            )

        def halo_list(k):
            fk = field[k]
            mid = slice(1, F + 1)
            return (
                (fk.at[mid, H : H + 8, :], fk.at[mid, 0:8, :], (1, 0, 0)),
                (fk.at[mid, 8:16, :], fk.at[mid, H + 8 : H + 16, :], (-1, 0, 0)),
                (fk.at[F, 8:9, :], fk.at[0, H + 8 : H + 9, :], (-1, 0, 1)),
                (fk.at[1, H + 7 : H + 8, :], fk.at[F + 1, 7:8, :], (1, 0, -1)),
                (fk.at[mid, H : H + 8, 0:128], corner.at[k, 0], (1, -1, 0)),
                (fk.at[mid, 8:16, W - 128 : W], corner.at[k, 1], (-1, 1, 0)),
            )

        def halo_copy(k, i, leave, src, dst, step):
            return pltpu.make_async_remote_copy(
                src_ref=src, dst_ref=dst,
                send_sem=halo_send.at[k % 2, leave], recv_sem=halo_recv.at[k % 2, i],
                device_id=(r + step[0], c + step[1], z + step[2]), device_id_type=MESH,
            )

        def send_columns(k, j):
            for i, (src, dst, step) in enumerate(column_list(k, j)):
                @pl.when(inside(*step))
                def _(i=i, src=src, dst=dst, step=step):
                    halo_copy(k, 3 + 2 * j + i % 2, 3 + i, src, dst, step).start()

        def wait_columns(k, j):
            for side, step, corner_step, small, large in (
                (0, (0, -1, 0), (0, -1, 1), slice(1, F + 1), slice(0, F + 1)),
                (1, (0, 1, 0), (0, 1, -1), slice(8, 8 + F), slice(8, 9 + F)),
            ):
                near = inside(*(-s for s in step))
                both = inside(*(-s for s in corner_step))
                for turn, rows in ((near & ~both, small), (both, large)):
                    @pl.when(turn)
                    def _(side=side, step=step, rows=rows):
                        ref = arrived.at[k, j, rows]
                        halo_copy(k, 3 + 2 * j + side, 0, ref, ref, step).wait_recv()

        def face(k, step, up):
            fk = field[k]
            rows = rows_at(step, 8)
            at = 3 + 2 * SEGMENTS + step
            mine, theirs = (F, 0) if up else (1, F + 1)
            src = fore_hbm.at[mine - 1, rows_at(step)] if k == 0 else fk.at[mine, rows]
            return halo_copy(
                k, at, 7 if up else 8, src, fk.at[theirs, rows], (0, 0, 1 if up else -1)
            )

        def send_faces(k, low, high):
            @pl.loop(low, high)
            def _(step):
                for up in (True, False):
                    @pl.when(inside(0, 0, 1 if up else -1))
                    def _(up=up):
                        face(k, step, up).start()

        def wait_face(k, step):
            for turn, frames in ((inner, slice(0, 2)), (~inner, slice(0, 1))):
                @pl.when(turn)
                def _(frames=frames):
                    ref = field[k].at[frames, rows_at(step, 8), :]
                    halo_copy(k, 3 + 2 * SEGMENTS + step, 0, ref, ref, (0, 0, 1)).wait_recv()

        def send_halos(k, which):
            every = halo_list(k)
            for i in which:
                src, dst, step = every[i]

                @pl.when(inside(*step))
                def _(i=i, src=src, dst=dst, step=step):
                    halo_copy(k, i // 2, i // 2, src, dst, step).start()

        def wait_halos(k, which):
            every = halo_list(k)
            for i in which:
                src, dst, step = every[i]

                @pl.when(inside(*(-s for s in step)))
                def _(i=i, src=src, dst=dst, step=step):
                    halo_copy(k, i // 2, i // 2, src, dst, step).wait_recv()

        def finish_sends(k):
            for i, (src, dst, step) in enumerate(halo_list(k)):
                @pl.when(inside(*step))
                def _(i=i, src=src, dst=dst, step=step):
                    halo_copy(k, i // 2, i // 2, src, dst, step).wait_send()

            every = (
                (packed.at[k, :, 0:F], arrived.at[k, :, 1 : F + 1], (0, -1, 0)),
                (packed.at[k, :, 8 : 8 + F], arrived.at[k, :, 8 : 8 + F], (0, 1, 0)),
                (packed.at[k, :, F - 1 : F], arrived.at[k, :, 0:1], (0, -1, 1)),
                (packed.at[k, :, 8:9], arrived.at[k, :, 8 + F : 9 + F], (0, 1, -1)),
                (field[k].at[F, 8 : H + 8, :], field[k].at[0, 8 : H + 8, :], (0, 0, 1)),
                (field[k].at[1, 8 : H + 8, :], field[k].at[F + 1, 8 : H + 8, :], (0, 0, -1)),
            )
            for i, (src, dst, step) in enumerate(every):
                @pl.when(inside(*step))
                def _(i=i, src=src, dst=dst, step=step):
                    halo_copy(k, 0, 3 + i, src, dst, step).wait_send()

        def prepare_columns(k, j):
            base = segment_start(j)
            spread = jnp.concatenate(
                [arrived[k, j], jnp.zeros((112, span), jnp.float32)], axis=0
            ).T
            edge_next[pl.ds(base + 8, span), :] = spread
            left_now[pl.ds(base + 8, span), :] = pltpu.roll(spread, 120, 1)
            left_next[pl.ds(base + 8, span), :] = pltpu.roll(spread, 119, 1)
            low, count = pl.multiple_of(base + 8 * flip, 8), span + 8
            here = left_now[pl.ds(low, count), :]
            ahead = left_next[pl.ds(low, count), :]
            lane = lax.broadcasted_iota(jnp.int32, (count, 128), 1)
            row = lax.broadcasted_iota(jnp.int32, (count, 128), 0) + (low - 8)
            slope0 = jnp.where((lane == F - 1) & (z == nz - 1), 0.0, ahead - here)
            after = left_now[pl.ds(low, count + 8), :]
            below = jnp.where(
                row == H - 1, bottom_row[0:1, :], pltpu.roll(after, count + 7, 0)[:count]
            )
            slope1 = jnp.where((row == H - 1) & (r == nr - 1), 0.0, below - here)
            slope2 = first_cols[pl.ds(low, count), :] - here
            weight = lax.rsqrt(smooth_floor + slope0 * slope0 + slope1 * slope1 + slope2 * slope2)
            edge_flux[pl.ds(low, count), :] = jnp.where(c == 0, 0.0, slope2 * weight)

        def take_corners(k):
            wait_halos(k, corners)
            lane8 = lax.broadcasted_iota(jnp.int32, (8, 128), 1)
            top = jnp.zeros((8, 128), jnp.float32)
            bottom = jnp.zeros((8, 128), jnp.float32)
            for f in range(F):
                top = jnp.where(lane8 == f + 1, corner[k, 0, f][:, 0:1], top)
                bottom = jnp.where(lane8 == f, corner[k, 1, f][:, 127:128], bottom)
            edge_next[0:8, :] = top
            bottom_row[...] = bottom

        def sweep(k, last, start):
            R = CHUNK
            tiles = W // 128
            row_8 = lax.broadcasted_iota(jnp.int32, (8, 128), 0) + (r * H + start)
            above_image = row_8 - 8 < 0
            last_image_row = row_8 + (R - 8) >= nr * H - 1
            columns = edge_next[pl.ds(start, R + 8), :]
            fluxes_in = edge_flux[pl.ds(start + 8, R), :]
            at = pl.ds(start, R)

            def frame(f):
                return [
                    field[k][f, pl.ds(start, R + 16), w * 128 : w * 128 + 128] for w in range(tiles)
                ]

            now = frame(0)
            flux0_before = None
            for f in range(-1, F):
                after = frame(f + 2)
                skip = 8 if f < 0 else 0
                n = R + 8 - skip
                lane = lax.broadcasted_iota(jnp.int32, (n, 128), 1)
                here = [t[skip : R + 8] for t in now]
                turned = [pltpu.roll(t, 127, 1) for t in here]
                wall = jnp.broadcast_to(columns[skip:, f + 1 : f + 2], (n, 128))
                flux0, flux1, flux2 = [], [], []
                for w in range(tiles):
                    slope0 = after[w][skip : R + 8] - here[w]
                    if f == F - 1:
                        slope0 = jnp.where(z == nz - 1, 0.0, slope0)
                    slope1 = pltpu.roll(now[w][skip:], n + 7, 0)[:n] - here[w]
                    slope1 = jnp.concatenate(
                        [slope1[: n - 8], jnp.where(last_image_row, 0.0, slope1[n - 8 :])], axis=0
                    )
                    beyond = turned[w + 1] if w + 1 < tiles else wall
                    slope2 = jnp.where(lane == 127, beyond, turned[w]) - here[w]
                    if w + 1 == tiles:
                        slope2 = jnp.where((lane == 127) & (c == nc - 1), 0.0, slope2)
                    weight = lax.rsqrt(
                        smooth_floor + slope0 * slope0 + slope1 * slope1 + slope2 * slope2
                    )
                    flux0.append((slope0 * weight)[8 - skip :])
                    if f >= 0:
                        flux = slope1 * weight
                        flux1.append(
                            jnp.concatenate(
                                [jnp.where(above_image, 0.0, flux[:8]), flux[8:]], axis=0
                            )
                        )
                        flux2.append((slope2 * weight)[8:])
                if f < 0:
                    flux0 = [jnp.where(z == 0, 0.0, t) for t in flux0]
                else:
                    moved = [pltpu.roll(t, 1, 1) for t in flux2]
                    entry = jnp.broadcast_to(fluxes_in[:, f : f + 1], (R, 128))
                    lane = lax.broadcasted_iota(jnp.int32, (R, 128), 1)
                    for w in range(tiles):
                        left = jnp.where(lane == 0, moved[w - 1] if w > 0 else entry, moved[w])
                        above = pltpu.roll(flux1[w], 1, 0)[8:]
                        spread = (flux0[w] - flux0_before[w]) + (flux1[w][8:] - above) + (flux2[w] - left)
                        lanes = slice(w * 128, w * 128 + 128)
                        value = (1.0 - relax_rate) * here[w][8:] + (
                            target[f, at, lanes] + (relax_rate * smooth_weight) * spread
                        )
                        if last:
                            shrunk = value - jnp.clip(value, -shrink_level, shrink_level)
                            result[f, at, lanes] = shrunk
                            anchor[f, at, lanes] = anchor[f, at, lanes] - shrunk
                        else:
                            field[k + 1][f + 1, pl.ds(start + 8, R), lanes] = value
                flux0_before = flux0
                now = after

        def products(left_of, right_of, lefts, rights, first, count, start, store):
            def body(step, totals):
                rows = pl.ds(pl.multiple_of(first + step * 8, 8), 8)
                a = [left_of[i, rows, :] for i in lefts]
                b = [right_of[j, rows, :] for j in rights]
                out = []
                for x in range(len(lefts)):
                    for y in range(len(rights)):
                        prod = a[x] * b[y]
                        total = totals[len(out)]
                        for w in range(W // 128):
                            total = total + prod[:, w * 128 : w * 128 + 128]
                        out.append(total)
                return tuple(out)

            totals = lax.fori_loop(
                0, count // 8, body, tuple(start(i, j) for i in lefts for j in rights), unroll=3 if count % 24 == 0 else 1
            )
            n = 0
            for i in lefts:
                for j in rights:
                    store(i, j, totals[n])
                    n += 1

        def held(block):
            return (block - z >= 2) | (z - block >= 2)

        def move(block, piece):
            rows = pl.ds(pl.multiple_of(block * own + piece * CHUNK, 8), CHUNK)
            spot = pl.ds(pl.multiple_of(piece * CHUNK, 8), CHUNK)
            return pltpu.make_async_remote_copy(
                src_ref=anchor.at[:, rows, :], dst_ref=owned.at[pl.ds(z * F, F), spot, :],
                send_sem=move_send.at[block], recv_sem=move_recv.at[z, piece],
                device_id=(r, c, block), device_id_type=MESH,
            )

        send_faces(0, 0, 1)
        for j in range(SEGMENTS):
            if j % (SEGMENTS // 2) == 0:
                loads[j // (SEGMENTS // 2)].wait()
            pack_columns(0, j)
            send_columns(0, j)
            if j == SEGMENTS // 2:
                send_halos(0, strips)
                send_halos(0, corners)
            send_faces(0, max(1, j * per), (j + 1) * per)

        zero_tile = jnp.zeros((8, 128), jnp.float32)

        def store_gram(i, j, value):
            row = jnp.sum(value, axis=0, keepdims=True)
            sums[j, i : i + 1, :] = row
            if i // 4 != j // 4:
                sums[i, j : j + 1, :] = row

        lane_r = lax.broadcasted_iota(jnp.int32, (rank, 128), 1)
        row_r = lax.broadcasted_iota(jnp.int32, (rank, 128), 0)

        def gram_share():
            for i in range(0, rank, 4):
                for j in range(i, rank, 4):
                    products(
                        basis, basis, range(i, i + 4), range(j, j + 4), z * own, own,
                        lambda i, j: zero_tile, store_gram,
                    )
            tile = jnp.zeros((rank, 128), jnp.float32)
            for q in range(rank):
                tile = jnp.where(lane_r == q, jnp.sum(sums[q], axis=1, keepdims=True), tile)
            lane = lax.broadcasted_iota(jnp.int32, (8, 128), 1)
            tile = jnp.where(lane < rank, tile[:8], pltpu.roll(tile[8:], rank, 1))
            tile = jnp.where(lane < 2 * rank, tile, pltpu.roll(pltpu.roll(tile, 4, 0), 2 * rank, 1))
            tile = jnp.where(lane < 4 * rank, tile, pltpu.roll(pltpu.roll(tile, 6, 0), 4 * rank, 1))
            grams[z] = tile

        def unfold(tile):
            row = lax.broadcasted_iota(jnp.int32, (8, 128), 0)
            tile = jnp.where(row < 2, tile, pltpu.roll(pltpu.roll(tile, 2, 0), 128 - 4 * rank, 1))
            tile = jnp.where(row < 4, tile, pltpu.roll(pltpu.roll(tile, 4, 0), 128 - 2 * rank, 1))
            tile = jnp.concatenate([tile, pltpu.roll(tile, 128 - rank, 1)], axis=0)
            return jnp.where(lane_r < rank, tile, 0.0)

        def all_sent(block, sem):
            return pltpu.make_async_remote_copy(
                src_ref=block, dst_ref=block, send_sem=sem.at[0], recv_sem=sem.at[0],
                device_id=(r, c, lax.rem(z + 1, nz)), device_id_type=MESH,
            )

        def all_here(block, sem):
            return pltpu.make_async_remote_copy(
                src_ref=block, dst_ref=block, send_sem=sem.at[0], recv_sem=sem.at[0],
                device_id=(r, c, lax.rem(z + 1, nz)), device_id_type=MESH,
            )

        def share_gram(d):
            return pltpu.make_async_remote_copy(
                src_ref=grams.at[z, 0:2], dst_ref=grams.at[z, 0:2],
                send_sem=gram_send.at[0], recv_sem=gram_recv.at[0],
                device_id=(r, c, lax.rem(z + d, nz)), device_id_type=MESH,
            )

        group = nr * nc
        me = r * nc + c

        def share_total(d):
            other = lax.rem(me + d, group)
            return pltpu.make_async_remote_copy(
                src_ref=gram_parts.at[me, 0:2], dst_ref=gram_parts.at[me, 0:2],
                send_sem=total_send.at[0], recv_sem=total_recv.at[0],
                device_id=(other // nc, lax.rem(other, nc), z), device_id_type=MESH,
            )

        def store_cross(i, j, value):
            cross[j, i] = value

        def find_target(h):
            for load in loads[3 + 3 * h : 6 + 3 * h]:
                load.wait()

            @pl.loop(0, half // 8)
            def _(step):
                rows = pl.ds(pl.multiple_of(half_start(h) + step * 8, 8), 8)
                totals = [None] * F
                for q in range(rank):
                    plane = basis[q, rows, :]
                    for f in range(F):
                        term = coeff_ref[f, q] * plane
                        totals[f] = term if totals[f] is None else totals[f] + term
                for f in range(F):
                    lifted = dual_scale * mult[f, rows, :]
                    anchor[f, rows, :] = video[f, rows, :] + lifted
                    target[f, rows, :] = relax_rate * (video[f, rows, :] - totals[f] + lifted)

        loads[2].wait()
        find_target(0)
        find_target(1)
        gram_share()

        def advance(k, step):
            start = pl.multiple_of(chunk_at(step) * CHUNK, 8)
            sweep(k, k == PASSES - 1, start)
            if k == PASSES - 1:
                place, piece = chunk_at(step) // pieces, lax.rem(chunk_at(step), pieces)

                @pl.when((place - z == 1) | (z - place == 1))
                def _():
                    move(place, piece).start()

                for i in range(0, rank, 4):
                    products(
                        basis, anchor, range(i, i + 4), range(F), start, CHUNK,
                        lambda i, j: cross[j, i], store_cross,
                    )

        cross[...] = jnp.zeros_like(cross)
        bottom_row[...] = jnp.zeros_like(bottom_row)
        for k in range(PASSES):
            last = k == PASSES - 1
            if k > 0 and not last:
                finish_sends(k - 1)
            wait_columns(k, 0)
            prepare_columns(k, 0)
            wait_face(k, 0)

            @pl.loop(0, SEGMENTS)
            def _(j, k=k, last=last):
                @pl.loop(j * per, (j + 1) * per - 1)
                def _(step):
                    wait_face(k, step + 1)
                    advance(k, step)

                final = j == SEGMENTS - 1
                if k == PASSES - 2:
                    @pl.when(j == 1)
                    def _():
                        for d in range(1, nz):
                            share_gram(d).start()
                if k == PASSES - 1:
                    @pl.when(j == 1)
                    def _():
                        all_here(grams.at[0 : nz - 1, 0:2], gram_recv).wait_recv()
                        total = grams[0]
                        for i in range(1, nz):
                            total = total + grams[i]
                        gram_parts[me] = total
                        for d in range(1, group):
                            share_total(d).start()

                @pl.when(j == SEGMENTS - 2)
                def _():
                    take_corners(k)

                @pl.when(~final)
                def _():
                    wait_columns(k, j + 1)
                    prepare_columns(k, j + 1)
                    wait_face(k, (j + 1) * per)

                @pl.when(final)
                def _():
                    wait_halos(k, strips)

                advance(k, (j + 1) * per - 1)
                if not last:
                    @pl.when(final)
                    def _():
                        send_halos(k + 1, strips)
                        send_halos(k + 1, corners)

                    pack_columns(k + 1, j)
                    send_columns(k + 1, j)
                    send_faces(k + 1, j * per, (j + 1) * per)


        def send_held(turn, low, high):
            for b in range(nz):
                @pl.when(held(b) & turn)
                def _(b=b):
                    for p in range(low, high):
                        move(b, p).start()

        for far, near in ((nz - 1, 0), (0, nz - 1)):
            place = far - 1 if far > near else far + 1

            @pl.when((z == near) & held(jnp.int32(place)))
            def _(place=place):
                move(place, 0).start()

        for j in range(F):
            for i in range(rank):
                sums[rank + j, i : i + 1, :] = jnp.sum(cross[j, i], axis=0, keepdims=True)

        part = jnp.zeros((rank, 128), jnp.float32)
        for q in range(rank, rank + F):
            part = jnp.where(lane_r == q, jnp.sum(sums[q], axis=1, keepdims=True), part)
        parts[me] = part

        def share_part(d):
            other = lax.rem(me + d, group)
            return pltpu.make_async_remote_copy(
                src_ref=parts.at[me], dst_ref=parts.at[me],
                send_sem=part_send.at[0], recv_sem=part_recv.at[0],
                device_id=(other // nc, lax.rem(other, nc), z), device_id_type=MESH,
            )

        for d in range(1, group):
            share_part(d).start()
        pixel_ridge = ridge_share * H * W * group
        diagonal = lane_r == row_r
        before = jnp.zeros((rank, 128), jnp.float32)
        for q in range(rank):
            for f in range(F):
                before = jnp.where((row_r == q) & (lane_r == rank + f), coeff_ref[f, q], before)
        all_here(gram_parts.at[0 : group - 1, 0:2], total_recv).wait_recv()
        total = gram_parts[0]
        for i in range(1, group):
            total = total + gram_parts[i]
        diagonal = lane_r == row_r
        system = unfold(total) + jnp.where(
            diagonal, pixel_ridge, jnp.where(lane_r == row_r + rank, 1.0, 0.0)
        )
        system = eliminate(system, rank)
        for q in range(rank):
            inverse[q] = jnp.broadcast_to(system[:, rank + q : rank + q + 1], (rank, 128))
        all_here(parts.at[0 : group - 1], part_recv).wait_recv()
        total = parts[0]
        for i in range(1, group):
            total = total + parts[i]
        total = total + pixel_ridge * before
        solved = inverse[0] * total[0:1, :]
        for q in range(1, rank):
            solved = solved + inverse[q] * total[q : q + 1, :]
        square[...] = jnp.zeros_like(square)
        square[0:rank, :] = solved
        mine = square[...].T[rank : rank + F, :]
        shares[pl.ds(z * F, F), :] = mine

        def share_rows(d):
            return pltpu.make_async_remote_copy(
                src_ref=shares.at[pl.ds(z * F, F)], dst_ref=shares.at[pl.ds(z * F, F)],
                send_sem=share_send.at[0], recv_sem=share_recv.at[0],
                device_id=(r, c, lax.rem(z + d, nz)), device_id_type=MESH,
            )

        for d in range(1, nz):
            share_rows(d).start()

        send_held(inner, 0, pieces)
        coeff_out[...] = mine[:, 0:rank]
        all_here(shares.at[0 : (nz - 1) * F], share_recv).wait_recv()
        for end, b in [(0, b) for b in reversed(range(nz))] + [(nz - 1, b) for b in range(nz)]:
            @pl.when(held(b) & (z == end))
            def _(b=b):
                first = jnp.where(((z == 0) & (b == nz - 2)) | ((z == nz - 1) & (b == 1)), 1, 0)

                @pl.loop(first, pieces)
                def _(p):
                    move(b, p).start()

        frames = F * nz
        square[0:frames, :] = shares[...]
        wide = pltpu.roll(square[...].T[0:rank, :], rank, 1)
        square[0:rank, :] = wide
        gram = lax.dot_general(
            wide, square[...], (((1,), (1,)), ((), ())),
            precision=lax.Precision.HIGHEST, preferred_element_type=jnp.float32,
        )
        frame_ridge = ridge_share * frames
        system = jnp.where(diagonal, gram + frame_ridge, gram) + wide
        system = system + jnp.where(lane_r == row_r + rank + frames, frame_ridge, 0.0)
        table[...] = eliminate(system, rank)
        to_scalar = pltpu.make_async_copy(table, table_smem, small_sem.at[0])
        to_scalar.start()
        to_scalar.wait()
        my_base = z * own

        @pl.loop(0, own // 8)
        def _(step):
            rows = pl.ds(pl.multiple_of(step * 8, 8), 8)
            old = pl.ds(pl.multiple_of(my_base + step * 8, 8), 8)
            for half in range(0, rank, 8):
                totals = [None] * 8
                for f in range(F + rank):
                    plane = anchor[f, old, :] if f < F else basis[f - F, old, :]
                    place = rank + z * F + f if f < F else rank + frames + f - F
                    for q in range(8):
                        term = table_smem[half + q, place] * plane
                        totals[q] = term if totals[q] is None else totals[q] + term
                for q in range(8):
                    fresh[half + q, rows, :] = totals[q]

        for k in range(PASSES - 2, PASSES):
            finish_sends(k)
        all_sent(shares.at[0 : (nz - 1) * F], share_send).wait_send()
        all_sent(grams.at[0 : nz - 1, 0:2], gram_send).wait_send()
        all_sent(gram_parts.at[0 : group - 1, 0:2], total_send).wait_send()
        all_sent(parts.at[0 : group - 1], part_send).wait_send()

        for n in range(nz - 1):
            near = n + (n >= z).astype(jnp.int32)
            far = nz - 1 - (n + (n >= nz - 1 - z).astype(jnp.int32))
            distance = 1 if n == 0 else nz - n
            source = jnp.where(2 * z < nz, near, far)
            source = jnp.where(z == 0, distance, jnp.where(z == nz - 1, nz - 1 - distance, source))

            @pl.loop(0, pieces)
            def _(piece, source=source):
                take(source, piece).wait_recv()
                for step in range(CHUNK // 8):
                    rows = pl.ds(pl.multiple_of(piece * CHUNK + step * 8, 8), 8)
                    planes = [owned[source * F + f, rows, :] for f in range(F)]
                    for q in range(rank):
                        value = fresh[q, rows, :]
                        for f in range(F):
                            value = value + table_smem[q, rank + source * F + f] * planes[f]
                        fresh[q, rows, :] = value

        for b in range(nz):
            @pl.when(z != b)
            def _(b=b):
                rows = pl.ds(b * own, own)
                pltpu.make_async_remote_copy(
                    src_ref=anchor.at[:, rows, :], dst_ref=owned.at[pl.ds(z * F, F)],
                    send_sem=move_send.at[b], recv_sem=move_recv.at[z, 0],
                    device_id=(r, c, b), device_id_type=MESH,
                ).wait_send()

    dma = pltpu.SemaphoreType.DMA
    one = dma((1,))
    pl.run_scoped(
        work,
        dma((9,)),
        dma((2, 9)),
        dma((2, 3 + 2 * SEGMENTS + steps)),
        *(one,) * 9,
        dma((nz,)),
        dma((nz, pieces)),
    )


def deliver(shrunk, coeff, fresh, shrunk_hbm, coeff_hbm, fresh_hbm):
    def work(sems):
        copies = [pltpu.make_async_copy(coeff, coeff_hbm, sems.at[0])]
        for source, place in ((fresh, fresh_hbm), (shrunk, shrunk_hbm)):
            share = source.shape[0] // 1
            for i in range(1):
                part = pl.ds(i * share, share)
                copies.append(
                    pltpu.make_async_copy(source.at[part], place.at[part], sems.at[len(copies)])
                )
        for copy in copies:
            copy.start()
        for copy in copies:
            copy.wait()

    pl.run_scoped(work, pltpu.SemaphoreType.DMA((3,)))


def whole_kernel(video, multiplier, foreground, basis, coefficients):
    F, H, W = video.shape
    rank = basis.shape[0]
    nr, nc, nz = (lax.axis_size(name) for name in ("row", "col", "frame"))
    f32 = jnp.float32
    own = H // nz
    group = nr * nc
    vmem = pltpu.VMEM
    dma = pltpu.SemaphoreType.DMA
    pieces = own // CHUNK
    hbm = pl.BlockSpec(memory_space=pl.ANY)
    on_chip = pl.BlockSpec(memory_space=pltpu.VMEM)
    found = pl.pallas_call(
        functools.partial(kernel, (F, H, W, rank, nr, nc, nz)),
        out_shape=(vmem((F, H, W), f32), vmem((F, rank), f32), vmem((rank, own, W), f32)),
        in_specs=[hbm] * 5,
        out_specs=[on_chip] * 3,
        scratch_shapes=[vmem((F + 2, H + 16, W), f32)] * PASSES
        + [
            vmem((F, H, W), f32),
            vmem((F, H, W), f32),
            vmem((rank, H, W), f32),
            vmem((F, H, W), f32),
            vmem((F, H, W), f32),
            vmem((F * nz, own, W), f32),
            vmem((PASSES, SEGMENTS, 16, H // SEGMENTS), f32),
            vmem((PASSES, SEGMENTS, 16, H // SEGMENTS), f32),
            vmem((PASSES, 2, F, 8, 128), f32),
            vmem((H + 8, 128), f32),
            vmem((H + 16, 128), f32),
            vmem((H + 16, 128), f32),
            vmem((H + 24, 128), f32),
            vmem((H + 24, 128), f32),
            vmem((8, 128), f32),
            vmem((F, rank, 8, 128), f32),
            vmem((rank + F, rank, 128), f32),
            vmem((nz, 8, 128), f32),
            vmem((group, 8, 128), f32),
            vmem((rank, rank, 128), f32),
            vmem((group, rank, 128), f32),
            vmem((nz * F, 128), f32),
            vmem((128, 128), f32),
            vmem((rank, 128), f32),
            pltpu.SMEM((F, rank), f32),
            pltpu.SMEM((rank, 128), f32),
        ],
        compiler_params=pltpu.CompilerParams(
            collective_id=0, has_side_effects=True, vmem_limit_bytes=32 * 1024 * 1024
        ),
    )(
        *(
            pltpu.with_memory_space_constraint(x, pltpu.HBM)
            for x in (coefficients, video, multiplier, foreground, basis)
        )
    )
    return pl.pallas_call(
        deliver,
        out_shape=(
            jax.ShapeDtypeStruct((F, H, W), f32),
            jax.ShapeDtypeStruct((F, rank), f32),
            jax.ShapeDtypeStruct((rank, own, W), f32),
        ),
        in_specs=[on_chip] * 3,
        out_specs=[hbm] * 3,
    )(*(pltpu.with_memory_space_constraint(x, pltpu.VMEM) for x in found))


def body(video, multiplier, foreground, basis, coefficients):
    F, H, W = video.shape
    rank = basis.shape[0]
    nz = lax.axis_size("frame")
    fits = (
        H % nz == 0 and (H // nz) % 8 == 0 and (H // nz) % CHUNK == 0 and W % 128 == 0
        and H % 16 == 0 and H % (SEGMENTS * CHUNK) == 0 and lax.axis_size("row") <= 2
        and F % 4 == 0 and F < 8 and rank == 16 and nz >= 2 and F * nz == rank and 2 * rank + F * nz <= 128
    )
    run = whole_kernel if fits else local
    return run(video, multiplier, foreground, basis, coefficients)


def solution(mesh):
    placed = (
        P("frame", "row", "col"),
        P("frame", "row", "col"),
        P("frame", "row", "col"),
        P(None, "row", "col"),
        P("frame", None),
    )
    return jax.shard_map(
        body,
        mesh=mesh,
        in_specs=placed,
        out_specs=(P("frame", "row", "col"), P("frame", None), P(None, ("row", "frame"), "col")),
        check_vma=False,
    )
```
